32 devices in a mesh: dp: 8 (over z, x), tensor: 4 (over y, core).
Axes of the slice: x: 2, y: 2, z: 4, core: 2. Of those that a mesh axis runs over, the one named last changes fastest.
Arguments:
- inputs: bfloat16 [2, 8192, 768], P(None, 'dp'), may hold values from -6 to 6
- cotangent: bfloat16 [2, 8192, 768], P(None, 'dp'), may hold values from -6 to 6
- segment: int32 [2, 8192], P(None, 'dp'), may hold values from 0 to 15, never falling along the last dimension, each value on 1 to 4096 neighbouring positions
- attn_gain: bfloat16 [768], replicated, may hold values from 0.5 to 1.5
- attn_shift: bfloat16 [768], replicated, may hold values from -2 to 2
- qkv_weight: bfloat16 [768, 3, 768], P('dp', None, 'tensor'), may hold values from -0.21875 to 0.21875
- qkv_bias: bfloat16 [3, 768], P(None, 'tensor'), may hold values from -2 to 2
- query_map: bfloat16 [12, 64, 64], P('tensor'), may hold values from -2 to 2
- key_map: bfloat16 [12, 64, 64], P('tensor'), may hold values from -2 to 2
- proj_weight: bfloat16 [768, 768], P('tensor', 'dp'), may hold values from -0.875 to 0.875
- proj_bias: bfloat16 [768], replicated, may hold values from -2 to 2
- mlp_gain: bfloat16 [768], replicated, may hold values from 0.5 to 1.5
- mlp_shift: bfloat16 [768], replicated, may hold values from -2 to 2
- fc_weight: bfloat16 [768, 3072], P('dp', 'tensor'), may hold values from -0.21875 to 0.21875
- fc_bias: bfloat16 [3072], P('tensor'), may hold values from -2 to 2
- out_weight: bfloat16 [3072, 768], P('tensor', 'dp'), may hold values from -0.109375 to 0.109375
- out_bias: bfloat16 [768], replicated, may hold values from -2 to 2
Outputs:
- output: bfloat16 [2, 8192, 768], P(None, 'dp')
- input_grad: bfloat16 [2, 8192, 768], P(None, 'dp')
- grad_attn_gain: float32 [768], replicated
- grad_attn_shift: float32 [768], replicated
- grad_qkv_weight: float32 [768, 3, 768], P('dp', None, 'tensor')
- grad_qkv_bias: float32 [3, 768], P(None, 'tensor')
- grad_query_map: float32 [12, 64, 64], P('tensor')
- grad_key_map: float32 [12, 64, 64], P('tensor')
- grad_proj_weight: float32 [768, 768], P('tensor', 'dp')
- grad_proj_bias: float32 [768], replicated
- grad_mlp_gain: float32 [768], replicated
- grad_mlp_shift: float32 [768], replicated
- grad_fc_weight: float32 [768, 3072], P('dp', 'tensor')
- grad_fc_bias: float32 [3072], P('tensor')
- grad_out_weight: float32 [3072, 768], P('tensor', 'dp')
- grad_out_bias: float32 [768], replicated
The draws below stay inside these ranges and needn't reach their ends.
Inputs may be any that keep to these rules, and one draw needn't show every extreme that they name: `segment`: along each micro-batch's tokens the numbers never fall; each number covers 1 to 4096 consecutive tokens, some number exactly that many, and every number in the range occurs.
All inputs are finite; a program needn't handle non-finite values.
Results may differ from the reference program's by a relative error of at most 0.018.
Values may be sent and summed in bfloat16 or wider, within the bound.
No kernel may reach another device: no remote copies, remote signals or barrier semaphores. Data moves between devices by JAX's collectives and lax.ppermute only.
A program may use at most 256 MiB of HBM per device.

```python
import math
import jax
import jax.numpy as jnp
import numpy as np
from jax import lax

D = 768
HEADS = 12
HD = 64
FF = 3072
FEAT = 128
BLOCK = 64
SEQ_LEN = 8192
MB = 2
TOK_DEV = 1024
TOKENS = 8192
SEGS = 16
N_TENSOR = 4


def steps_of(rng, shape, split, low, high):
    factor_of = 1.0
    for axis_at, parts in split:
        heights = jax.random.uniform(jax.random.fold_in(jax.random.fold_in(rng, 6), axis_at), (parts,), jnp.float32, low / len(split), high / len(split))
        factor_of = factor_of * jnp.repeat(jnp.exp(heights), shape[axis_at] // parts).reshape((-1,) + (1,) * (len(shape) - 1 - axis_at))
    return factor_of


def length_profile(number_of, total, bound, lean):
    weights = [(1 << 20) // math.isqrt(grade ** lean) + 1 for grade in range(2, number_of + 1)]
    surplus, given = total - bound - (number_of - 1), [1] * (number_of - 1)
    while surplus > 0:
        free = [i for i in range(number_of - 1) if given[i] < bound]
        whole, remaining = sum([weights[i] for i in free]), surplus
        for i in free:
            extra = min(bound - given[i], max(1, remaining * weights[i] // whole), surplus)
            given[i] = given[i] + extra
            surplus = surplus - extra
    return np.array([bound] + given)


def ragged_sizes(rng, count, total, bound, lean):
    if count == 2:
        one = jax.random.randint(rng, (), max(1, total - bound), min(bound, total - 1) + 1)
        return jnp.stack([one, total - one])
    sizes = jnp.asarray(length_profile(count, total, bound, lean), jnp.int32)
    twos = (count - 1) // 2
    source_of, taker = sizes[1:1 + 2 * twos:2], sizes[2:2 + 2 * twos:2]
    room = jnp.minimum(source_of - 1, bound - taker)
    passed = jax.random.randint(jax.random.fold_in(rng, 1), (twos,), 0, 1 << 20) % (room + 1)
    sizes = sizes.at[1:1 + 2 * twos:2].set(source_of - passed).at[2:2 + 2 * twos:2].set(taker + passed)
    return sizes[jax.random.permutation(jax.random.fold_in(rng, 2), count)]


def scatter_about(key, shape, width, limit, cuts=(), kind=jnp.bfloat16):
    values = jax.random.normal(key, shape, jnp.float32) * width
    if len(cuts) > 0:
        values = steps_of(key, shape, cuts, -0.22, 0.18) * values
    return jnp.clip(values, min=-limit, max=limit).astype(kind)


def setup_inputs(seed: int = 0) -> dict:
    seeds = jax.random.split(jax.random.key(seed), 18)
    inputs = scatter_about(seeds[0], (MB, TOKENS, D), 1.0, 6.0, ((1, 8),))
    cotangent = scatter_about(seeds[1], (MB, TOKENS, D), 1.0, 6.0, ((1, 8),))
    segment = jax.vmap(lambda own: jnp.searchsorted(jnp.cumsum(ragged_sizes(own, SEGS, TOKENS, 4 * TOK_DEV, 2)), jnp.arange(TOKENS), side="right"))(jax.random.split(seeds[2], MB)).reshape((MB, TOKENS)).astype(jnp.int32)
    attn_gain = jnp.clip(1.0 + 0.1 * jax.random.normal(seeds[3], (D,), jnp.float32), 0.5, 1.5).astype(jnp.bfloat16)
    attn_shift = scatter_about(seeds[4], (D,), 0.3, 2.0)
    qkv_weight = scatter_about(seeds[5], (D, 3, D), D ** -0.5, 0.21875, ((0, 8), (2, 4)))
    qkv_bias = scatter_about(seeds[6], (3, D), 0.3, 2.0, ((1, 4),))
    query_map = scatter_about(seeds[7], (HEADS, HD, HD), (HD // 8) ** -0.5, 2.0, ((0, 4),))
    key_map = scatter_about(seeds[8], (HEADS, HD, HD), (HD // 8) ** -0.5, 2.0, ((0, 4),))
    proj_weight = scatter_about(seeds[9], (D, D), (D // 16) ** -0.5, 0.875, ((0, 4), (1, 8)))
    proj_bias = scatter_about(seeds[10], (D,), 0.3, 2.0)
    mlp_gain = jnp.clip(1.0 + 0.1 * jax.random.normal(seeds[11], (D,), jnp.float32), 0.5, 1.5).astype(jnp.bfloat16)
    mlp_shift = scatter_about(seeds[12], (D,), 0.3, 2.0)
    fc_weight = scatter_about(seeds[13], (D, FF), D ** -0.5, 0.21875, ((0, 8), (1, 4)))
    fc_bias = scatter_about(seeds[14], (FF,), 0.3, 2.0, ((0, 4),))
    out_weight = scatter_about(seeds[15], (FF, D), FF ** -0.5, 0.109375, ((0, 4), (1, 8)))
    out_bias = scatter_about(seeds[16], (D,), 0.3, 2.0)
    return {"inputs": inputs, "cotangent": cotangent, "segment": segment, "attn_gain": attn_gain, "attn_shift": attn_shift, "qkv_weight": qkv_weight, "qkv_bias": qkv_bias, "query_map": query_map, "key_map": key_map, "proj_weight": proj_weight, "proj_bias": proj_bias, "mlp_gain": mlp_gain, "mlp_shift": mlp_shift, "fc_weight": fc_weight, "fc_bias": fc_bias, "out_weight": out_weight, "out_bias": out_bias}


EPSILON = 1e-05
PRECISION_TOP = lax.Precision.HIGHEST
GELU_SCALE = 0.7978845608028654
GELU_CUBIC = 0.044715

@jax.custom_vjp
def low(v):
    return lax.optimization_barrier(v.astype(jnp.bfloat16)).astype(jnp.float32)

@jax.custom_vjp
def low_back(v):
    return v

def low_keep(v):
    return (low(v), None)

def low_pass(kept, grad):
    return (grad,)

def back_keep(v):
    return (v, None)

def back_low(kept, grad):
    return (low(grad),)
low.defvjp(low_keep, low_pass)
low_back.defvjp(back_keep, back_low)

def layer_norm(values, norm_gain, norm_bias):
    centred = values - lax.optimization_barrier(jnp.mean(values, axis=-1, keepdims=True))
    variance = lax.optimization_barrier(jnp.mean(centred * centred, axis=-1, keepdims=True))
    return centred * lax.rsqrt(variance + EPSILON) * norm_gain + norm_bias

def softmax_last(values):
    shifted = values - lax.optimization_barrier(jnp.max(values, axis=-1, keepdims=True))
    raised = jnp.exp(shifted)
    return raised / lax.optimization_barrier(jnp.sum(raised, axis=-1, keepdims=True))

def features(mapped):
    return jnp.concatenate([softmax_last(mapped), softmax_last(-mapped)], axis=-1)

def gelu_tanh(preact):
    return 0.5 * preact * (1.0 + jnp.tanh(GELU_SCALE * (preact + GELU_CUBIC * preact * preact * preact)))

def attend_sequence(query_feat, key_feat, values_in, segments):
    block_count = SEQ_LEN // BLOCK
    query_blocks = query_feat.reshape(block_count, BLOCK, HEADS, FEAT)
    key_blocks = key_feat.reshape(block_count, BLOCK, HEADS, FEAT)
    value_blocks = values_in.reshape(block_count, BLOCK, HEADS, HD)
    seg_blocks = segments.reshape(block_count, BLOCK)
    causal = jnp.arange(BLOCK)[:, None] >= jnp.arange(BLOCK)[None, :]

    def block_step(carried_in, pieces):
        kv_state, normalizer, previous = carried_in
        block_query, block_key, block_value, block_seg = pieces
        allowed = jnp.logical_and(causal, block_seg[:, None] == block_seg[None, :]).astype(jnp.float32)
        scores = jnp.einsum('thf,shf->hts', block_query, block_key, precision=PRECISION_TOP)
        scores = low(low_back(scores)) * allowed[None]
        numerator = jnp.einsum('hts,shd->thd', scores, block_value, precision=PRECISION_TOP)
        denominator = jnp.transpose(lax.optimization_barrier(jnp.sum(scores, axis=-1)))
        carried = (block_seg == previous).astype(jnp.float32)
        numerator = numerator + carried[:, None, None] * jnp.einsum('thf,hfd->thd', block_query, kv_state, precision=PRECISION_TOP)
        denominator = denominator + carried[:, None] * jnp.einsum('thf,hf->th', block_query, normalizer, precision=PRECISION_TOP)
        final_seg = block_seg[-1]
        tail_mask = (block_seg == final_seg).astype(jnp.float32)
        keep_flag = (final_seg == previous).astype(jnp.float32)
        tail_key = block_key * tail_mask[:, None, None]
        kv_state = keep_flag * kv_state + jnp.einsum('shf,shd->hfd', tail_key, block_value, precision=PRECISION_TOP)
        normalizer = keep_flag * normalizer + lax.optimization_barrier(jnp.sum(tail_key, axis=0))
        return ((kv_state, normalizer, final_seg), numerator / denominator[:, :, None])
    start = (jnp.zeros((HEADS, FEAT, HD), jnp.float32), jnp.zeros((HEADS, FEAT), jnp.float32), jnp.int32(-1))
    ignored, attended = lax.scan(jax.checkpoint(block_step), start, (query_blocks, key_blocks, value_blocks, seg_blocks))
    return attended.reshape(SEQ_LEN, HEADS, HD)

def layer_sequence(params, rows, segments):
    attn_gain, attn_shift, qkv_weight, qkv_bias, query_map, key_map, proj_weight, proj_bias, mlp_gain, mlp_shift, fc_weight, fc_bias, out_weight, out_bias = params
    attn_in = low(layer_norm(rows, attn_gain, attn_shift))
    qkv = low_back(jnp.einsum('td,dce->tce', attn_in, qkv_weight, precision=PRECISION_TOP) + qkv_bias)
    queries = low(qkv[:, 0]).reshape(SEQ_LEN, HEADS, HD)
    keys_in = low(qkv[:, 1]).reshape(SEQ_LEN, HEADS, HD)
    values_in = low(qkv[:, 2]).reshape(SEQ_LEN, HEADS, HD)
    query_feat = low(features(low_back(jnp.einsum('the,hef->thf', queries, query_map, precision=PRECISION_TOP))))
    key_feat = low(features(low_back(jnp.einsum('the,hef->thf', keys_in, key_map, precision=PRECISION_TOP))))
    attended = low(attend_sequence(query_feat, key_feat, values_in, segments).reshape(SEQ_LEN, D))
    attn_parts = jnp.einsum('tje,jed->jtd', attended.reshape(SEQ_LEN, N_TENSOR, D // N_TENSOR), proj_weight.reshape(N_TENSOR, D // N_TENSOR, D), precision=PRECISION_TOP)
    attn_out = low_back(lax.optimization_barrier(jnp.sum(low(attn_parts), axis=0)) + proj_bias)
    residual = rows + attn_out
    mlp_in = low(layer_norm(residual, mlp_gain, mlp_shift))
    preact = low_back(jnp.einsum('td,df->tf', mlp_in, fc_weight, precision=PRECISION_TOP) + fc_bias)
    activ = low(gelu_tanh(preact))
    mlp_parts = jnp.einsum('tjf,jfd->jtd', activ.reshape(SEQ_LEN, N_TENSOR, FF // N_TENSOR), out_weight.reshape(N_TENSOR, FF // N_TENSOR, D), precision=PRECISION_TOP)
    return residual + lax.optimization_barrier(jnp.sum(low(mlp_parts), axis=0)) + out_bias

def reference(inputs, cotangent, segment, attn_gain, attn_shift, qkv_weight, qkv_bias, query_map, key_map, proj_weight, proj_bias, mlp_gain, mlp_shift, fc_weight, fc_bias, out_weight, out_bias):
    params = tuple((item.astype(jnp.float32) for item in (attn_gain, attn_shift, qkv_weight, qkv_bias, query_map, key_map, proj_weight, proj_bias, mlp_gain, mlp_shift, fc_weight, fc_bias, out_weight, out_bias)))
    sequences = MB * TOKENS // SEQ_LEN
    rows = inputs.astype(jnp.float32).reshape(sequences, SEQ_LEN, D)
    seg_rows = segment.reshape(sequences, SEQ_LEN)

    def forward(weights, rows_in):

        def single(pair):
            return layer_sequence(weights, pair[0], pair[1])
        return lax.map(jax.checkpoint(single), (rows_in, seg_rows))
    result, pull_back = jax.vjp(forward, params, rows)
    grad_params, grad_rows = pull_back(cotangent.astype(jnp.float32).reshape(sequences, SEQ_LEN, D))
    return (result.reshape(MB, TOKENS, D).astype(jnp.bfloat16), grad_rows.reshape(MB, TOKENS, D).astype(jnp.bfloat16), grad_params[0], grad_params[1], grad_params[2], grad_params[3], grad_params[4], grad_params[5], grad_params[6], grad_params[7], grad_params[8], grad_params[9], grad_params[10], grad_params[11], grad_params[12], grad_params[13])
```

```python
import functools

import jax
import jax.numpy as jnp
from jax import lax
from jax.experimental import pallas as pl
from jax.experimental.pallas import tpu as pltpu
from jax.sharding import PartitionSpec as P

SEQ_LEN = 8192
MAX_SEGMENT = 4096
EPSILON = 1e-05
GELU_SCALE = 0.7978845608028654
GELU_CUBIC = 0.044715
PAD = 16

f32 = jnp.float32
bf16 = jnp.bfloat16


def dot_nn(a, b):
    return lax.dot_general(a, b, (((1,), (0,)), ((), ())), preferred_element_type=f32)


def dot_nt(a, b):
    return lax.dot_general(a, b, (((1,), (1,)), ((), ())), preferred_element_type=f32)


def dot_tn(a, b):
    return lax.dot_general(a, b, (((0,), (0,)), ((), ())), preferred_element_type=f32)


def split(value):
    high = value.astype(bf16)
    return high, (value - high.astype(f32)).astype(bf16)


def norm_parts(values):
    centred = values - jnp.mean(values, axis=-1, keepdims=True)
    inverse = lax.rsqrt(jnp.mean(centred * centred, axis=-1, keepdims=True) + EPSILON)
    return centred * inverse, inverse


def norm_back(grad, normed, inverse, gain):
    scaled = grad * gain
    return inverse * (
        scaled
        - jnp.mean(scaled, axis=-1, keepdims=True)
        - normed * jnp.mean(scaled * normed, axis=-1, keepdims=True)
    )


def softmax_rows(values):
    raised = jnp.exp(values - jnp.max(values, axis=0, keepdims=True))
    return raised * (1.0 / jnp.sum(raised, axis=0, keepdims=True))


def relative(value):
    return ((value & 1) << 1) | (value >> 1)


def with_ones(values):
    width = values.shape[1]
    rows = lax.broadcasted_iota(jnp.int32, (PAD, width), 0)
    return jnp.concatenate([values, (rows == 0).astype(f32).astype(bf16)], axis=0)


def call(kernel, grid, ids, inputs, outputs, scratch, flops, vmem=None):
    moved = sum(a.size * a.dtype.itemsize for a, _, _ in inputs)
    return pl.pallas_call(
        kernel,
        grid_spec=pltpu.PrefetchScalarGridSpec(
            num_scalar_prefetch=1,
            grid=grid,
            in_specs=[pl.BlockSpec(block, index) for _, block, index in inputs],
            out_specs=[pl.BlockSpec(block, index) for _, _, block, index in outputs],
            scratch_shapes=scratch,
        ),
        out_shape=[jax.ShapeDtypeStruct(shape, kind) for shape, kind, _, _ in outputs],
        cost_estimate=pl.CostEstimate(flops=flops, bytes_accessed=moved, transcendentals=0),
        compiler_params=pltpu.CompilerParams(dimension_semantics=("arbitrary",) * len(grid)),
    )(ids, *[a for a, _, _ in inputs])


def whole(array):
    return (array, array.shape, lambda i, ids: (0,) * array.ndim)


def whole_out(shape, kind):
    return (shape, kind, shape, lambda i, ids: (0,) * len(shape))


def join_kernel(count, widths, flip, ids, *refs):
    pieces, outs = refs[:count], refs[count : count + len(widths)]
    rows = pieces[0].shape[0]
    place = ids[1]
    target = refs[-1] if flip else None
    for step in range(count):
        source = lax.rem(place - step + count, count)
        where = pl.ds(pl.multiple_of(source * rows, rows), rows)
        if flip:
            target[where, :] = pieces[step][...].astype(f32)
        else:
            at = 0
            for out, width in zip(outs, widths):
                out[where, :] = pieces[step][:, at : at + width]
                at += width
    if flip:
        outs[0][...] = target[...].T.astype(bf16)


def project_kernel(heads, ids, x, gain, shift, weight, bias, maps, seg, seg_last, attn_in, qkv, feats, state, total):
    step = pl.program_id(0)
    normed, _ = norm_parts(x[...].astype(f32))
    rows = (normed * gain[...] + shift[...]).astype(bf16)
    attn_in[...] = rows
    low = (dot_nt(weight[...], rows) + bias[...]).astype(bf16)
    qkv[...] = low
    width = low.shape[0] // 3
    size = width // heads
    mapped = [dot_nn(maps[part], low[part * width : (part + 1) * width]) for part in range(2)]

    @pl.when(step == 0)
    def _():
        total[...] = jnp.zeros_like(total)

    tail = (seg[...] == seg_last[:, -1:]).astype(f32).astype(bf16)
    for head in range(heads):
        for part in range(2):
            own = mapped[part][head * size : (head + 1) * size]
            both = jnp.concatenate([softmax_rows(own), softmax_rows(-own)], axis=0).astype(bf16)
            at = (part * heads + head) * 2 * size
            feats[at : at + 2 * size, :] = both
        value = with_ones(low[2 * width + head * size : 2 * width + (head + 1) * size])
        at = head * (size + PAD)
        total[at : at + size + PAD, :] += dot_nt(value * tail, both)
    used = heads * (size + PAD)

    @pl.when(step == pl.num_programs(0) - 1)
    def _():
        state[:used, :] = total[...].astype(bf16)
        state[used:, :] = jnp.broadcast_to(seg_last[:, -1:], (PAD, 2 * size)).astype(bf16)


def pair_mask(seg_col, seg_row):
    tile = seg_row.shape[1]
    early = lax.broadcasted_iota(jnp.int32, (tile, tile), 0)
    late = lax.broadcasted_iota(jnp.int32, (tile, tile), 1)
    return jnp.where(early <= late, (seg_col == seg_row).astype(f32), 0.0)


def attend_kernel(heads, pieces, hops, ids, qkv_v, feats, seg, seg_col, *refs):
    received, refs = refs[:hops], refs[hops:]
    attended, attended_low, denominators, states, state, previous = refs
    step = pl.program_id(0)
    size = qkv_v.shape[0] // heads
    rows = size + PAD
    used = heads * rows
    place = lax.rem(ids[1], pieces)

    @pl.when(step == 0)
    def _():
        start = jnp.zeros((used, 2 * size), f32)
        for hop in range(hops):
            latest = received[0][used : used + 1, :].astype(f32)
            linked = (received[hop][used : used + 1, :].astype(f32) == latest).astype(f32)
            linked = linked * (place > hop).astype(f32)
            start = start + linked * received[hop][:used, :].astype(f32)
        state[...] = start
        first = received[0][used : used + 1, :1].astype(f32)
        previous[...] = jnp.broadcast_to(jnp.where(place > 0, first, -2.0), previous.shape)

    row = seg[...]
    end = row[:, -1:]
    mask = pair_mask(seg_col[...], row)
    before = previous[...]
    carried = (row == before).astype(f32)
    tail = (row == end).astype(f32).astype(bf16)
    keep = (before[:, : 2 * size] == end).astype(f32)
    states[...] = state[...]
    for head in range(heads):
        query = feats[head * 2 * size : (head + 1) * 2 * size, :]
        key = feats[(heads + head) * 2 * size : (heads + head + 1) * 2 * size, :]
        value = with_ones(qkv_v[head * size : (head + 1) * size, :])
        scores = (dot_tn(key, query) * mask).astype(bf16)
        own = state[head * rows : (head + 1) * rows, :]
        inter = dot_nn(jnp.concatenate(split(own), axis=0), query)
        both = dot_nn(value, scores) + carried * (inter[:rows] + inter[rows:])
        lower = both[size : size + 1]
        result = both[:size] / lower
        attended[head * size : (head + 1) * size, :] = result
        attended_low[head * size : (head + 1) * size, :] = result.astype(bf16)
        denominators[head : head + 1, :] = lower
        state[head * rows : (head + 1) * rows, :] = keep * own + dot_nt(value * tail, key)
    previous[...] = jnp.broadcast_to(end, previous.shape)


def mlp_kernel(chunks, first, ids, x, cot, a0, a1, a2, a3, p0, p1, p2, p3, proj_bias, gain, shift, fc, out_t, fc_bias, *refs):
    if first:
        residual, out_part, grad_part, fc_acc, out_acc, bias_acc = refs
    else:
        fc_in, out_in, bias_in, residual, out_part, grad_part, vectors, bias_out = refs[:8]
        pieces = refs[8 : 8 + chunks]
        fc_acc, out_acc, bias_acc = refs[8 + chunks :]
    step = pl.program_id(0)

    @pl.when(step == 0)
    def _():
        if first:
            fc_acc[...] = jnp.zeros_like(fc_acc)
            out_acc[...] = jnp.zeros_like(out_acc)
            bias_acc[...] = jnp.zeros_like(bias_acc)
        else:
            fc_acc[...] = fc_in[...]
            out_acc[...] = out_in[...]
            bias_acc[...] = bias_in[...]

    resid = x[...].astype(f32) + proj_bias[...]
    for part, proj in zip((a0, a1, a2, a3), (p0, p1, p2, p3)):
        resid = resid + dot_nt(part[...].T, proj[...])
    residual[...] = resid
    normed, _ = norm_parts(resid)
    mlp_in = (normed * gain[...] + shift[...]).astype(bf16)
    preact = dot_nn(mlp_in, fc[...]) + fc_bias[...]
    square = preact * preact
    tangent = jnp.tanh(GELU_SCALE * (preact + GELU_CUBIC * square * preact))
    half = 0.5 * (1.0 + tangent)
    activ = (preact * half).astype(bf16)
    slope = half + 0.5 * preact * (1.0 - tangent * tangent) * GELU_SCALE * (1.0 + 3.0 * GELU_CUBIC * square)
    out_part[...] = dot_nt(activ, out_t[...]).astype(bf16)
    top = cot[...]
    grad_pre = (dot_nn(top, out_t[...]) * slope).astype(bf16)
    grad_part[...] = dot_nt(grad_pre, fc[...]).astype(bf16)
    fc_acc[...] += dot_tn(mlp_in, grad_pre)
    out_acc[...] += dot_tn(top, activ)
    bias_acc[...] += jnp.sum(grad_pre.astype(f32), axis=0, keepdims=True)
    if not first:

        @pl.when(step == pl.num_programs(0) - 1)
        def _():
            rows, width = fc_acc.shape[0] // chunks, fc_acc.shape[1]
            for ahead in range(chunks):
                source = lax.rem(ids[1] + ahead, chunks)
                where = pl.ds(pl.multiple_of(source * rows, rows), rows)
                pieces[ahead][:, :width] = fc_acc[where, :].astype(bf16)
                pieces[ahead][:, width:] = out_acc[where, :].astype(bf16)
            wide = fc[...].astype(f32)
            vectors[:, 0:1] = jnp.sum(wide * fc_acc[...], axis=1, keepdims=True)
            vectors[:, 1:2] = jnp.sum(wide * bias_acc[...], axis=1, keepdims=True)
            bias_out[...] = bias_acc[...]


def middle_kernel(ids, residual, cot, part, arrived, gain, grad_residual, grad_attn, sums):
    normed, inverse = norm_parts(residual[...])
    grad = part[...].astype(f32) + arrived[...].astype(f32)
    top = cot[...].astype(f32)
    total = top + norm_back(grad, normed, inverse, gain[...])
    grad_residual[...] = total
    low = total.astype(bf16)
    grad_attn[...] = low
    sums[0:1, :] = jnp.sum(low.astype(f32), axis=0, keepdims=True)
    sums[1:2, :] = jnp.sum(top, axis=0, keepdims=True)


def last_kernel(ids, x, part, arrived, grad_residual, gain, out):
    normed, inverse = norm_parts(x[...].astype(f32))
    grad = part[...].astype(f32) + arrived[...].astype(f32)
    out[...] = (grad_residual[...] + norm_back(grad, normed, inverse, gain[...])).astype(bf16)


def finish_kernel(ids, residual, part, arrived, bias, out):
    out[...] = (residual[...] + bias[...] + part[...].astype(f32) + arrived[...].astype(f32)).astype(bf16)


def order_kernel(count, ids, *refs):
    out = refs[count]
    for at in range(count):

        @pl.when(pl.program_id(0) == at)
        def _():
            out[...] = refs[at][...]


def grads_in_kernel(heads, pieces, first, ids, g0, g1, g2, g3, proj_t, feats_q, attended, attended_low, denominators, seg, seg_last_before, *refs):
    if first:
        grads, state, proj_acc, total = refs
    else:
        proj_in, grads, state, proj_acc, total = refs
    step = pl.program_id(0)
    size = attended.shape[0] // heads
    rows = size + PAD
    used = heads * rows

    @pl.when(step == 0)
    def _():
        total[...] = jnp.zeros_like(total)
        proj_acc[...] = jnp.zeros_like(proj_acc) if first else proj_in[...]

    def work(source):
        grad = source[...]
        proj_acc[...] += dot_nn(attended_low[...], grad)
        grad_att = dot_tn(proj_t[...], grad.T)
        before = seg_last_before[used : used + 1, :1].astype(f32)
        before = jnp.where(lax.rem(ids[1], pieces) > 0, before, -2.0)
        carried = (seg[...] == before).astype(f32)
        for head in range(heads):
            own = grad_att[head * size : (head + 1) * size]
            inverse = 1.0 / denominators[head : head + 1, :]
            lower = -inverse * jnp.sum(own * attended[head * size : (head + 1) * size, :], axis=0, keepdims=True)
            filler = lax.broadcasted_iota(jnp.int32, (PAD, own.shape[1]), 0)
            both = jnp.concatenate([own * inverse, jnp.where(filler == 0, lower, 0.0)], axis=0)
            grads[head * rows : (head + 1) * rows, :] = both
            query = feats_q[head * 2 * size : (head + 1) * 2 * size, :]
            sums = dot_nt(jnp.concatenate(split(both * carried), axis=0), query)
            total[head * rows : (head + 1) * rows, :] += sums[:rows] + sums[rows:]

    for at, source in enumerate((g0, g1, g2, g3)):

        @pl.when(step == at)
        def _():
            work(source)

    @pl.when(step == pl.num_programs(0) - 1)
    def _():
        state[:used, :] = total[...].astype(bf16)
        before = seg_last_before[used:, :].astype(f32)
        state[used:, :] = jnp.where(lax.rem(ids[1], pieces) > 0, before, -2.0).astype(bf16)


def softmax_back(grad, positive, negative):
    size = positive.shape[0]
    upper, lower = grad[:size], grad[size:]
    return positive * (upper - jnp.sum(positive * upper, axis=0, keepdims=True)) - negative * (
        lower - jnp.sum(negative * lower, axis=0, keepdims=True)
    )


def grads_kernel(
    heads, pieces, hops, chunks, first, ids, qkv, feats, grads, states, seg, seg_col, seg_before, attn_in, weight, maps, maps_back, *refs
):
    received, refs = refs[:hops], refs[hops:]
    if first:
        grad_part, weight_acc, map_acc, bias_acc, state, total = refs
    else:
        weight_in, map_in, bias_in, proj_in, gain, shift, grad_part, map_out, bias_out, vectors = refs[:10]
        outs = refs[10 : 10 + chunks]
        weight_acc, map_acc, bias_acc, state, total = refs[10 + chunks :]
    step = pl.program_id(0)
    count = pl.num_programs(0)
    width = qkv.shape[0] // 3
    size = width // heads
    rows = size + PAD
    used = heads * rows
    row = seg[...]
    end = row[:, -1:]

    @pl.when(step == 0)
    def _():
        start = jnp.zeros((used, 2 * size), f32)
        place = lax.rem(ids[1], pieces)
        for hop in range(hops):
            linked = (received[hop][used : used + 1, :].astype(f32) == end).astype(f32)
            linked = linked * (place + hop + 1 < pieces).astype(f32)
            start = start + linked * received[hop][:used, :].astype(f32)
        state[...] = start
        if first:
            weight_acc[...] = jnp.zeros_like(weight_acc)
            map_acc[...] = jnp.zeros_like(map_acc)
            bias_acc[...] = jnp.zeros_like(bias_acc)
        else:
            weight_acc[...] = weight_in[...]
            map_acc[...] = map_in[...]
            bias_acc[...] = bias_in[...]

    before = seg_before[...]
    mask = pair_mask(seg_col[...], row)
    carried = (row == before).astype(f32)
    tail = (row == end).astype(f32)
    keep = (before == end).astype(f32)
    mapped = [dot_nn(maps[part], qkv[part * width : (part + 1) * width, :]) for part in range(2)]
    back = [[], []]
    grad_values = []
    for head in range(heads):
        query = feats[head * 2 * size : (head + 1) * 2 * size, :]
        key = feats[(heads + head) * 2 * size : (heads + head + 1) * 2 * size, :]
        at = 2 * width + head * size
        value = with_ones(qkv[at : at + size, :])
        value_two = jnp.concatenate([value, value], axis=0)
        own = grads[head * rows : (head + 1) * rows, :]
        high, low = split(own)
        grad_two = jnp.concatenate([high, low], axis=0)
        scores = (dot_tn(key, query) * mask).astype(bf16)
        grad_scores = (dot_tn(value_two, grad_two) * mask).astype(bf16)
        into = states[head * rows : (head + 1) * rows, :]
        into_high, into_low = split(into)
        inter = dot_tn(
            jnp.concatenate([into_high, into_low, into_high], axis=0),
            jnp.concatenate([high, high, low], axis=0),
        )
        grad_query = dot_nn(key, grad_scores) + carried * inter
        after = state[head * rows : (head + 1) * rows, :]
        after_two = jnp.concatenate(split(after), axis=0)
        grad_key = dot_nt(query, grad_scores) + tail * dot_tn(after_two, value_two)
        straight = dot_nt(grad_two, scores)
        through = dot_nn(after_two, key)
        grad_values.append(
            straight[:size] + straight[rows : rows + size] + tail * (through[:size] + through[rows : rows + size])
        )
        carried_two = jnp.concatenate(split(own * carried), axis=0)
        added = dot_nt(carried_two, query)
        state[head * rows : (head + 1) * rows, :] = keep * after + added[:rows] + added[rows:]
        for part, grad in ((0, grad_query), (1, grad_key)):
            plain = mapped[part][head * size : (head + 1) * size]
            back[part].append(softmax_back(grad, softmax_rows(plain), softmax_rows(-plain)))
    pieces_low = []
    for part in range(2):
        grad_mapped = jnp.concatenate(back[part], axis=0).astype(bf16)
        map_acc[part] += dot_nt(qkv[part * width : (part + 1) * width, :], grad_mapped)
        pieces_low.append(dot_nn(maps_back[part], grad_mapped))
    pieces_low.append(jnp.concatenate(grad_values, axis=0))
    grad_qkv = jnp.concatenate(pieces_low, axis=0).astype(bf16)
    grad_part[...] = dot_tn(grad_qkv, weight[...]).astype(bf16)
    weight_acc[...] += dot_nn(grad_qkv, attn_in[...])
    bias_acc[...] += jnp.sum(grad_qkv.astype(f32), axis=1, keepdims=True)
    if not first:

        @pl.when(step == count - 1)
        def _():
            total[:, : 3 * width] = weight_acc[...].T
            total[:, 3 * width :] = proj_in[...].T
            chunk = total.shape[0] // chunks
            for ahead in range(chunks):
                source = lax.rem(ids[1] + ahead, chunks)
                where = pl.ds(pl.multiple_of(source * chunk, chunk), chunk)
                outs[ahead][...] = total[where, :].astype(bf16)
            wide = weight[...].astype(f32)
            grad_shift = jnp.sum(wide * bias_acc[...], axis=0, keepdims=True)
            grad_gain = jnp.sum(wide * weight_acc[...], axis=0, keepdims=True)
            vectors[0:1, :] = (grad_gain - shift[...] * grad_shift) / gain[...]
            vectors[1:2, :] = grad_shift
            map_out[...] = map_acc[...]
            bias_out[...] = bias_acc[...]


def around(array, axis, shift, size):
    return lax.ppermute(array, axis, [(i, (i + shift) % size) for i in range(size)])


def swap(array, bit):
    return lax.ppermute(array, "tensor", [(i, i ^ bit) for i in range(4)])


def gather_tensor(array):
    across = swap(array, 2)
    return (array, across, swap(array, 1), swap(across, 1))


def scatter_tensor(parts):
    arrived = swap(parts[2:], 1)
    sums = (parts[:2].astype(f32) + arrived.astype(f32)).astype(bf16)
    return sums[0], swap(sums[1], 2)


def block_diagonal(blocks):
    count, size, _ = blocks.shape
    eye = jnp.eye(count, dtype=blocks.dtype)
    return (eye[:, None, :, None] * blocks[:, :, None, :]).reshape(count * size, count * size)


def on_device(
    inputs, cotangent, segment, attn_gain, attn_shift, qkv_weight, qkv_bias, query_map, key_map,
    proj_weight, proj_bias, mlp_gain, mlp_shift, fc_weight, fc_bias, out_weight, out_bias,
):
    micro, tokens, dim = inputs.shape
    heads, size, _ = query_map.shape
    width = heads * size
    units = fc_weight.shape[1]
    count = lax.axis_size("dp")
    tiles = lax.axis_size("tensor")
    tile = tokens // tiles
    pieces = SEQ_LEN // tokens
    hops = min(-(-MAX_SEGMENT // tokens), pieces - 1)
    rows = size + PAD
    used = heads * rows
    shard = dim // count
    direct = shard % 16 == 0
    chunks = count if direct else 1
    place = lax.axis_index("dp")
    ids = jnp.stack([lax.axis_index("tensor"), place]).astype(jnp.int32)

    qkv_own = qkv_weight.reshape(shard, 3 * width)
    rest_own = jnp.concatenate([fc_weight, out_weight.T, proj_weight.T], axis=1)
    if direct:
        qkv_pieces = [qkv_own] + [around(qkv_own, "dp", k, count) for k in range(1, count)]
        rest_own, qkv_pieces = lax.optimization_barrier((rest_own, qkv_pieces))
        rest_pieces = [rest_own] + [around(rest_own, "dp", k, count) for k in range(1, count)]
        (weight_t,) = call(
            functools.partial(join_kernel, count, (3 * width,), True), (1,), ids,
            [whole(a) for a in qkv_pieces], [whole_out((3 * width, dim), bf16)],
            [pltpu.VMEM((dim, 3 * width), f32)], 0,
        )
        fc_full, out_t, proj_t = call(
            functools.partial(join_kernel, count, (units, units, width), False), (1,), ids,
            [whole(a) for a in rest_pieces],
            [whole_out((dim, units), bf16), whole_out((dim, units), bf16), whole_out((dim, width), bf16)],
            [], 0,
        )
    else:
        weight_t = lax.all_gather(qkv_own, "dp", axis=0, tiled=True).T
        rest = lax.all_gather(rest_own, "dp", axis=0, tiled=True)
        fc_full, out_t, proj_t = rest[:, :units], rest[:, units : 2 * units], rest[:, 2 * units :]
    proj_slots = gather_tensor(proj_t)

    row = lambda v: v.astype(f32).reshape(1, -1)
    gain_a, shift_a, gain_m, shift_m = row(attn_gain), row(attn_shift), row(mlp_gain), row(mlp_shift)
    bias_p, bias_f, bias_o = row(proj_bias), row(fc_bias), row(out_bias)
    bias_qkv = qkv_bias.astype(f32).reshape(3 * width, 1)
    maps_back = jnp.stack([block_diagonal(query_map), block_diagonal(key_map)])
    maps = jnp.swapaxes(maps_back, 1, 2)
    seg = segment.astype(f32).reshape(micro, tiles, 1, tile)
    seg_col = segment.astype(f32).reshape(micro, tiles, tile, 1)

    def rows_of(array, m, at=None):
        return (array, (None, tile, dim), lambda i, ids: (m, i if at is None else at(i, ids), 0))

    def own_rows(array, m):
        return (array, (None, tile, dim), lambda i, ids: (m, ids[0], 0))

    def columns(array, at=None):
        return (array, (array.shape[0], tile), lambda i, ids: (0, i if at is None else at(i, ids)))

    def columns_out(height, kind, at=None):
        return ((height, tokens), kind, (height, tile), lambda i, ids: (0, i if at is None else at(i, ids)))

    def seg_row(m, at=None):
        return (seg, (None, None, 1, tile), lambda i, ids: (m, i if at is None else at(i, ids), 0, 0))

    def seg_column(m, at=None):
        return (seg_col, (None, None, tile, 1), lambda i, ids: (m, i if at is None else at(i, ids), 0, 0))

    slots_out = lambda at=None: (
        (tiles, tile, dim), bf16, (None, tile, dim),
        lambda i, ids: (relative(ids[0] ^ (i if at is None else at(i, ids))), 0, 0),
    )
    near = lambda i, ids: ids[0] ^ relative(i)

    attn_ins, qkvs, feats, incoming = [], [], [], []
    for m in range(micro):
        attn_in, qkv, feat, state = call(
            functools.partial(project_kernel, heads), (tiles,), ids,
            [
                rows_of(inputs, m), whole(gain_a), whole(shift_a), whole(weight_t), whole(bias_qkv), whole(maps),
                seg_row(m), seg_row(m, lambda i, ids: tiles - 1),
            ],
            [
                ((tokens, dim), bf16, (tile, dim), lambda i, ids: (i, 0)),
                columns_out(3 * width, bf16), columns_out(4 * width, bf16), whole_out((used + PAD, 2 * size), bf16),
            ],
            [pltpu.VMEM((used, 2 * size), f32)],
            2 * tokens * dim * 3 * width,
        )
        attn_ins.append(attn_in)
        qkvs.append(qkv)
        feats.append(feat)
        incoming.append([
            lax.ppermute(state, "dp", [(i, i + k) for i in range(count - k)]) for k in range(1, hops + 1)
        ])
    attended, attended_low, denominators, states, slots = [], [], [], [], []
    for m in range(micro):
        result = call(
            functools.partial(attend_kernel, heads, pieces, hops), (tiles,), ids,
            [
                (qkvs[m], (width, tile), lambda i, ids: (2, i)), columns(feats[m]), seg_row(m), seg_column(m),
            ]
            + [whole(a) for a in incoming[m]],
            [
                columns_out(width, f32), columns_out(width, bf16), columns_out(8, f32),
                ((tiles, used, 2 * size), f32, (None, used, 2 * size), lambda i, ids: (i, 0, 0)),
            ],
            [pltpu.VMEM((used, 2 * size), f32), pltpu.VMEM((1, tile), f32)],
            4 * tokens * tile * width,
        )
        attended.append(result[0])
        attended_low.append(result[1])
        denominators.append(result[2])
        states.append(result[3])
        slots.append(gather_tensor(result[1]))

    acc = ()
    residuals, out_parts, mlp_parts = [], [], []
    for m in range(micro):
        first = m == 0
        final = m == micro - 1
        result = call(
            functools.partial(mlp_kernel, chunks, not final), (tiles,), ids,
            [rows_of(inputs, m), rows_of(cotangent, m)]
            + [columns(a) for a in slots[m]]
            + [whole(a) for a in proj_slots]
            + [whole(a) for a in (bias_p, gain_m, shift_m, fc_full, out_t, bias_f)]
            + [whole(a) for a in acc],
            [
                ((tiles, tile, dim), f32, (None, tile, dim), lambda i, ids: (i, 0, 0)),
                slots_out(), slots_out(),
            ]
            + (
                [whole_out((dim, 2), f32), whole_out((1, units), f32)]
                + [whole_out((dim // chunks, 2 * units), bf16)] * chunks
                if final
                else [whole_out((dim, units), f32), whole_out((dim, units), f32), whole_out((1, units), f32)]
            ),
            [pltpu.VMEM((dim, units), f32), pltpu.VMEM((dim, units), f32), pltpu.VMEM((1, units), f32)] if final else [],
            2 * tokens * dim * (dim + 6 * units),
        )
        residuals.append(result[0])
        out_parts.append(result[1])
        mlp_parts.append(result[2])
        acc = result[3:]
    mlp_vectors, grad_fc_bias, rest_grads = acc[0], acc[1], acc[2:]

    grad_residuals, grad_slots, row_sums, outputs = [], [], [], []
    own_tile = lambda array: (array, (None, tile, dim), lambda i, ids: (ids[0], 0, 0))
    for m in range(micro):
        kept, arrived = scatter_tensor(mlp_parts[m])
        grad_residual, grad_attn, sums = call(
            middle_kernel, (1,), ids,
            [own_tile(residuals[m]), own_rows(cotangent, m), whole(kept), whole(arrived), whole(gain_m)],
            [whole_out((tile, dim), f32), whole_out((tile, dim), bf16), whole_out((2, dim), f32)],
            [], 0,
        )
        grad_residuals.append(grad_residual)
        grad_slots.append(gather_tensor(grad_attn))
        row_sums.append(sums)
    if direct:
        rest_terms = [rest_grads[0]] + [around(rest_grads[k], "dp", k, count) for k in range(1, count)]
        rest_sum = sum(a.astype(f32) for a in rest_terms)
    else:
        rest_sum = lax.psum_scatter(rest_grads[0], "dp", scatter_dimension=0, tiled=True).astype(f32)
    for m in range(micro):
        kept, arrived = scatter_tensor(out_parts[m])
        (finished,) = call(
            finish_kernel, (1,), ids,
            [own_tile(residuals[m]), whole(kept), whole(arrived), whole(bias_o)],
            [whole_out((tile, dim), bf16)], [], 0,
        )
        outputs.append(gather_tensor(finished))

    proj_acc = ()
    grads, returned = [], []
    for m in range(micro):
        first = m == 0
        result = call(
            functools.partial(grads_in_kernel, heads, pieces, first), (tiles,), ids,
            [whole(a) for a in grad_slots[m]]
            + [
                whole(proj_t), (feats[m], (2 * width, tile), lambda i, ids: (0, near(i, ids))),
                columns(attended[m], near), columns(attended_low[m], near), columns(denominators[m], near),
                seg_row(m, near), whole(incoming[m][0]),
            ]
            + [whole(a) for a in proj_acc],
            [columns_out(used, f32, near), whole_out((used + PAD, 2 * size), bf16), whole_out((width, dim), f32)],
            [pltpu.VMEM((used, 2 * size), f32)],
            4 * tokens * dim * width,
        )
        grads.append(result[0])
        proj_acc = (result[2],)
        returned.append([
            lax.ppermute(result[1], "dp", [(i + k, i) for i in range(count - k)]) for k in range(1, hops + 1)
        ])
    acc = ()
    attn_parts = []
    turned = lambda i, ids: tiles - 1 - i
    for m in range(micro):
        first = m == 0
        final = m == micro - 1
        lasts = jnp.concatenate([
            jnp.where(place % pieces > 0, incoming[m][0][used, 0].astype(f32), -2.0)[None],
            seg[m, :-1, 0, -1],
        ]).reshape(tiles, 1, 1)
        result = call(
            functools.partial(grads_kernel, heads, pieces, hops, chunks, not final), (tiles,), ids,
            [
                columns(qkvs[m], turned), columns(feats[m], turned), columns(grads[m], turned),
                (states[m], (None, used, 2 * size), lambda i, ids: (tiles - 1 - i, 0, 0)),
                seg_row(m, turned), seg_column(m, turned),
                (lasts, (None, 1, 1), lambda i, ids: (tiles - 1 - i, 0, 0)),
                (attn_ins[m], (tile, dim), lambda i, ids: (tiles - 1 - i, 0)),
                whole(weight_t), whole(maps), whole(maps_back),
            ]
            + [whole(a) for a in returned[m]]
            + [whole(a) for a in acc]
            + ([whole(a) for a in (proj_acc[0], gain_a, shift_a)] if final else []),
            [slots_out(turned)]
            + (
                [whole_out((2, width, width), f32), whole_out((3 * width, 1), f32), whole_out((2, dim), f32)]
                + [whole_out((dim // chunks, 4 * width), bf16)] * chunks
                if final
                else [whole_out((3 * width, dim), f32), whole_out((2, width, width), f32), whole_out((3 * width, 1), f32)]
            ),
            (
                [pltpu.VMEM((3 * width, dim), f32), pltpu.VMEM((2, width, width), f32), pltpu.VMEM((3 * width, 1), f32)]
                if final
                else []
            )
            + [pltpu.VMEM((used, 2 * size), f32), pltpu.VMEM((dim, 4 * width), f32)],
            4 * tokens * dim * 3 * width + 16 * tokens * tile * width,
        )
        attn_parts.append(result[0])
        acc = result[1:]
    grad_maps, grad_qkv_bias, attn_vectors, qkv_grads = acc[0], acc[1], acc[2], acc[3:]
    if direct:
        qkv_terms = [qkv_grads[0]] + [around(qkv_grads[k], "dp", k, count) for k in range(1, count)]
        qkv_sum = sum(a.astype(f32) for a in qkv_terms)
    else:
        qkv_sum = lax.psum_scatter(qkv_grads[0], "dp", scatter_dimension=0, tiled=True).astype(f32)
    input_grads = []
    for m in range(micro):
        kept, arrived = scatter_tensor(attn_parts[m])
        (finished,) = call(
            last_kernel, (1,), ids,
            [own_rows(inputs, m), whole(kept), whole(arrived), whole(grad_residuals[m]), whole(gain_a)],
            [whole_out((tile, dim), bf16)], [], 0,
        )
        input_grads.append(gather_tensor(finished))

    def ordered(slots_of):
        flat = [a for slot in slots_of for a in slot]
        (result,) = call(
            functools.partial(order_kernel, len(flat)), (len(flat),), ids,
            [whole(a) for a in flat],
            [(
                (micro, tokens, dim), bf16, (None, tile, dim),
                lambda i, ids: (lax.div(i, tiles), ids[0] ^ relative(lax.rem(i, tiles)), 0),
            )],
            [], 0,
        )
        return result

    mlp_shift_grad = mlp_vectors[:, 1]
    mlp_gain_grad = (mlp_vectors[:, 0] - mlp_shift.astype(f32) * mlp_shift_grad) / mlp_gain.astype(f32)
    shared = jnp.concatenate([attn_vectors, sum(row_sums), mlp_gain_grad[None], mlp_shift_grad[None]], axis=0)
    shared = shared + swap(shared, 1)
    shared = shared + swap(shared, 2)
    blocks = jnp.stack([
        grad_maps[:, h * size : (h + 1) * size, h * size : (h + 1) * size] for h in range(heads)
    ], axis=1)
    small = jnp.concatenate([
        shared.reshape(-1, 2 * size), blocks.reshape(-1, 2 * size), grad_fc_bias.reshape(-1, 2 * size),
        jnp.pad(grad_qkv_bias.reshape(-1), (0, -(3 * width) % (2 * size))).reshape(-1, 2 * size),
    ], axis=0)
    if direct:
        small_low = small.astype(bf16)
        terms = [around(small_low, "dp", k, count) for k in range(1, count)]
        small = small + sum(a.astype(f32) for a in terms)
        small = lax.optimization_barrier(small)
    else:
        small = lax.psum(small, "dp")
    n_shared = 6 * dim // (2 * size)
    n_blocks = 2 * heads * size * size // (2 * size)
    n_units = units // (2 * size)
    shared = small[:n_shared].reshape(6, dim)
    blocks = small[n_shared : n_shared + n_blocks].reshape(2, heads, size, size)
    grad_fc_bias = small[n_shared + n_blocks : n_shared + n_blocks + n_units].reshape(units)
    grad_qkv_bias = small[n_shared + n_blocks + n_units :].reshape(-1)[: 3 * width].reshape(3, width)
    return (
        ordered(outputs),
        ordered(input_grads),
        shared[0],
        shared[1],
        qkv_sum[:, : 3 * width].reshape(shard, 3, width),
        grad_qkv_bias,
        blocks[0],
        blocks[1],
        qkv_sum[:, 3 * width :].T,
        shared[2],
        shared[4],
        shared[5],
        rest_sum[:, :units],
        grad_fc_bias,
        rest_sum[:, units:].T,
        shared[3],
    )


def solution(mesh):
    in_specs = (
        P(None, "dp", None), P(None, "dp", None), P(None, "dp"), P(), P(), P("dp", None, "tensor"),
        P(None, "tensor"), P("tensor", None, None), P("tensor", None, None), P("tensor", "dp"), P(), P(), P(),
        P("dp", "tensor"), P("tensor"), P("tensor", "dp"), P(),
    )
    out_specs = (
        P(None, "dp", None), P(None, "dp", None), P(), P(), P("dp", None, "tensor"), P(None, "tensor"),
        P("tensor", None, None), P("tensor", None, None), P("tensor", "dp"), P(), P(), P(),
        P("dp", "tensor"), P("tensor"), P("tensor", "dp"), P(),
    )
    return jax.shard_map(
        on_device, mesh=mesh, in_specs=in_specs, out_specs=out_specs, check_vma=False
    )
```

```python
import functools

import jax
import jax.numpy as jnp
from jax import lax
from jax.experimental import pallas as pl
from jax.experimental.pallas import tpu as pltpu
from jax.sharding import PartitionSpec as P

SEQ_LEN = 8192
MAX_SEGMENT = 4096
EPSILON = 1e-05
GELU_SCALE = 0.7978845608028654
GELU_CUBIC = 0.044715
PAD = 16
SMALL = 48

f32 = jnp.float32
bf16 = jnp.bfloat16


def dot_nn(a, b):
    return lax.dot_general(a, b, (((1,), (0,)), ((), ())), preferred_element_type=f32)


def dot_nt(a, b):
    return lax.dot_general(a, b, (((1,), (1,)), ((), ())), preferred_element_type=f32)


def dot_tn(a, b):
    return lax.dot_general(a, b, (((0,), (0,)), ((), ())), preferred_element_type=f32)


def split(value):
    high = value.astype(bf16)
    return high, (value - high.astype(f32)).astype(bf16)


def norm_parts(values):
    centred = values - jnp.mean(values, axis=-1, keepdims=True)
    inverse = lax.rsqrt(jnp.mean(centred * centred, axis=-1, keepdims=True) + EPSILON)
    return centred * inverse, inverse


def norm_back(grad, normed, inverse, gain):
    scaled = grad * gain
    return inverse * (
        scaled
        - jnp.mean(scaled, axis=-1, keepdims=True)
        - normed * jnp.mean(scaled * normed, axis=-1, keepdims=True)
    )


def softmax_rows(values):
    raised = jnp.exp(values - jnp.max(values, axis=0, keepdims=True))
    return raised * (1.0 / jnp.sum(raised, axis=0, keepdims=True))


def relative(value):
    return ((value & 1) << 1) | (value >> 1)


def with_ones(values):
    width = values.shape[1]
    rows = lax.broadcasted_iota(jnp.int32, (PAD, width), 0)
    return jnp.concatenate([values, (rows == 0).astype(f32).astype(bf16)], axis=0)


def call(kernel, grid, ids, inputs, outputs, scratch, flops, aliases=None):
    moved = sum(a.size * a.dtype.itemsize for a, _, _ in inputs)
    return pl.pallas_call(
        kernel,
        grid_spec=pltpu.PrefetchScalarGridSpec(
            num_scalar_prefetch=1,
            grid=grid,
            in_specs=[
                pl.BlockSpec(block, index) if block else pl.BlockSpec(memory_space=pl.ANY)
                for _, block, index in inputs
            ],
            out_specs=[pl.BlockSpec(block, index) for _, _, block, index in outputs],
            scratch_shapes=scratch,
        ),
        out_shape=[jax.ShapeDtypeStruct(shape, kind) for shape, kind, _, _ in outputs],
        cost_estimate=pl.CostEstimate(flops=flops, bytes_accessed=moved, transcendentals=0),
        input_output_aliases=aliases or {},
        compiler_params=pltpu.CompilerParams(dimension_semantics=("arbitrary",) * len(grid)),
    )(ids, *[a for a, _, _ in inputs])


def whole(array):
    return (array, array.shape, lambda i, ids: (0,) * array.ndim)


def whole_out(shape, kind):
    return (shape, kind, shape, lambda i, ids: (0,) * len(shape))


def norm_kernel(ids, x, gain, shift, attn_in):
    normed, _ = norm_parts(x[...].astype(f32))
    attn_in[...] = (normed * gain[...] + shift[...]).astype(bf16)


def project_kernel(heads, tiles, ids, attn_in, weight, bias, maps, seg, seg_last, qkv, feats, state, total, turned):
    step = pl.program_id(0)
    wide = bias.shape[0]

    @pl.when(step == 0)
    def _():
        turned[...] = weight[:, :wide].T

    low = (dot_nt(turned[...], attn_in[...]) + bias[...]).astype(bf16)
    qkv[...] = low
    width = wide // 3
    size = width // heads
    mapped = [dot_nn(maps[part], low[part * width : (part + 1) * width]) for part in range(2)]

    @pl.when(lax.rem(step, tiles) == 0)
    def _():
        total[...] = jnp.zeros_like(total)

    tail = (seg[...] == seg_last[:, -1:]).astype(f32).astype(bf16)
    for head in range(heads):
        for part in range(2):
            own = mapped[part][head * size : (head + 1) * size]
            both = jnp.concatenate([softmax_rows(own), softmax_rows(-own)], axis=0).astype(bf16)
            at = (part * heads + head) * 2 * size
            feats[at : at + 2 * size, :] = both
        value = with_ones(low[2 * width + head * size : 2 * width + (head + 1) * size])
        at = head * (size + PAD)
        total[at : at + size + PAD, :] += dot_nt(value * tail, both)

    @pl.when(lax.rem(step, tiles) == tiles - 1)
    def _():
        whole_state = jnp.concatenate(
            [total[...], jnp.broadcast_to(seg_last[:, -1:], (PAD, 2 * size))], axis=0
        ).astype(bf16)
        for copy in range(state.shape[0]):
            state[copy] = whole_state


def pair_mask(seg_col, seg_row):
    tile = seg_row.shape[1]
    early = lax.broadcasted_iota(jnp.int32, (tile, tile), 0)
    late = lax.broadcasted_iota(jnp.int32, (tile, tile), 1)
    return jnp.where(early <= late, (seg_col == seg_row).astype(f32), 0.0)


def attend_kernel(
    heads, pieces, hops, ids, qkv_v, feats, seg, seg_col, received, attended, attended_low, denominators, states, state, previous
):
    step = pl.program_id(0)
    size = qkv_v.shape[0] // heads
    rows = size + PAD
    used = heads * rows
    place = lax.rem(ids[1], pieces)

    @pl.when(step == 0)
    def _():
        start = jnp.zeros((used, 2 * size), f32)
        latest = received[jnp.maximum(ids[1] - 1, 0), used:, :].astype(f32)[:1]
        for hop in range(hops):
            source = jnp.maximum(ids[1] - 1 - hop, 0)
            linked = (received[source, used:, :].astype(f32)[:1] == latest).astype(f32)
            linked = linked * (place > hop).astype(f32)
            start = start + linked * received[source, :used, :].astype(f32)
        state[...] = start
        first = latest[:, :1]
        previous[...] = jnp.broadcast_to(jnp.where(place > 0, first, -2.0), previous.shape)

    row = seg[...]
    end = row[:, -1:]
    mask = pair_mask(seg_col[...], row)
    before = previous[...]
    carried = (row == before).astype(f32)
    tail = (row == end).astype(f32).astype(bf16)
    keep = (before[:, : 2 * size] == end).astype(f32)
    states[...] = state[...]
    for head in range(heads):
        query = feats[head * 2 * size : (head + 1) * 2 * size, :]
        key = feats[(heads + head) * 2 * size : (heads + head + 1) * 2 * size, :]
        value = with_ones(qkv_v[head * size : (head + 1) * size, :])
        scores = (dot_tn(key, query) * mask).astype(bf16)
        own = state[head * rows : (head + 1) * rows, :]
        inter = dot_nn(jnp.concatenate(split(own), axis=0), query)
        both = dot_nn(value, scores) + carried * (inter[:rows] + inter[rows:])
        lower = both[size : size + 1]
        result = both[:size] / lower
        attended[head * size : (head + 1) * size, :] = result
        attended_low[head * size : (head + 1) * size, :] = result.astype(bf16)
        denominators[head : head + 1, :] = lower
        state[head * rows : (head + 1) * rows, :] = keep * own + dot_nt(value * tail, key)
    previous[...] = jnp.broadcast_to(end, previous.shape)


def sum_of(*terms):
    total = terms[0][...].astype(f32)
    for term in terms[1:]:
        total = total + term[...].astype(f32)
    return total


def store_slots(step, ids, low, slots):
    apart = ids[0] ^ step
    if len(slots) == 4:
        slot = relative(apart)
        for at in range(4):

            @pl.when(slot == at)
            def _():
                slots[at][...] = low
    else:
        for at in range(2):

            @pl.when((apart & 1) == at)
            def _():
                slots[at][apart >> 1] = low


def turn_columns(*columns):
    lane = lax.broadcasted_iota(jnp.int32, (columns[0].shape[0], 128), 1)
    wide = jnp.zeros(lane.shape, f32)
    for at, column in enumerate(columns):
        wide = jnp.where(lane == at, column, wide)
    return wide.T[:8]


def mlp_kernel(first, ids, x, cot, a0, a1, a2, a3, p0, p1, p2, p3, proj_bias, gain, shift, fc, out_t, fc_bias, *refs):
    if not first:
        fc_in, out_in, bias_in = refs[:3]
        refs = refs[3:]
    slots = 4 if first else 2
    residual, grad_slots, out_slots, refs = refs[0], refs[1 : 1 + slots], refs[1 + slots : 3 + slots], refs[3 + slots :]
    if not first:
        vectors, products = refs[:2]
        refs = refs[2:]
    fc_acc, out_acc, bias_acc = refs
    step = pl.program_id(0)

    @pl.when(step == 0)
    def _():
        if first:
            fc_acc[...] = jnp.zeros_like(fc_acc)
            out_acc[...] = jnp.zeros_like(out_acc)
            bias_acc[...] = jnp.zeros_like(bias_acc)
        else:
            fc_acc[...] = fc_in[...]
            out_acc[...] = out_in[...]
            bias_acc[...] = bias_in[...]

    resid = x[...].astype(f32) + proj_bias[...]
    for part, proj in zip((a0, a1, a2, a3), (p0, p1, p2, p3)):
        resid = resid + dot_nt(part[...].T, proj[...])
    residual[...] = resid
    normed, _ = norm_parts(resid)
    mlp_in = (normed * gain[...] + shift[...]).astype(bf16)
    preact = dot_nn(mlp_in, fc[...]) + fc_bias[...]
    square = preact * preact
    tangent = jnp.tanh(GELU_SCALE * (preact + GELU_CUBIC * square * preact))
    half = 0.5 * (1.0 + tangent)
    activ = (preact * half).astype(bf16)
    slope = half + 0.5 * preact * (1.0 - tangent * tangent) * GELU_SCALE * (1.0 + 3.0 * GELU_CUBIC * square)
    top = cot[...]
    grad_pre = (dot_nn(top, out_t[...]) * slope).astype(bf16)
    grad_low = dot_nt(grad_pre, fc[...]).astype(bf16)
    out_low = dot_nt(activ, out_t[...]).astype(bf16)
    store_slots(step, ids, grad_low, grad_slots)
    store_slots(step, ids, out_low, out_slots)
    fc_acc[...] += dot_tn(mlp_in, grad_pre)
    out_acc[...] += dot_tn(top, activ)
    bias_acc[...] += jnp.sum(grad_pre.astype(f32), axis=0, keepdims=True)
    if not first:

        @pl.when(step == pl.num_programs(0) - 1)
        def _():
            width = fc_acc.shape[1]
            products[:, :width] = fc_acc[...].astype(bf16)
            products[:, width:] = out_acc[...].astype(bf16)
            wide = fc[...].astype(f32)
            sums = turn_columns(
                jnp.sum(wide * fc_acc[...], axis=1, keepdims=True),
                jnp.sum(wide * bias_acc[...], axis=1, keepdims=True),
            )
            vectors[0:1, :] = (sums[0:1] - shift[...] * sums[1:2]) / gain[...]
            vectors[1:2, :] = sums[1:2]
            vectors[2:3, :] = bias_acc[...]


def middle_kernel(ids, residual, cot, gain, *refs):
    grad_residual, grad_attn, sums = refs[-3:]
    normed, inverse = norm_parts(residual[...])
    grad = sum_of(*refs[:-3])
    top = cot[...].astype(f32)
    total = top + norm_back(grad, normed, inverse, gain[...])
    grad_residual[...] = total
    low = total.astype(bf16)
    grad_attn[...] = low
    sums[0:1, :] = jnp.sum(low.astype(f32), axis=0, keepdims=True)
    sums[1:2, :] = jnp.sum(top, axis=0, keepdims=True)


def last_kernel(ids, x, grad_residual, gain, *refs):
    normed, inverse = norm_parts(x[...].astype(f32))
    grad = sum_of(*refs[:-1])
    refs[-1][...] = (grad_residual[...] + norm_back(grad, normed, inverse, gain[...])).astype(bf16)


def finish_kernel(micro, ids, bias, crossed, *refs):
    out = refs[-1]
    for m in range(micro):
        out[m] = (sum_of(*refs[3 * m : 3 * m + 3]) + bias[...] + crossed[m].astype(f32)).astype(bf16)


def fold_kernel(count, ids, *refs):
    out = refs[-1]
    for at in range(count):
        out[at] = sum_of(*refs[2 * at : 2 * at + 2]).astype(bf16)


def order_kernel(tiles, ids, *refs):
    out = refs[-1]
    for at in range(tiles):

        @pl.when(lax.rem(pl.program_id(0), tiles) == at)
        def _():
            out[...] = refs[at][...]


def before_segment(pieces, tile_index, ids, received, seg_before):
    entering = jnp.where(lax.rem(ids[1], pieces) > 0, received[...].astype(f32)[:1, :1], -2.0)
    return jnp.where(tile_index == 0, entering, seg_before[:, -1:])


def grads_in_kernel(heads, pieces, first, ids, g0, g1, g2, g3, proj_t, feats_q, attended, attended_low, denominators, seg, received, *refs):
    if first:
        grads, state, proj_acc, total, proj = refs
    else:
        proj_in, grads, state, proj_acc, total, proj = refs
    step = pl.program_id(0)
    size = attended.shape[0] // heads
    rows = size + PAD
    used = heads * rows
    before = before_segment(pieces, 0, ids, received, seg)

    @pl.when(step == 0)
    def _():
        proj[...] = proj_t[...].T
        total[...] = jnp.zeros_like(total)
        proj_acc[...] = jnp.zeros_like(proj_acc) if first else proj_in[...]

    def work(source):
        grad = source[...]
        proj_acc[...] += dot_nn(attended_low[...], grad)
        grad_att = dot_nt(proj[...], grad)
        carried = (seg[...] == before).astype(f32)
        for head in range(heads):
            own = grad_att[head * size : (head + 1) * size]
            inverse = 1.0 / denominators[head : head + 1, :]
            lower = -inverse * jnp.sum(own * attended[head * size : (head + 1) * size, :], axis=0, keepdims=True)
            filler = lax.broadcasted_iota(jnp.int32, (PAD, own.shape[1]), 0)
            both = jnp.concatenate([own * inverse, jnp.where(filler == 0, lower, 0.0)], axis=0)
            grads[head * rows : (head + 1) * rows, :] = both
            query = feats_q[head * 2 * size : (head + 1) * 2 * size, :]
            sums = dot_nt(jnp.concatenate(split(both * carried), axis=0), query)
            total[head * rows : (head + 1) * rows, :] += sums[:rows] + sums[rows:]

    for at, source in enumerate((g0, g1, g2, g3)):

        @pl.when(step == at)
        def _():
            work(source)

    @pl.when(step == pl.num_programs(0) - 1)
    def _():
        whole_state = jnp.concatenate(
            [total[...], jnp.broadcast_to(before, (PAD, 2 * size))], axis=0
        ).astype(bf16)
        for copy in range(state.shape[0]):
            state[copy] = whole_state


def softmax_back(grad, positive, negative):
    size = positive.shape[0]
    upper, lower = grad[:size], grad[size:]
    return positive * (upper - jnp.sum(positive * upper, axis=0, keepdims=True)) - negative * (
        lower - jnp.sum(negative * lower, axis=0, keepdims=True)
    )


def grads_kernel(
    heads, pieces, hops, first, ids, qkv, feats, grads, states, seg, seg_col, seg_before, entering, attn_in, weight, maps, maps_back,
    received, *refs
):
    if not first:
        weight_in, map_in, bias_in, proj_in, gain, shift, mlp_rows, sums_a, sums_b = refs[:9]
        refs = refs[9:]
    slots, refs = (refs[:4], refs[4:]) if first else (refs[:2], refs[2:])
    if not first:
        packed, refs = refs[0], refs[1:]
    weight_acc, map_acc, bias_acc, state = refs
    step = pl.program_id(0)
    count = pl.num_programs(0)
    width = qkv.shape[0] // 3
    size = width // heads
    rows = size + PAD
    used = heads * rows
    row = seg[...]
    end = row[:, -1:]

    @pl.when(step == 0)
    def _():
        start = jnp.zeros((used, 2 * size), f32)
        place = lax.rem(ids[1], pieces)
        for hop in range(hops):
            source = jnp.minimum(ids[1] + 1 + hop, received.shape[0] - 1)
            linked = (received[source, used:, :].astype(f32)[:1] == end).astype(f32)
            linked = linked * (place + hop + 1 < pieces).astype(f32)
            start = start + linked * received[source, :used, :].astype(f32)
        state[...] = start
        if first:
            weight_acc[...] = jnp.zeros_like(weight_acc)
            map_acc[...] = jnp.zeros_like(map_acc)
            bias_acc[...] = jnp.zeros_like(bias_acc)
        else:
            weight_acc[...] = weight_in[...]
            map_acc[...] = map_in[...]
            bias_acc[...] = bias_in[...]

    before = before_segment(pieces, count - 1 - step, ids, entering, seg_before)
    mask = pair_mask(seg_col[...], row)
    carried = (row == before).astype(f32)
    tail = (row == end).astype(f32)
    keep = (before == end).astype(f32)
    mapped = [dot_nn(maps[part], qkv[part * width : (part + 1) * width, :]) for part in range(2)]
    back = [[], []]
    grad_values = []
    for head in range(heads):
        query = feats[head * 2 * size : (head + 1) * 2 * size, :]
        key = feats[(heads + head) * 2 * size : (heads + head + 1) * 2 * size, :]
        at = 2 * width + head * size
        value = with_ones(qkv[at : at + size, :])
        value_two = jnp.concatenate([value, value], axis=0)
        own = grads[head * rows : (head + 1) * rows, :]
        high, low = split(own)
        grad_two = jnp.concatenate([high, low], axis=0)
        scores = (dot_tn(key, query) * mask).astype(bf16)
        grad_scores = (dot_tn(value_two, grad_two) * mask).astype(bf16)
        into = states[head * rows : (head + 1) * rows, :]
        into_high, into_low = split(into)
        inter = dot_tn(
            jnp.concatenate([into_high, into_low, into_high], axis=0),
            jnp.concatenate([high, high, low], axis=0),
        )
        grad_query = dot_nn(key, grad_scores) + carried * inter
        after = state[head * rows : (head + 1) * rows, :]
        after_two = jnp.concatenate(split(after), axis=0)
        grad_key = dot_nt(query, grad_scores) + tail * dot_tn(after_two, value_two)
        straight = dot_nt(grad_two, scores)
        through = dot_nn(after_two, key)
        grad_values.append(
            straight[:size] + straight[rows : rows + size] + tail * (through[:size] + through[rows : rows + size])
        )
        carried_two = jnp.concatenate(split(own * carried), axis=0)
        added = dot_nt(carried_two, query)
        state[head * rows : (head + 1) * rows, :] = keep * after + added[:rows] + added[rows:]
        for part, grad in ((0, grad_query), (1, grad_key)):
            plain = mapped[part][head * size : (head + 1) * size]
            back[part].append(softmax_back(grad, softmax_rows(plain), softmax_rows(-plain)))
    pieces_low = []
    for part in range(2):
        grad_mapped = jnp.concatenate(back[part], axis=0).astype(bf16)
        map_acc[part] += dot_nt(qkv[part * width : (part + 1) * width, :], grad_mapped)
        pieces_low.append(dot_nn(maps_back[part], grad_mapped))
    pieces_low.append(jnp.concatenate(grad_values, axis=0))
    grad_qkv = jnp.concatenate(pieces_low, axis=0).astype(bf16)
    part_low = dot_nt(grad_qkv.T, weight[:, : 3 * width]).astype(bf16)
    store_slots(count - 1 - step, ids, part_low, slots)
    weight_acc[...] += dot_nn(grad_qkv, attn_in[...])
    bias_acc[...] += jnp.sum(grad_qkv.astype(f32), axis=1, keepdims=True)
    if not first:

        @pl.when(step == count - 1)
        def _():
            wide = weight[:, : 3 * width].astype(f32)
            total = weight_acc[...].T
            bias_row = turn_columns(bias_acc[...])[0:1]
            sums = turn_columns(
                jnp.sum(wide * total, axis=1, keepdims=True), jnp.sum(wide * bias_row, axis=1, keepdims=True)
            )
            dim = wide.shape[0]
            blocks = []
            for part in range(2):
                lane = lax.broadcasted_iota(jnp.int32, (size, width), 1) // size
                own = jnp.zeros((size, width), f32)
                for head in range(heads):
                    own = jnp.where(lane == head, map_acc[part, head * size : (head + 1) * size, :], own)
                blocks.append(own)
            half = size // 2
            turned = jnp.concatenate(
                [blocks[0][:half], blocks[1][:half], blocks[0][half:], blocks[1][half:]], axis=1
            )
            lines = [
                (sums[0:1] - shift[...] * sums[1:2]) / gain[...],
                sums[1:2],
                sums_a[...] + sums_b[...],
                mlp_rows[...],
                jnp.concatenate([bias_row, jnp.zeros((1, dim - 3 * width), f32)], axis=1),
                turned,
            ]
            small = jnp.concatenate(lines, axis=0)
            small = jnp.concatenate([small, jnp.zeros((SMALL - small.shape[0], dim), f32)], axis=0).astype(bf16)
            proj_total = proj_in[...].T
            shard = packed.shape[1] - SMALL
            for copy in range(packed.shape[0]):
                packed[copy, :SMALL, :] = small
                at = copy * shard
                packed[copy, SMALL:, : 3 * width] = total[at : at + shard].astype(bf16)
                packed[copy, SMALL:, 3 * width :] = proj_total[at : at + shard].astype(bf16)


def exchange(array):
    return lax.all_to_all(array, "dp", 0, 0)


def gather_dp(array):
    return exchange(jnp.broadcast_to(array, (lax.axis_size("dp"),) + array.shape)).reshape(-1, array.shape[1])


def swap(array, bit):
    return lax.ppermute(array, "tensor", [(i, i ^ bit) for i in range(4)])


def gather_tensor(array, direct=False):
    across = swap(array, 2)
    return (array, across, swap(array, 1), swap(array, 3) if direct else swap(across, 1))


def scatter_tensor(slots):
    return (slots[0], swap(slots[1], 2), swap(slots[2], 1), swap(slots[3], 3))


def block_diagonal(blocks):
    count, size, _ = blocks.shape
    eye = jnp.eye(count, dtype=blocks.dtype)
    return (eye[:, None, :, None] * blocks[:, :, None, :]).reshape(count * size, count * size)


def on_device(
    inputs, cotangent, segment, attn_gain, attn_shift, qkv_weight, qkv_bias, query_map, key_map,
    proj_weight, proj_bias, mlp_gain, mlp_shift, fc_weight, fc_bias, out_weight, out_bias,
):
    micro, tokens, dim = inputs.shape
    heads, size, _ = query_map.shape
    width = heads * size
    units = fc_weight.shape[1]
    count = lax.axis_size("dp")
    tiles = lax.axis_size("tensor")
    tile = tokens // tiles
    pieces = SEQ_LEN // tokens
    hops = min(-(-MAX_SEGMENT // tokens), pieces - 1)
    rows = size + PAD
    used = heads * rows
    shard = dim // count
    ids = jnp.stack([lax.axis_index("tensor"), lax.axis_index("dp")]).astype(jnp.int32)

    weight = gather_dp(jnp.concatenate([qkv_weight.reshape(shard, 3 * width), proj_weight.T], axis=1))
    proj_t = weight[:, 3 * width :]
    proj_slots = gather_tensor(proj_t)

    row = lambda v: v.astype(f32).reshape(1, -1)
    gain_a, shift_a, gain_m, shift_m = row(attn_gain), row(attn_shift), row(mlp_gain), row(mlp_shift)
    bias_p, bias_f, bias_o = row(proj_bias), row(fc_bias), row(out_bias)
    bias_qkv = qkv_bias.astype(f32).reshape(3 * width, 1)
    maps_back = jnp.stack([block_diagonal(query_map), block_diagonal(key_map)])
    maps = jnp.swapaxes(maps_back, 1, 2)
    seg = segment.astype(f32).reshape(micro, tiles, 1, tile)
    seg_col = segment.astype(f32).reshape(micro, tiles, tile, 1)

    def rows_of(array, m, at=None):
        return (array, (None, tile, dim), lambda i, ids: (m, i if at is None else at(i, ids), 0))

    def own_rows(array, m):
        return (array, (None, tile, dim), lambda i, ids: (m, ids[0], 0))

    def columns(array, at=None, m=0):
        return (
            array, (array.shape[0], tile), lambda i, ids: (0, m * tiles + (i if at is None else at(i, ids)))
        )

    def columns_out(height, kind, at=None):
        return ((height, tokens), kind, (height, tile), lambda i, ids: (0, i if at is None else at(i, ids)))

    def seg_row(m, at=None):
        return (seg, (None, None, 1, tile), lambda i, ids: (m, i if at is None else at(i, ids), 0, 0))

    def seg_column(m, at=None):
        return (seg_col, (None, None, tile, 1), lambda i, ids: (m, i if at is None else at(i, ids), 0, 0))

    def states_of(m):
        return (incoming, (count, used + PAD, 2 * size), lambda i, ids: (0, m, 0))

    def entering(m):
        return (
            incoming, (None, PAD, 2 * size),
            lambda i, ids: (jnp.maximum(ids[1] - 1, 0), (m * (used + PAD) + used) // PAD, 0),
        )

    def half(array, at):
        return (array, (None, tile, dim), lambda i, ids: (at, 0, 0))

    near = lambda i, ids: ids[0] ^ relative(i)

    def pin(*arrays):
        nonlocal ids
        ids, arrays = lax.optimization_barrier((ids, arrays))
        return arrays

    def run(*arguments, **options):
        return pin(*call(arguments[0], arguments[1], ids, *arguments[2:], **options))

    def fold(*pairs):
        (result,) = run(
            functools.partial(fold_kernel, len(pairs)), (1,),
            [half(a, 1) for pair in pairs for a in pair],
            [whole_out((len(pairs), tile, dim), bf16)], [], 0,
        )
        return result

    attn_ins = []
    for m in range(micro):
        (normed,) = run(
            norm_kernel, (tiles,), [rows_of(inputs, m), whole(gain_a), whole(shift_a)],
            [((1, tokens, dim), bf16, (None, tile, dim), lambda i, ids: (0, i, 0))], [], 0,
        )
        attn_ins.append(normed)
        if m == 0:
            fc_own, out_own = pin(fc_weight, out_weight)
            rest = lax.all_gather(jnp.concatenate([fc_own, out_own.T], axis=1), "dp", axis=0, tiled=True)
    fc_block = (rest, (dim, units), lambda i, ids: (0, 0))
    out_block = (rest, (dim, units), lambda i, ids: (0, 1))
    state_out = ((count, used + PAD, 2 * size), bf16)
    every = micro * tiles
    attn_in = jnp.concatenate(attn_ins, axis=0)
    qkv, feats, state = run(
        functools.partial(project_kernel, heads, tiles), (every,),
        [
            (attn_in, (None, tile, dim), lambda i, ids: (lax.div(i, tiles), lax.rem(i, tiles), 0)),
            whole(weight), whole(bias_qkv), whole(maps),
            (seg, (None, None, 1, tile), lambda i, ids: (lax.div(i, tiles), lax.rem(i, tiles), 0, 0)),
            (seg, (None, None, 1, tile), lambda i, ids: (lax.div(i, tiles), tiles - 1, 0, 0)),
        ],
        [
            ((3 * width, micro * tokens), bf16, (3 * width, tile), lambda i, ids: (0, i)),
            ((4 * width, micro * tokens), bf16, (4 * width, tile), lambda i, ids: (0, i)),
            (
                (count, micro * (used + PAD), 2 * size), bf16, (count, used + PAD, 2 * size),
                lambda i, ids: (0, lax.div(i, tiles), 0),
            ),
        ],
        [pltpu.VMEM((used, 2 * size), f32), pltpu.VMEM((3 * width, dim), bf16)],
        2 * micro * tokens * dim * 3 * width,
    )
    incoming = exchange(state)
    attended, attended_low, denominators, states, slots = [], [], [], [], []
    for m in range(micro):
        result = run(
            functools.partial(attend_kernel, heads, pieces, hops), (tiles,),
            [
                (qkv, (width, tile), lambda i, ids, m=m: (2, m * tiles + i)), columns(feats, None, m), seg_row(m), seg_column(m),
                states_of(m),
            ],
            [
                columns_out(width, f32), columns_out(width, bf16), columns_out(8, f32),
                ((tiles, used, 2 * size), f32, (None, used, 2 * size), lambda i, ids: (i, 0, 0)),
            ],
            [pltpu.VMEM((used, 2 * size), f32), pltpu.VMEM((1, tile), f32)],
            4 * tokens * tile * width,
        )
        attended.append(result[0])
        attended_low.append(result[1])
        denominators.append(result[2])
        states.append(result[3])
        slots.append(gather_tensor(result[1]))

    acc = ()
    residuals, mlp_terms, out_pairs = [], [], []
    for m in range(micro):
        final = m == micro - 1
        kept = [((dim, units), f32), ((dim, units), f32), ((1, units), f32)]
        pair = [whole_out((2, tile, dim), bf16)] * 2
        result = run(
            functools.partial(mlp_kernel, not final), (tiles,),
            [rows_of(inputs, m), rows_of(cotangent, m)]
            + [columns(a) for a in slots[m]]
            + [whole(a) for a in proj_slots]
            + [whole(bias_p), whole(gain_m), whole(shift_m), fc_block, out_block, whole(bias_f)]
            + [whole(a) for a in acc],
            [((tiles, tile, dim), f32, (None, tile, dim), lambda i, ids: (i, 0, 0))]
            + (pair if final else [whole_out((tile, dim), bf16)] * 4)
            + pair
            + ([whole_out((3, dim), f32), whole_out((dim, 2 * units), bf16)] if final else [whole_out(*k) for k in kept]),
            [pltpu.VMEM(*k) for k in kept] if final else [],
            2 * tokens * dim * (dim + 6 * units),
        )
        residuals.append(result[0])
        parts = result[1:3] if final else result[1:5]
        mlp_terms.append((parts[0], swap(parts[1], 1)) if final else scatter_tensor(parts))
        result = result[3:] if final else result[5:]
        out_pairs.append((result[0], swap(result[1], 1)))
        acc = result[2:]
    mlp_rows, rest_grads = acc

    own_tile = lambda array: (array, (None, tile, dim), lambda i, ids: (ids[0], 0, 0))
    grad_residuals, grad_slots, row_sums = [], [], []

    def middle(m, terms):
        grad_residual, grad_attn, sums = run(
            middle_kernel, (1,), [own_tile(residuals[m]), own_rows(cotangent, m), whole(gain_m)] + terms,
            [whole_out((tile, dim), f32), whole_out((tile, dim), bf16), whole_out((2, dim), f32)],
            [], 0,
        )
        grad_residuals.append(grad_residual)
        grad_slots.append(gather_tensor(grad_attn))
        row_sums.append(sums)

    proj_acc = ()
    grads, returned = [], []

    def grads_in(m):
        nonlocal proj_acc
        result = run(
            functools.partial(grads_in_kernel, heads, pieces, m == 0), (tiles,),
            [whole(a) for a in grad_slots[m]]
            + [
                whole(proj_t), (feats, (2 * width, tile), lambda i, ids: (0, m * tiles + near(i, ids))),
                columns(attended[m], near), columns(attended_low[m], near), columns(denominators[m], near),
                seg_row(m, near), entering(m),
            ]
            + [whole(a) for a in proj_acc],
            [columns_out(used, f32, near), whole_out(*state_out), whole_out((width, dim), f32)],
            [pltpu.VMEM((used, 2 * size), f32), pltpu.VMEM((width, dim), bf16)],
            4 * tokens * dim * width,
        )
        grads.append(result[0])
        proj_acc = (result[2],)
        returned.append(exchange(result[1]))

    acc = ()
    turned = lambda i, ids: tiles - 1 - i

    def attention_back(m):
        nonlocal acc
        final = m == micro - 1
        kept = [((3 * width, dim), f32), ((2, width, width), f32), ((3 * width, 1), f32)]
        result = run(
            functools.partial(grads_kernel, heads, pieces, hops, not final), (tiles,),
            [
                columns(qkv, turned, m), columns(feats, turned, m), columns(grads[m], turned),
                (states[m], (None, used, 2 * size), lambda i, ids: (tiles - 1 - i, 0, 0)),
                seg_row(m, turned), seg_column(m, turned), seg_row(m, lambda i, ids: jnp.maximum(tiles - 2 - i, 0)),
                entering(m), rows_of(attn_in, m, turned),
                whole(weight), whole(maps), whole(maps_back), whole(returned[m]),
            ]
            + [whole(a) for a in acc]
            + ([whole(a) for a in (proj_acc[0], gain_a, shift_a, mlp_rows, *row_sums)] if final else []),
            ([whole_out((2, tile, dim), bf16)] * 2 if final else [whole_out((tile, dim), bf16)] * 4)
            + ([whole_out((count, SMALL + shard, 4 * width), bf16)] if final else [whole_out(*k) for k in kept]),
            ([pltpu.VMEM(*k) for k in kept] if final else []) + [pltpu.VMEM((used, 2 * size), f32)],
            4 * tokens * dim * 3 * width + 16 * tokens * tile * width,
        )
        acc = result[2:] if final else result[4:]
        return result[:2] if final else result[:4]

    def last(m, terms):
        (finished,) = run(
            last_kernel, (1,), [own_rows(inputs, m), whole(grad_residuals[m]), whole(gain_a)] + terms,
            [whole_out((tile, dim), bf16)], [], 0,
        )
        return gather_tensor(finished)

    def ordered(parts, m, base=()):
        (result,) = run(
            functools.partial(order_kernel, tiles), (tiles,),
            [whole(a) for a in parts] + [(a, None, None) for a in base],
            [((micro, tokens, dim), bf16, (None, tile, dim), lambda i, ids: (m, ids[0] ^ relative(i), 0))],
            [], 0, aliases={tiles + 1: 0} if base else None,
        )
        return result

    def paired(pair, crossed):
        return [half(pair[0], 0), half(pair[1], 0), half(crossed, 0)]

    middle(0, [whole(a) for a in mlp_terms[0]])
    crossed = swap(fold(mlp_terms[1]), 2)
    (rest_grads,) = pin(rest_grads)
    rest_sum = lax.psum_scatter(rest_grads, "dp", scatter_dimension=0, tiled=True)
    grads_in(0)
    middle(1, paired(mlp_terms[1], crossed))
    out_crossed = swap(fold(*out_pairs), 2)
    grads_in(1)
    (finished,) = run(
        functools.partial(finish_kernel, micro), (1,),
        [whole(bias_o), whole(out_crossed)]
        + [spec for m in range(micro) for spec in (own_tile(residuals[m]), half(out_pairs[m][0], 0), half(out_pairs[m][1], 0))],
        [whole_out((micro, tile, dim), bf16)], [], 0,
    )
    outputs = gather_tensor(finished)
    first_terms = scatter_tensor(attention_back(0))
    kept, away = attention_back(1)
    last_pair = (kept, swap(away, 1))
    total = exchange(acc[0])
    crossed = swap(fold(last_pair), 2)
    early = last(0, [whole(a) for a in first_terms])
    (output,) = run(
        functools.partial(order_kernel, tiles), (every,),
        [(a, (None, tile, dim), lambda i, ids: (lax.div(i, tiles), 0, 0)) for a in outputs],
        [(
            (micro, tokens, dim), bf16, (None, tile, dim),
            lambda i, ids: (lax.div(i, tiles), ids[0] ^ relative(lax.rem(i, tiles)), 0),
        )],
        [], 0,
    )
    (rest_sum,) = pin(rest_sum)
    rest_sum = rest_sum.astype(f32)
    fc_grad, out_grad = pin(rest_sum[:, :units], rest_sum[:, units:].T)
    late = last(1, paired(last_pair, crossed))
    input_grad = ordered(early, 0)
    (input_grad,) = (ordered(late, 1, (input_grad,)),)
    total = jnp.sum(total.astype(f32), axis=0)

    shared = total[:6]
    shared = (shared + swap(shared, 1)) + (swap(shared, 2) + swap(shared, 3))
    blocks = total[8 : 8 + size // 2].reshape(size // 2, 2, 2, heads, size)
    blocks = jnp.transpose(blocks, (2, 3, 1, 0, 4)).reshape(2, heads, size, size)
    qkv_sum = total[SMALL:]
    return (
        output,
        input_grad,
        shared[0],
        shared[1],
        qkv_sum[:, : 3 * width].reshape(shard, 3, width),
        total[7, : 3 * width].reshape(3, width),
        blocks[0],
        blocks[1],
        qkv_sum[:, 3 * width :].T,
        shared[2],
        shared[4],
        shared[5],
        fc_grad,
        total[6],
        out_grad,
        shared[3],
    )


def solution(mesh):
    in_specs = (
        P(None, "dp", None), P(None, "dp", None), P(None, "dp"), P(), P(), P("dp", None, "tensor"),
        P(None, "tensor"), P("tensor", None, None), P("tensor", None, None), P("tensor", "dp"), P(), P(), P(),
        P("dp", "tensor"), P("tensor"), P("tensor", "dp"), P(),
    )
    out_specs = (
        P(None, "dp", None), P(None, "dp", None), P(), P(), P("dp", None, "tensor"), P(None, "tensor"),
        P("tensor", None, None), P("tensor", None, None), P("tensor", "dp"), P(), P(), P(),
        P("dp", "tensor"), P("tensor"), P("tensor", "dp"), P(),
    )
    return jax.shard_map(
        on_device, mesh=mesh, in_specs=in_specs, out_specs=out_specs, check_vma=False
    )
```

```python
import functools

import jax
import jax.numpy as jnp
from jax import lax
from jax.experimental import pallas as pl
from jax.experimental.pallas import tpu as pltpu
from jax.sharding import PartitionSpec as P

SEQ_LEN = 8192
MAX_SEGMENT = 4096
EPSILON = 1e-05
GELU_SCALE = 0.7978845608028654
GELU_CUBIC = 0.044715
PAD = 16
SMALL = 48
RATE = 1.1e9

f32 = jnp.float32
bf16 = jnp.bfloat16


def dot_nn(a, b):
    return lax.dot_general(a, b, (((1,), (0,)), ((), ())), preferred_element_type=f32)


def dot_nt(a, b):
    return lax.dot_general(a, b, (((1,), (1,)), ((), ())), preferred_element_type=f32)


def dot_tn(a, b):
    return lax.dot_general(a, b, (((0,), (0,)), ((), ())), preferred_element_type=f32)


def split(value):
    high = value.astype(bf16)
    return high, (value - high.astype(f32)).astype(bf16)


def norm_parts(values):
    centred = values - jnp.mean(values, axis=-1, keepdims=True)
    inverse = lax.rsqrt(jnp.mean(centred * centred, axis=-1, keepdims=True) + EPSILON)
    return centred * inverse, inverse


def norm_back(grad, normed, inverse, gain):
    scaled = grad * gain
    return inverse * (
        scaled
        - jnp.mean(scaled, axis=-1, keepdims=True)
        - normed * jnp.mean(scaled * normed, axis=-1, keepdims=True)
    )


def softmax_rows(values):
    raised = jnp.exp(values - jnp.max(values, axis=0, keepdims=True))
    return raised * (1.0 / jnp.sum(raised, axis=0, keepdims=True))


def relative(value):
    return ((value & 1) << 1) | (value >> 1)


def with_ones(values):
    width = values.shape[1]
    rows = lax.broadcasted_iota(jnp.int32, (PAD, width), 0)
    return jnp.concatenate([values, (rows == 0).astype(f32).astype(bf16)], axis=0)


def call(kernel, grid, ids, inputs, outputs, scratch, micros, aliases=None):
    moved = sum(a.size * a.dtype.itemsize for a, _, _ in inputs)
    return pl.pallas_call(
        kernel,
        grid_spec=pltpu.PrefetchScalarGridSpec(
            num_scalar_prefetch=1,
            grid=grid,
            in_specs=[
                pl.BlockSpec(block, index) if block else pl.BlockSpec(memory_space=pl.ANY)
                for _, block, index in inputs
            ],
            out_specs=[pl.BlockSpec(block, index) for _, _, block, index in outputs],
            scratch_shapes=scratch,
        ),
        out_shape=[jax.ShapeDtypeStruct(shape, kind) for shape, kind, _, _ in outputs],
        cost_estimate=pl.CostEstimate(flops=int(micros * RATE), bytes_accessed=moved, transcendentals=0),
        input_output_aliases=aliases or {},
        compiler_params=pltpu.CompilerParams(dimension_semantics=("arbitrary",) * len(grid)),
    )(ids, *[a for a, _, _ in inputs])


def whole(array):
    return (array, array.shape, lambda i, ids: (0,) * array.ndim)


def whole_out(shape, kind):
    return (shape, kind, shape, lambda i, ids: (0,) * len(shape))


def norm_kernel(ids, x, gain, shift, attn_in):
    normed, _ = norm_parts(x[...].astype(f32))
    attn_in[...] = (normed * gain[...] + shift[...]).astype(bf16)


def project_kernel(heads, tiles, ids, attn_in, weight, bias, maps, seg, seg_last, qkv, feats, state, total, turned):
    step = pl.program_id(0)
    wide = bias.shape[0]

    @pl.when(step == 0)
    def _():
        turned[...] = weight[:, :wide].T

    low = (dot_nt(turned[...], attn_in[...]) + bias[...]).astype(bf16)
    qkv[...] = low
    width = wide // 3
    size = width // heads
    mapped = [dot_nn(maps[part], low[part * width : (part + 1) * width]) for part in range(2)]

    @pl.when(lax.rem(step, tiles) == 0)
    def _():
        total[...] = jnp.zeros_like(total)

    tail = (seg[...] == seg_last[:, -1:]).astype(f32).astype(bf16)
    for head in range(heads):
        for part in range(2):
            own = mapped[part][head * size : (head + 1) * size]
            both = jnp.concatenate([softmax_rows(own), softmax_rows(-own)], axis=0).astype(bf16)
            at = (part * heads + head) * 2 * size
            feats[at : at + 2 * size, :] = both
        value = with_ones(low[2 * width + head * size : 2 * width + (head + 1) * size])
        at = head * (size + PAD)
        total[at : at + size + PAD, :] += dot_nt(value * tail, both)

    @pl.when(lax.rem(step, tiles) == tiles - 1)
    def _():
        state[...] = jnp.concatenate(
            [total[...], jnp.broadcast_to(seg_last[:, -1:], (PAD, 2 * size))], axis=0
        ).astype(bf16)


def pair_mask(seg_col, seg_row):
    tile = seg_row.shape[1]
    early = lax.broadcasted_iota(jnp.int32, (tile, tile), 0)
    late = lax.broadcasted_iota(jnp.int32, (tile, tile), 1)
    return jnp.where(early <= late, (seg_col == seg_row).astype(f32), 0.0)


def attend_kernel(
    heads, pieces, hops, ids, qkv_v, feats, seg, seg_col, *refs
):
    received, (attended, attended_low, denominators, states, state, previous) = refs[:hops], refs[hops:]
    step = pl.program_id(0)
    size = qkv_v.shape[0] // heads
    rows = size + PAD
    used = heads * rows
    place = lax.rem(ids[1], pieces)

    @pl.when(step == 0)
    def _():
        start = jnp.zeros((used, 2 * size), f32)
        latest = received[0][used:, :].astype(f32)[:1]
        for hop in range(hops):
            linked = (received[hop][used:, :].astype(f32)[:1] == latest).astype(f32)
            linked = linked * (place > hop).astype(f32)
            start = start + linked * received[hop][:used, :].astype(f32)
        state[...] = start
        first = latest[:, :1]
        previous[...] = jnp.broadcast_to(jnp.where(place > 0, first, -2.0), previous.shape)

    row = seg[...]
    end = row[:, -1:]
    mask = pair_mask(seg_col[...], row)
    before = previous[...]
    carried = (row == before).astype(f32)
    tail = (row == end).astype(f32).astype(bf16)
    keep = (before[:, : 2 * size] == end).astype(f32)
    states[...] = state[...]
    for head in range(heads):
        query = feats[head * 2 * size : (head + 1) * 2 * size, :]
        key = feats[(heads + head) * 2 * size : (heads + head + 1) * 2 * size, :]
        value = with_ones(qkv_v[head * size : (head + 1) * size, :])
        scores = (dot_tn(key, query) * mask).astype(bf16)
        own = state[head * rows : (head + 1) * rows, :]
        inter = dot_nn(jnp.concatenate(split(own), axis=0), query)
        both = dot_nn(value, scores) + carried * (inter[:rows] + inter[rows:])
        lower = both[size : size + 1]
        result = both[:size] / lower
        attended[head * size : (head + 1) * size, :] = result
        attended_low[head * size : (head + 1) * size, :] = result.astype(bf16)
        denominators[head : head + 1, :] = lower
        state[head * rows : (head + 1) * rows, :] = keep * own + dot_nt(value * tail, key)
    previous[...] = jnp.broadcast_to(end, previous.shape)


def sum_of(*terms):
    total = terms[0][...].astype(f32)
    for term in terms[1:]:
        total = total + term[...].astype(f32)
    return total


def store_slots(step, ids, low, slots):
    apart = ids[0] ^ step
    if len(slots) == 4:
        slot = relative(apart)
        for at in range(4):

            @pl.when(slot == at)
            def _():
                slots[at][...] = low
    else:
        for at in range(2):

            @pl.when((apart & 1) == at)
            def _():
                slots[at][apart >> 1] = low


def turn_columns(*columns):
    lane = lax.broadcasted_iota(jnp.int32, (columns[0].shape[0], 128), 1)
    wide = jnp.zeros(lane.shape, f32)
    for at, column in enumerate(columns):
        wide = jnp.where(lane == at, column, wide)
    return wide.T[:8]


def mlp_kernel(first, ids, x, cot, a0, a1, a2, a3, p0, p1, p2, p3, proj_bias, gain, shift, fc, out_t, fc_bias, *refs):
    if not first:
        fc_in, out_in, bias_in = refs[:3]
        refs = refs[3:]
    slots = 4 if first else 2
    residual, grad_slots, out_slots, refs = refs[0], refs[1 : 1 + slots], refs[1 + slots : 3 + slots], refs[3 + slots :]
    if not first:
        vectors, products = refs[:2]
        refs = refs[2:]
    fc_acc, out_acc, bias_acc = refs
    step = pl.program_id(0)

    @pl.when(step == 0)
    def _():
        if first:
            fc_acc[...] = jnp.zeros_like(fc_acc)
            out_acc[...] = jnp.zeros_like(out_acc)
            bias_acc[...] = jnp.zeros_like(bias_acc)
        else:
            fc_acc[...] = fc_in[...]
            out_acc[...] = out_in[...]
            bias_acc[...] = bias_in[...]

    resid = x[...].astype(f32) + proj_bias[...]
    for part, proj in zip((a0, a1, a2, a3), (p0, p1, p2, p3)):
        resid = resid + dot_nt(part[...].T, proj[...])
    residual[...] = resid
    normed, _ = norm_parts(resid)
    mlp_in = (normed * gain[...] + shift[...]).astype(bf16)
    preact = dot_nn(mlp_in, fc[...]) + fc_bias[...]
    square = preact * preact
    tangent = jnp.tanh(GELU_SCALE * (preact + GELU_CUBIC * square * preact))
    half = 0.5 * (1.0 + tangent)
    activ = (preact * half).astype(bf16)
    slope = half + 0.5 * preact * (1.0 - tangent * tangent) * GELU_SCALE * (1.0 + 3.0 * GELU_CUBIC * square)
    top = cot[...]
    grad_pre = (dot_nn(top, out_t[...]) * slope).astype(bf16)
    grad_low = dot_nt(grad_pre, fc[...]).astype(bf16)
    out_low = dot_nt(activ, out_t[...]).astype(bf16)
    store_slots(step, ids, grad_low, grad_slots)
    store_slots(step, ids, out_low, out_slots)
    fc_acc[...] += dot_tn(mlp_in, grad_pre)
    out_acc[...] += dot_tn(top, activ)
    bias_acc[...] += jnp.sum(grad_pre.astype(f32), axis=0, keepdims=True)
    if not first:

        @pl.when(step == pl.num_programs(0) - 1)
        def _():
            width = fc_acc.shape[1]
            products[:, :width] = fc_acc[...].astype(bf16)
            products[:, width:] = out_acc[...].astype(bf16)
            wide = fc[...].astype(f32)
            sums = turn_columns(
                jnp.sum(wide * fc_acc[...], axis=1, keepdims=True),
                jnp.sum(wide * bias_acc[...], axis=1, keepdims=True),
            )
            vectors[0:1, :] = (sums[0:1] - shift[...] * sums[1:2]) / gain[...]
            vectors[1:2, :] = sums[1:2]
            vectors[2:3, :] = bias_acc[...]


def middle_kernel(ids, residual, cot, gain, *refs):
    grad_residual, grad_attn, sums = refs[-3:]
    normed, inverse = norm_parts(residual[...])
    grad = sum_of(*refs[:-3])
    top = cot[...].astype(f32)
    total = top + norm_back(grad, normed, inverse, gain[...])
    grad_residual[...] = total
    low = total.astype(bf16)
    grad_attn[...] = low
    sums[0:1, :] = jnp.sum(low.astype(f32), axis=0, keepdims=True)
    sums[1:2, :] = jnp.sum(top, axis=0, keepdims=True)


def last_kernel(ids, x, grad_residual, gain, *refs):
    normed, inverse = norm_parts(x[...].astype(f32))
    grad = sum_of(*refs[:-1])
    refs[-1][...] = (grad_residual[...] + norm_back(grad, normed, inverse, gain[...])).astype(bf16)


def finish_kernel(micro, ids, bias, crossed, *refs):
    out = refs[-1]
    for m in range(micro):
        out[m] = (sum_of(*refs[3 * m : 3 * m + 3]) + bias[...] + crossed[m].astype(f32)).astype(bf16)


def fold_kernel(count, ids, *refs):
    out = refs[-1]
    for at in range(count):
        out[at] = sum_of(*refs[2 * at : 2 * at + 2]).astype(bf16)


def order_kernel(tiles, ids, *refs):
    out = refs[-1]
    for at in range(tiles):

        @pl.when(lax.rem(pl.program_id(0), tiles) == at)
        def _():
            out[...] = refs[at][...]


def before_segment(pieces, tile_index, ids, received, seg_before):
    entering = jnp.where(lax.rem(ids[1], pieces) > 0, received[...].astype(f32)[:1, :1], -2.0)
    return jnp.where(tile_index == 0, entering, seg_before[:, -1:])


def grads_in_kernel(heads, pieces, first, ids, g0, g1, g2, g3, proj_t, feats_q, attended, attended_low, denominators, seg, received, *refs):
    if first:
        grads, state, proj_acc, total, proj = refs
    else:
        proj_in, grads, state, proj_acc, total, proj = refs
    step = pl.program_id(0)
    size = attended.shape[0] // heads
    rows = size + PAD
    used = heads * rows
    before = before_segment(pieces, 0, ids, received, seg)

    @pl.when(step == 0)
    def _():
        proj[...] = proj_t[...].T
        total[...] = jnp.zeros_like(total)
        proj_acc[...] = jnp.zeros_like(proj_acc) if first else proj_in[...]

    def work(source):
        grad = source[...]
        proj_acc[...] += dot_nn(attended_low[...], grad)
        grad_att = dot_nt(proj[...], grad)
        carried = (seg[...] == before).astype(f32)
        for head in range(heads):
            own = grad_att[head * size : (head + 1) * size]
            inverse = 1.0 / denominators[head : head + 1, :]
            lower = -inverse * jnp.sum(own * attended[head * size : (head + 1) * size, :], axis=0, keepdims=True)
            filler = lax.broadcasted_iota(jnp.int32, (PAD, own.shape[1]), 0)
            both = jnp.concatenate([own * inverse, jnp.where(filler == 0, lower, 0.0)], axis=0)
            grads[head * rows : (head + 1) * rows, :] = both
            query = feats_q[head * 2 * size : (head + 1) * 2 * size, :]
            sums = dot_nt(jnp.concatenate(split(both * carried), axis=0), query)
            total[head * rows : (head + 1) * rows, :] += sums[:rows] + sums[rows:]

    for at, source in enumerate((g0, g1, g2, g3)):

        @pl.when(step == at)
        def _():
            work(source)

    @pl.when(step == pl.num_programs(0) - 1)
    def _():
        whole_state = jnp.concatenate(
            [total[...], jnp.broadcast_to(before, (PAD, 2 * size))], axis=0
        ).astype(bf16)
        for copy in range(state.shape[0]):
            state[copy] = whole_state


def softmax_back(grad, positive, negative):
    size = positive.shape[0]
    upper, lower = grad[:size], grad[size:]
    return positive * (upper - jnp.sum(positive * upper, axis=0, keepdims=True)) - negative * (
        lower - jnp.sum(negative * lower, axis=0, keepdims=True)
    )


def grads_kernel(
    heads, pieces, hops, first, ids, qkv, feats, grads, states, seg, seg_col, seg_before, entering, attn_in, weight, maps, maps_back,
    received, *refs
):
    if not first:
        weight_in, map_in, bias_in, proj_in, gain, shift, mlp_rows, sums_a, sums_b = refs[:9]
        refs = refs[9:]
    slots, refs = (refs[:4], refs[4:]) if first else (refs[:2], refs[2:])
    if not first:
        packed, refs = refs[0], refs[1:]
    weight_acc, map_acc, bias_acc, state = refs
    step = pl.program_id(0)
    count = pl.num_programs(0)
    width = qkv.shape[0] // 3
    size = width // heads
    rows = size + PAD
    used = heads * rows
    row = seg[...]
    end = row[:, -1:]

    @pl.when(step == 0)
    def _():
        start = jnp.zeros((used, 2 * size), f32)
        place = lax.rem(ids[1], pieces)
        for hop in range(hops):
            source = jnp.minimum(ids[1] + 1 + hop, received.shape[0] - 1)
            linked = (received[source, used:, :].astype(f32)[:1] == end).astype(f32)
            linked = linked * (place + hop + 1 < pieces).astype(f32)
            start = start + linked * received[source, :used, :].astype(f32)
        state[...] = start
        if first:
            weight_acc[...] = jnp.zeros_like(weight_acc)
            map_acc[...] = jnp.zeros_like(map_acc)
            bias_acc[...] = jnp.zeros_like(bias_acc)
        else:
            weight_acc[...] = weight_in[...]
            map_acc[...] = map_in[...]
            bias_acc[...] = bias_in[...]

    before = before_segment(pieces, count - 1 - step, ids, entering, seg_before)
    mask = pair_mask(seg_col[...], row)
    carried = (row == before).astype(f32)
    tail = (row == end).astype(f32)
    keep = (before == end).astype(f32)
    mapped = [dot_nn(maps[part], qkv[part * width : (part + 1) * width, :]) for part in range(2)]
    back = [[], []]
    grad_values = []
    for head in range(heads):
        query = feats[head * 2 * size : (head + 1) * 2 * size, :]
        key = feats[(heads + head) * 2 * size : (heads + head + 1) * 2 * size, :]
        at = 2 * width + head * size
        value = with_ones(qkv[at : at + size, :])
        value_two = jnp.concatenate([value, value], axis=0)
        own = grads[head * rows : (head + 1) * rows, :]
        high, low = split(own)
        grad_two = jnp.concatenate([high, low], axis=0)
        scores = (dot_tn(key, query) * mask).astype(bf16)
        grad_scores = (dot_tn(value_two, grad_two) * mask).astype(bf16)
        into = states[head * rows : (head + 1) * rows, :]
        into_high, into_low = split(into)
        inter = dot_tn(
            jnp.concatenate([into_high, into_low, into_high], axis=0),
            jnp.concatenate([high, high, low], axis=0),
        )
        grad_query = dot_nn(key, grad_scores) + carried * inter
        after = state[head * rows : (head + 1) * rows, :]
        after_two = jnp.concatenate(split(after), axis=0)
        grad_key = dot_nt(query, grad_scores) + tail * dot_tn(after_two, value_two)
        straight = dot_nt(grad_two, scores)
        through = dot_nn(after_two, key)
        grad_values.append(
            straight[:size] + straight[rows : rows + size] + tail * (through[:size] + through[rows : rows + size])
        )
        carried_two = jnp.concatenate(split(own * carried), axis=0)
        added = dot_nt(carried_two, query)
        state[head * rows : (head + 1) * rows, :] = keep * after + added[:rows] + added[rows:]
        for part, grad in ((0, grad_query), (1, grad_key)):
            plain = mapped[part][head * size : (head + 1) * size]
            back[part].append(softmax_back(grad, softmax_rows(plain), softmax_rows(-plain)))
    pieces_low = []
    for part in range(2):
        grad_mapped = jnp.concatenate(back[part], axis=0).astype(bf16)
        map_acc[part] += dot_nt(qkv[part * width : (part + 1) * width, :], grad_mapped)
        pieces_low.append(dot_nn(maps_back[part], grad_mapped))
    pieces_low.append(jnp.concatenate(grad_values, axis=0))
    grad_qkv = jnp.concatenate(pieces_low, axis=0).astype(bf16)
    part_low = dot_nt(grad_qkv.T, weight[:, : 3 * width]).astype(bf16)
    store_slots(count - 1 - step, ids, part_low, slots)
    weight_acc[...] += dot_nn(grad_qkv, attn_in[...])
    bias_acc[...] += jnp.sum(grad_qkv.astype(f32), axis=1, keepdims=True)
    if not first:

        @pl.when(step == count - 1)
        def _():
            wide = weight[:, : 3 * width].astype(f32)
            total = weight_acc[...].T
            bias_row = turn_columns(bias_acc[...])[0:1]
            sums = turn_columns(
                jnp.sum(wide * total, axis=1, keepdims=True), jnp.sum(wide * bias_row, axis=1, keepdims=True)
            )
            dim = wide.shape[0]
            blocks = []
            for part in range(2):
                lane = lax.broadcasted_iota(jnp.int32, (size, width), 1) // size
                own = jnp.zeros((size, width), f32)
                for head in range(heads):
                    own = jnp.where(lane == head, map_acc[part, head * size : (head + 1) * size, :], own)
                blocks.append(own)
            half = size // 2
            turned = jnp.concatenate(
                [blocks[0][:half], blocks[1][:half], blocks[0][half:], blocks[1][half:]], axis=1
            )
            lines = [
                (sums[0:1] - shift[...] * sums[1:2]) / gain[...],
                sums[1:2],
                sums_a[...] + sums_b[...],
                mlp_rows[...],
                jnp.concatenate([bias_row, jnp.zeros((1, dim - 3 * width), f32)], axis=1),
                turned,
            ]
            small = jnp.concatenate(lines, axis=0)
            small = jnp.concatenate([small, jnp.zeros((SMALL - small.shape[0], dim), f32)], axis=0).astype(bf16)
            proj_total = proj_in[...].T
            shard = packed.shape[1] - SMALL
            for copy in range(packed.shape[0]):
                packed[copy, :SMALL, :] = small
                at = copy * shard
                packed[copy, SMALL:, : 3 * width] = total[at : at + shard].astype(bf16)
                packed[copy, SMALL:, 3 * width :] = proj_total[at : at + shard].astype(bf16)


def exchange(array):
    return lax.all_to_all(array, "dp", 0, 0)


def gather_dp(array):
    return exchange(jnp.broadcast_to(array, (lax.axis_size("dp"),) + array.shape)).reshape(-1, array.shape[1])


def swap(array, bit):
    return lax.ppermute(array, "tensor", [(i, i ^ bit) for i in range(4)])


def gather_tensor(array, across=None):
    if across is None:
        return (array, swap(array, 2), swap(array, 1), swap(array, 3))
    return (array, across, swap(array, 1), swap(across, 1))


def scatter_tensor(slots):
    return (slots[0], swap(slots[1], 2), swap(slots[2], 1), swap(slots[3], 3))


def block_diagonal(blocks):
    count, size, _ = blocks.shape
    eye = jnp.eye(count, dtype=blocks.dtype)
    return (eye[:, None, :, None] * blocks[:, :, None, :]).reshape(count * size, count * size)


def on_device(
    inputs, cotangent, segment, attn_gain, attn_shift, qkv_weight, qkv_bias, query_map, key_map,
    proj_weight, proj_bias, mlp_gain, mlp_shift, fc_weight, fc_bias, out_weight, out_bias,
):
    micro, tokens, dim = inputs.shape
    heads, size, _ = query_map.shape
    width = heads * size
    units = fc_weight.shape[1]
    count = lax.axis_size("dp")
    tiles = lax.axis_size("tensor")
    tile = tokens // tiles
    pieces = SEQ_LEN // tokens
    hops = min(-(-MAX_SEGMENT // tokens), pieces - 1)
    rows = size + PAD
    used = heads * rows
    shard = dim // count
    ids = jnp.stack([lax.axis_index("tensor"), lax.axis_index("dp")]).astype(jnp.int32)

    weight = gather_dp(jnp.concatenate([qkv_weight.reshape(shard, 3 * width), proj_weight.T], axis=1))
    proj_t = weight[:, 3 * width :]

    row = lambda v: v.astype(f32).reshape(1, -1)
    gain_a, shift_a, gain_m, shift_m = row(attn_gain), row(attn_shift), row(mlp_gain), row(mlp_shift)
    bias_p, bias_f, bias_o = row(proj_bias), row(fc_bias), row(out_bias)
    bias_qkv = qkv_bias.astype(f32).reshape(3 * width, 1)
    maps_back = jnp.stack([block_diagonal(query_map), block_diagonal(key_map)])
    maps = jnp.swapaxes(maps_back, 1, 2)
    seg = segment.astype(f32).reshape(micro, tiles, 1, tile)
    seg_col = segment.astype(f32).reshape(micro, tiles, tile, 1)

    def rows_of(array, m, at=None):
        return (array, (None, tile, dim), lambda i, ids: (m, i if at is None else at(i, ids), 0))

    def own_rows(array, m):
        return (array, (None, tile, dim), lambda i, ids: (m, ids[0], 0))

    def columns(array, at=None, m=0):
        return (
            array, (array.shape[0], tile), lambda i, ids: (0, m * tiles + (i if at is None else at(i, ids)))
        )

    def columns_out(height, kind, at=None):
        return ((height, tokens), kind, (height, tile), lambda i, ids: (0, i if at is None else at(i, ids)))

    def seg_row(m, at=None):
        return (seg, (None, None, 1, tile), lambda i, ids: (m, i if at is None else at(i, ids), 0, 0))

    def seg_column(m, at=None):
        return (seg_col, (None, None, tile, 1), lambda i, ids: (m, i if at is None else at(i, ids), 0, 0))

    def states_of(m):
        return [(a, (used + PAD, 2 * size), lambda i, ids: (m, 0)) for a in incoming]

    def entering(m):
        return (incoming[0], (PAD, 2 * size), lambda i, ids: ((m * (used + PAD) + used) // PAD, 0))

    def half(array, at):
        return (array, (None, tile, dim), lambda i, ids: (at, 0, 0))

    near = lambda i, ids: ids[0] ^ relative(i)

    def pin(*arrays):
        nonlocal ids
        ids, arrays = lax.optimization_barrier((ids, arrays))
        return arrays

    def run(*arguments, **options):
        return pin(*call(arguments[0], arguments[1], ids, *arguments[2:], **options))

    def fold(*pairs):
        (result,) = run(
            functools.partial(fold_kernel, len(pairs)), (1,),
            [half(a, 1) for pair in pairs for a in pair],
            [whole_out((len(pairs), tile, dim), bf16)], [], 3,
        )
        return result

    rest_own = jnp.concatenate([fc_weight, out_weight.T], axis=1)
    rest = lax.all_gather(rest_own, "dp", axis=0, tiled=True)
    maps, maps_back, bias_qkv, seg, seg_col = pin(maps, maps_back, bias_qkv, seg, seg_col)
    row_tile = lambda array: (array, (None, tile, dim), lambda i, ids: (lax.div(i, tiles), lax.rem(i, tiles), 0))
    (attn_in,) = run(
        norm_kernel, (micro * tiles,), [row_tile(inputs), whole(gain_a), whole(shift_a)],
        [((micro, tokens, dim), bf16) + row_tile(inputs)[1:]], [], 8,
    )
    fc_block = (rest, (dim, units), lambda i, ids: (0, 0))
    out_block = (rest, (dim, units), lambda i, ids: (0, 1))
    state_out = ((count, used + PAD, 2 * size), bf16)
    proj_across = swap(proj_t, 2)
    every = micro * tiles
    qkv, feats, state = run(
        functools.partial(project_kernel, heads, tiles), (every,),
        [
            row_tile(attn_in), whole(weight), whole(bias_qkv), whole(maps),
            (seg, (None, None, 1, tile), lambda i, ids: (lax.div(i, tiles), lax.rem(i, tiles), 0, 0)),
            (seg, (None, None, 1, tile), lambda i, ids: (lax.div(i, tiles), tiles - 1, 0, 0)),
        ],
        [
            ((3 * width, micro * tokens), bf16, (3 * width, tile), lambda i, ids: (0, i)),
            ((4 * width, micro * tokens), bf16, (4 * width, tile), lambda i, ids: (0, i)),
            (
                (micro * (used + PAD), 2 * size), bf16, (used + PAD, 2 * size),
                lambda i, ids: (lax.div(i, tiles), 0),
            ),
        ],
        [pltpu.VMEM((used, 2 * size), f32), pltpu.VMEM((3 * width, dim), bf16)],
        13,
    )
    incoming = [
        lax.ppermute(state, "dp", [(i, i + k) for i in range(count) if i % pieces + k < pieces])
        for k in range(1, hops + 1)
    ]
    (proj_across,) = pin(proj_across)
    proj_slots = pin(*gather_tensor(proj_t, proj_across))
    attended, attended_low, denominators, states = [], [], [], []
    for m in range(micro):
        result = run(
            functools.partial(attend_kernel, heads, pieces, hops), (tiles,),
            [
                (qkv, (width, tile), lambda i, ids, m=m: (2, m * tiles + i)), columns(feats, None, m), seg_row(m), seg_column(m),
            ]
            + states_of(m),
            [
                columns_out(width, f32), columns_out(width, bf16), columns_out(8, f32),
                ((tiles, used, 2 * size), f32, (None, used, 2 * size), lambda i, ids: (i, 0, 0)),
            ],
            [pltpu.VMEM((used, 2 * size), f32), pltpu.VMEM((1, tile), f32)],
            6.5,
        )
        attended.append(result[0])
        attended_low.append(result[1])
        denominators.append(result[2])
        states.append(result[3])
        if m == 0:
            across = swap(result[1], 2)
        else:
            (across,) = pin(across)
            slots = [gather_tensor(attended_low[0], across), gather_tensor(result[1])]

    acc = ()
    residuals, mlp_terms, out_pairs = [], [], []
    for m in range(micro):
        final = m == micro - 1
        kept = [((dim, units), f32), ((dim, units), f32), ((1, units), f32)]
        pair = [whole_out((2, tile, dim), bf16)] * 2
        result = run(
            functools.partial(mlp_kernel, not final), (tiles,),
            [rows_of(inputs, m), rows_of(cotangent, m)]
            + [columns(a) for a in slots[m]]
            + [whole(a) for a in proj_slots]
            + [whole(bias_p), whole(gain_m), whole(shift_m), fc_block, out_block, whole(bias_f)]
            + [whole(a) for a in acc],
            [((tiles, tile, dim), f32, (None, tile, dim), lambda i, ids: (i, 0, 0))]
            + (pair if final else [whole_out((tile, dim), bf16)] * 4)
            + pair
            + ([whole_out((3, dim), f32), whole_out((dim, 2 * units), bf16)] if final else [whole_out(*k) for k in kept]),
            [pltpu.VMEM(*k) for k in kept] if final else [],
            21,
        )
        residuals.append(result[0])
        parts = result[1:3] if final else result[1:5]
        mlp_terms.append((parts[0], swap(parts[1], 1)) if final else scatter_tensor(parts))
        result = result[3:] if final else result[5:]
        out_pairs.append((result[0], swap(result[1], 1)))
        acc = result[2:]
    mlp_rows, rest_grads = acc

    own_tile = lambda array: (array, (None, tile, dim), lambda i, ids: (ids[0], 0, 0))
    grad_residuals, grad_slots, row_sums = [], [], []

    def middle(m, terms):
        grad_residual, grad_attn, sums = run(
            middle_kernel, (1,), [own_tile(residuals[m]), own_rows(cotangent, m), whole(gain_m)] + terms,
            [whole_out((tile, dim), f32), whole_out((tile, dim), bf16), whole_out((2, dim), f32)],
            [], 4,
        )
        grad_residuals.append(grad_residual)
        row_sums.append(sums)
        return grad_attn, swap(grad_attn, 2)

    proj_acc = ()
    grads, returned = [], []

    def grads_in(m, array, across):
        nonlocal proj_acc
        (across,) = pin(across)
        grad_slots.append(gather_tensor(array, across))
        result = run(
            functools.partial(grads_in_kernel, heads, pieces, m == 0), (tiles,),
            [whole(a) for a in grad_slots[m]]
            + [
                whole(proj_t), (feats, (2 * width, tile), lambda i, ids: (0, m * tiles + near(i, ids))),
                columns(attended[m], near), columns(attended_low[m], near), columns(denominators[m], near),
                seg_row(m, near), entering(m),
            ]
            + [whole(a) for a in proj_acc],
            [columns_out(used, f32, near), whole_out(*state_out), whole_out((width, dim), f32)],
            [pltpu.VMEM((used, 2 * size), f32), pltpu.VMEM((width, dim), bf16)],
            7,
        )
        grads.append(result[0])
        proj_acc = (result[2],)
        returned.append(exchange(result[1]))

    acc = ()
    turned = lambda i, ids: tiles - 1 - i

    def attention_back(m):
        nonlocal acc
        final = m == micro - 1
        kept = [((3 * width, dim), f32), ((2, width, width), f32), ((3 * width, 1), f32)]
        result = run(
            functools.partial(grads_kernel, heads, pieces, hops, not final), (tiles,),
            [
                columns(qkv, turned, m), columns(feats, turned, m), columns(grads[m], turned),
                (states[m], (None, used, 2 * size), lambda i, ids: (tiles - 1 - i, 0, 0)),
                seg_row(m, turned), seg_column(m, turned), seg_row(m, lambda i, ids: jnp.maximum(tiles - 2 - i, 0)),
                entering(m), rows_of(attn_in, m, turned),
                whole(weight), whole(maps), whole(maps_back), whole(returned[m]),
            ]
            + [whole(a) for a in acc]
            + ([whole(a) for a in (proj_acc[0], gain_a, shift_a, mlp_rows, *row_sums)] if final else []),
            ([whole_out((2, tile, dim), bf16)] * 2 if final else [whole_out((tile, dim), bf16)] * 4)
            + ([whole_out((count, SMALL + shard, 4 * width), bf16)] if final else [whole_out(*k) for k in kept]),
            ([pltpu.VMEM(*k) for k in kept] if final else []) + [pltpu.VMEM((used, 2 * size), f32)],
            16,
        )
        acc = result[2:] if final else result[4:]
        return result[:2] if final else result[:4]

    def last(m, terms):
        (finished,) = run(
            last_kernel, (1,), [own_rows(inputs, m), whole(grad_residuals[m]), whole(gain_a)] + terms,
            [whole_out((tile, dim), bf16)], [], 4,
        )
        return finished

    def ordered(parts, m, base=()):
        (result,) = run(
            functools.partial(order_kernel, tiles), (tiles,),
            [whole(a) for a in parts] + [(a, None, None) for a in base],
            [((micro, tokens, dim), bf16, (None, tile, dim), lambda i, ids: (m, ids[0] ^ relative(i), 0))],
            [], 4, aliases={tiles + 1: 0} if base else None,
        )
        return result

    def paired(pair, crossed):
        return [half(pair[0], 0), half(pair[1], 0), half(crossed, 0)]

    (rest_grads,) = pin(rest_grads)
    rest_sum = lax.psum_scatter(rest_grads, "dp", scatter_dimension=0, tiled=True)
    moved = middle(0, [whole(a) for a in mlp_terms[0]])
    crossed = swap(fold(mlp_terms[1]), 2)
    grads_in(0, *moved)
    moved = middle(1, paired(mlp_terms[1], crossed))
    out_crossed = swap(fold(*out_pairs), 2)
    returned = list(pin(*returned))
    grads_in(1, *moved)
    (finished,) = run(
        functools.partial(finish_kernel, micro), (1,),
        [whole(bias_o), whole(out_crossed)]
        + [spec for m in range(micro) for spec in (own_tile(residuals[m]), half(out_pairs[m][0], 0), half(out_pairs[m][1], 0))],
        [whole_out((micro, tile, dim), bf16)], [], 4,
    )
    across = swap(finished, 2)
    first_parts = attention_back(0)
    (across,) = pin(across)
    outputs = gather_tensor(finished, across)
    first_terms = scatter_tensor(first_parts)
    kept, away = attention_back(1)
    last_pair = (kept, swap(away, 1))
    total = exchange(acc[0])
    (rest_sum,) = pin(rest_sum)
    early = last(0, [whole(a) for a in first_terms])
    early, folded = pin(early, fold(last_pair))
    crossed = swap(folded, 2)
    early_across = swap(early, 2)
    (output,) = run(
        functools.partial(order_kernel, tiles), (every,),
        [(a, (None, tile, dim), lambda i, ids: (lax.div(i, tiles), 0, 0)) for a in outputs],
        [(
            (micro, tokens, dim), bf16, (None, tile, dim),
            lambda i, ids: (lax.div(i, tiles), ids[0] ^ relative(lax.rem(i, tiles)), 0),
        )],
        [], 6,
    )
    late = last(1, paired(last_pair, crossed))
    late_across = swap(late, 2)
    rest_sum = rest_sum.astype(f32)
    fc_grad, out_grad = pin(rest_sum[:, :units], rest_sum[:, units:].T)
    (early_across,) = pin(early_across)
    input_grad = ordered(gather_tensor(early, early_across), 0)
    total, late_across = pin(total, late_across)
    input_grad = ordered(gather_tensor(late, late_across), 1, (input_grad,))
    total = jnp.sum(total.astype(f32), axis=0)

    shared = total[:6]
    shared = (shared + swap(shared, 1)) + (swap(shared, 2) + swap(shared, 3))
    blocks = total[8 : 8 + size // 2].reshape(size // 2, 2, 2, heads, size)
    blocks = jnp.transpose(blocks, (2, 3, 1, 0, 4)).reshape(2, heads, size, size)
    qkv_sum = total[SMALL:]
    return (
        output,
        input_grad,
        shared[0],
        shared[1],
        qkv_sum[:, : 3 * width].reshape(shard, 3, width),
        total[7, : 3 * width].reshape(3, width),
        blocks[0],
        blocks[1],
        qkv_sum[:, 3 * width :].T,
        shared[2],
        shared[4],
        shared[5],
        fc_grad,
        total[6],
        out_grad,
        shared[3],
    )


def solution(mesh):
    in_specs = (
        P(None, "dp", None), P(None, "dp", None), P(None, "dp"), P(), P(), P("dp", None, "tensor"),
        P(None, "tensor"), P("tensor", None, None), P("tensor", None, None), P("tensor", "dp"), P(), P(), P(),
        P("dp", "tensor"), P("tensor"), P("tensor", "dp"), P(),
    )
    out_specs = (
        P(None, "dp", None), P(None, "dp", None), P(), P(), P("dp", None, "tensor"), P(None, "tensor"),
        P("tensor", None, None), P("tensor", None, None), P("tensor", "dp"), P(), P(), P(),
        P("dp", "tensor"), P("tensor"), P("tensor", "dp"), P(),
    )
    return jax.shard_map(
        on_device, mesh=mesh, in_specs=in_specs, out_specs=out_specs, check_vma=False
    )
```

```python
import functools

import jax
import jax.numpy as jnp
from jax import lax
from jax.experimental import pallas as pl
from jax.experimental.pallas import tpu as pltpu
from jax.sharding import PartitionSpec as P

SEQ_LEN = 8192
MAX_SEGMENT = 4096
EPSILON = 1e-05
GELU_SCALE = 0.7978845608028654
GELU_CUBIC = 0.044715
PAD = 16
SMALL = 48
RATE = 1.1e9

f32 = jnp.float32
bf16 = jnp.bfloat16


def dot_nn(a, b):
    return lax.dot_general(a, b, (((1,), (0,)), ((), ())), preferred_element_type=f32)


def dot_nt(a, b):
    return lax.dot_general(a, b, (((1,), (1,)), ((), ())), preferred_element_type=f32)


def dot_tn(a, b):
    return lax.dot_general(a, b, (((0,), (0,)), ((), ())), preferred_element_type=f32)


def split(value):
    high = value.astype(bf16)
    return high, (value - high.astype(f32)).astype(bf16)


def norm_parts(values):
    centred = values - jnp.mean(values, axis=-1, keepdims=True)
    inverse = lax.rsqrt(jnp.mean(centred * centred, axis=-1, keepdims=True) + EPSILON)
    return centred * inverse, inverse


def norm_back(grad, normed, inverse, gain):
    scaled = grad * gain
    return inverse * (
        scaled
        - jnp.mean(scaled, axis=-1, keepdims=True)
        - normed * jnp.mean(scaled * normed, axis=-1, keepdims=True)
    )


def softmax_rows(values):
    raised = jnp.exp(values - jnp.max(values, axis=0, keepdims=True))
    return raised * (1.0 / jnp.sum(raised, axis=0, keepdims=True))


def relative(value):
    return ((value & 1) << 1) | (value >> 1)


def with_ones(values):
    width = values.shape[1]
    rows = lax.broadcasted_iota(jnp.int32, (PAD, width), 0)
    return jnp.concatenate([values, (rows == 0).astype(f32).astype(bf16)], axis=0)


def call(kernel, grid, ids, inputs, outputs, scratch, micros, aliases=None):
    moved = sum(a.size * a.dtype.itemsize for a, _, _ in inputs) if micros else 0
    return pl.pallas_call(
        kernel,
        grid_spec=pltpu.PrefetchScalarGridSpec(
            num_scalar_prefetch=1,
            grid=grid,
            in_specs=[
                pl.BlockSpec(block, index) if block else pl.BlockSpec(memory_space=pl.ANY)
                for _, block, index in inputs
            ],
            out_specs=[pl.BlockSpec(block, index) for _, _, block, index in outputs],
            scratch_shapes=scratch,
        ),
        out_shape=[jax.ShapeDtypeStruct(shape, kind) for shape, kind, _, _ in outputs],
        cost_estimate=pl.CostEstimate(flops=int(micros * RATE), bytes_accessed=moved, transcendentals=0),
        input_output_aliases=aliases or {},
        compiler_params=pltpu.CompilerParams(dimension_semantics=("arbitrary",) * len(grid)),
    )(ids, *[a for a, _, _ in inputs])


def whole(array):
    return (array, array.shape, lambda i, ids: (0,) * array.ndim)


def whole_out(shape, kind):
    return (shape, kind, shape, lambda i, ids: (0,) * len(shape))


def norm_kernel(ids, x, gain, shift, attn_in):
    normed, _ = norm_parts(x[...].astype(f32))
    attn_in[...] = (normed * gain[...] + shift[...]).astype(bf16)


def project_kernel(heads, tiles, ids, attn_in, weight, bias, maps, seg, seg_last, qkv, feats, state, total, turned):
    step = pl.program_id(0)
    wide = bias.shape[0]

    @pl.when(step == 0)
    def _():
        turned[...] = weight[:, :wide].T

    low = (dot_nt(turned[...], attn_in[...]) + bias[...]).astype(bf16)
    qkv[...] = low
    width = wide // 3
    size = width // heads
    mapped = [dot_nn(maps[part], low[part * width : (part + 1) * width]) for part in range(2)]

    @pl.when(lax.rem(step, tiles) == 0)
    def _():
        total[...] = jnp.zeros_like(total)

    tail = (seg[...] == seg_last[:, -1:]).astype(f32).astype(bf16)
    for head in range(heads):
        for part in range(2):
            own = mapped[part][head * size : (head + 1) * size]
            both = jnp.concatenate([softmax_rows(own), softmax_rows(-own)], axis=0).astype(bf16)
            at = (part * heads + head) * 2 * size
            feats[at : at + 2 * size, :] = both
        value = with_ones(low[2 * width + head * size : 2 * width + (head + 1) * size])
        at = head * (size + PAD)
        total[at : at + size + PAD, :] += dot_nt(value * tail, both)

    @pl.when(lax.rem(step, tiles) == tiles - 1)
    def _():
        state[...] = jnp.concatenate(
            [total[...], jnp.broadcast_to(seg_last[:, -1:], (PAD, 2 * size))], axis=0
        ).astype(bf16)


def pair_mask(seg_col, seg_row):
    tile = seg_row.shape[1]
    early = lax.broadcasted_iota(jnp.int32, (tile, tile), 0)
    late = lax.broadcasted_iota(jnp.int32, (tile, tile), 1)
    return jnp.where(early <= late, (seg_col == seg_row).astype(f32), 0.0)


def attend_kernel(
    heads, pieces, hops, ids, qkv_v, feats, seg, seg_col, *refs
):
    received, (attended, attended_low, denominators, states, state, previous) = refs[:hops], refs[hops:]
    step = pl.program_id(0)
    size = qkv_v.shape[0] // heads
    rows = size + PAD
    used = heads * rows
    place = lax.rem(ids[1], pieces)

    @pl.when(step == 0)
    def _():
        start = jnp.zeros((used, 2 * size), f32)
        latest = received[0][used:, :].astype(f32)[:1]
        for hop in range(hops):
            linked = (received[hop][used:, :].astype(f32)[:1] == latest).astype(f32)
            linked = linked * (place > hop).astype(f32)
            start = start + linked * received[hop][:used, :].astype(f32)
        state[...] = start
        first = latest[:, :1]
        previous[...] = jnp.broadcast_to(jnp.where(place > 0, first, -2.0), previous.shape)

    row = seg[...]
    end = row[:, -1:]
    mask = pair_mask(seg_col[...], row)
    before = previous[...]
    carried = (row == before).astype(f32)
    tail = (row == end).astype(f32).astype(bf16)
    keep = (before[:, : 2 * size] == end).astype(f32)
    states[...] = state[...]
    for head in range(heads):
        query = feats[head * 2 * size : (head + 1) * 2 * size, :]
        key = feats[(heads + head) * 2 * size : (heads + head + 1) * 2 * size, :]
        value = with_ones(qkv_v[head * size : (head + 1) * size, :])
        scores = (dot_tn(key, query) * mask).astype(bf16)
        own = state[head * rows : (head + 1) * rows, :]
        inter = dot_nn(jnp.concatenate(split(own), axis=0), query)
        both = dot_nn(value, scores) + carried * (inter[:rows] + inter[rows:])
        lower = both[size : size + 1]
        result = both[:size] / lower
        attended[head * size : (head + 1) * size, :] = result
        attended_low[head * size : (head + 1) * size, :] = result.astype(bf16)
        denominators[head : head + 1, :] = lower
        state[head * rows : (head + 1) * rows, :] = keep * own + dot_nt(value * tail, key)
    previous[...] = jnp.broadcast_to(end, previous.shape)


def sum_of(*terms):
    total = terms[0][...].astype(f32)
    for term in terms[1:]:
        total = total + term[...].astype(f32)
    return total


def store_slots(step, ids, low, slots):
    apart = ids[0] ^ step
    if len(slots) == 4:
        slot = relative(apart)
        for at in range(4):

            @pl.when(slot == at)
            def _():
                slots[at][...] = low
    else:
        for at in range(2):

            @pl.when((apart & 1) == at)
            def _():
                slots[at][apart >> 1] = low


def turn_columns(*columns):
    lane = lax.broadcasted_iota(jnp.int32, (columns[0].shape[0], 128), 1)
    wide = jnp.zeros(lane.shape, f32)
    for at, column in enumerate(columns):
        wide = jnp.where(lane == at, column, wide)
    return wide.T[:8]


def mlp_kernel(first, ids, x, cot, a0, a1, a2, a3, p0, p1, p2, p3, proj_bias, gain, shift, fc, out_t, fc_bias, *refs):
    if not first:
        fc_in, out_in, bias_in = refs[:3]
        refs = refs[3:]
    slots = 4 if first else 2
    residual, grad_slots, out_slots, refs = refs[0], refs[1 : 1 + slots], refs[1 + slots : 3 + slots], refs[3 + slots :]
    if not first:
        vectors, products = refs[:2]
        refs = refs[2:]
    fc_acc, out_acc, bias_acc = refs
    step = pl.program_id(0)

    @pl.when(step == 0)
    def _():
        if first:
            fc_acc[...] = jnp.zeros_like(fc_acc)
            out_acc[...] = jnp.zeros_like(out_acc)
            bias_acc[...] = jnp.zeros_like(bias_acc)
        else:
            fc_acc[...] = fc_in[...]
            out_acc[...] = out_in[...]
            bias_acc[...] = bias_in[...]

    resid = x[...].astype(f32) + proj_bias[...]
    for part, proj in zip((a0, a1, a2, a3), (p0, p1, p2, p3)):
        resid = resid + dot_nt(part[...].T, proj[...])
    residual[...] = resid
    normed, _ = norm_parts(resid)
    mlp_in = (normed * gain[...] + shift[...]).astype(bf16)
    preact = dot_nn(mlp_in, fc[...]) + fc_bias[...]
    square = preact * preact
    tangent = jnp.tanh(GELU_SCALE * (preact + GELU_CUBIC * square * preact))
    half = 0.5 * (1.0 + tangent)
    activ = (preact * half).astype(bf16)
    slope = half + 0.5 * preact * (1.0 - tangent * tangent) * GELU_SCALE * (1.0 + 3.0 * GELU_CUBIC * square)
    top = cot[...]
    grad_pre = (dot_nn(top, out_t[...]) * slope).astype(bf16)
    grad_low = dot_nt(grad_pre, fc[...]).astype(bf16)
    out_low = dot_nt(activ, out_t[...]).astype(bf16)
    store_slots(step, ids, grad_low, grad_slots)
    store_slots(step, ids, out_low, out_slots)
    fc_acc[...] += dot_tn(mlp_in, grad_pre)
    out_acc[...] += dot_tn(top, activ)
    bias_acc[...] += jnp.sum(grad_pre.astype(f32), axis=0, keepdims=True)
    if not first:

        @pl.when(step == pl.num_programs(0) - 1)
        def _():
            width = fc_acc.shape[1]
            products[:, :width] = fc_acc[...].astype(bf16)
            products[:, width:] = out_acc[...].astype(bf16)
            wide = fc[...].astype(f32)
            sums = turn_columns(
                jnp.sum(wide * fc_acc[...], axis=1, keepdims=True),
                jnp.sum(wide * bias_acc[...], axis=1, keepdims=True),
            )
            vectors[0:1, :] = (sums[0:1] - shift[...] * sums[1:2]) / gain[...]
            vectors[1:2, :] = sums[1:2]
            vectors[2:3, :] = bias_acc[...]


def middle_kernel(ids, residual, cot, gain, *refs):
    grad_residual, grad_attn, sums = refs[-3:]
    normed, inverse = norm_parts(residual[...])
    grad = sum_of(*refs[:-3])
    top = cot[...].astype(f32)
    total = top + norm_back(grad, normed, inverse, gain[...])
    grad_residual[...] = total
    low = total.astype(bf16)
    grad_attn[...] = low
    sums[0:1, :] = jnp.sum(low.astype(f32), axis=0, keepdims=True)
    sums[1:2, :] = jnp.sum(top, axis=0, keepdims=True)


def last_kernel(ids, x, grad_residual, gain, *refs):
    normed, inverse = norm_parts(x[...].astype(f32))
    grad = sum_of(*refs[:-1])
    refs[-1][...] = (grad_residual[...] + norm_back(grad, normed, inverse, gain[...])).astype(bf16)


def finish_kernel(micro, ids, bias, crossed, *refs):
    out = refs[-1]
    for m in range(micro):
        out[m] = (sum_of(*refs[3 * m : 3 * m + 3]) + bias[...] + crossed[m].astype(f32)).astype(bf16)


def fold_kernel(count, ids, *refs):
    out = refs[-1]
    for at in range(count):
        out[at] = sum_of(*refs[2 * at : 2 * at + 2]).astype(bf16)


def order_kernel(tiles, ids, *refs):
    out = refs[-1]
    for at in range(tiles):

        @pl.when(lax.rem(pl.program_id(0), tiles) == at)
        def _():
            out[...] = refs[at][...]


def before_segment(pieces, tile_index, ids, received, seg_before):
    entering = jnp.where(lax.rem(ids[1], pieces) > 0, received[...].astype(f32)[:1, :1], -2.0)
    return jnp.where(tile_index == 0, entering, seg_before[:, -1:])


def grads_in_kernel(heads, pieces, first, ids, g0, g1, g2, g3, proj_t, feats_q, attended, attended_low, denominators, seg, received, *refs):
    if first:
        grads, state, proj_acc, total, proj = refs
    else:
        proj_in, grads, state, product, total, proj, proj_acc = refs
    step = pl.program_id(0)
    size = attended.shape[0] // heads
    rows = size + PAD
    used = heads * rows
    before = before_segment(pieces, 0, ids, received, seg)

    @pl.when(step == 0)
    def _():
        proj[...] = proj_t[...].T
        total[...] = jnp.zeros_like(total)
        proj_acc[...] = jnp.zeros_like(proj_acc) if first else proj_in[...]

    def work(source):
        grad = source[...]
        proj_acc[...] += dot_nn(attended_low[...], grad)
        grad_att = dot_nt(proj[...], grad)
        carried = (seg[...] == before).astype(f32)
        for head in range(heads):
            own = grad_att[head * size : (head + 1) * size]
            inverse = 1.0 / denominators[head : head + 1, :]
            lower = -inverse * jnp.sum(own * attended[head * size : (head + 1) * size, :], axis=0, keepdims=True)
            filler = lax.broadcasted_iota(jnp.int32, (PAD, own.shape[1]), 0)
            both = jnp.concatenate([own * inverse, jnp.where(filler == 0, lower, 0.0)], axis=0)
            grads[head * rows : (head + 1) * rows, :] = both
            query = feats_q[head * 2 * size : (head + 1) * 2 * size, :]
            sums = dot_nt(jnp.concatenate(split(both * carried), axis=0), query)
            total[head * rows : (head + 1) * rows, :] += sums[:rows] + sums[rows:]

    for at, source in enumerate((g0, g1, g2, g3)):

        @pl.when(step == at)
        def _():
            work(source)

    @pl.when(step == pl.num_programs(0) - 1)
    def _():
        whole_state = jnp.concatenate(
            [total[...], jnp.broadcast_to(before, (PAD, 2 * size))], axis=0
        ).astype(bf16)
        for copy in range(state.shape[0]):
            state[copy] = whole_state
        if not first:
            product[...] = proj_acc[...].T.astype(bf16)


def softmax_back(grad, positive, negative):
    size = positive.shape[0]
    upper, lower = grad[:size], grad[size:]
    return positive * (upper - jnp.sum(positive * upper, axis=0, keepdims=True)) - negative * (
        lower - jnp.sum(negative * lower, axis=0, keepdims=True)
    )


def grads_kernel(
    heads, pieces, hops, first, ids, qkv, feats, grads, states, seg, seg_col, seg_before, entering, attn_in, weight, maps, maps_back,
    received, *refs
):
    if not first:
        weight_in, map_in, bias_in, product, gain, shift, mlp_rows, sums_a, sums_b = refs[:9]
        refs = refs[9:]
    slots, refs = (refs[:4], refs[4:]) if first else (refs[:2], refs[2:])
    if not first:
        packed, refs = refs[0], refs[1:]
    weight_acc, map_acc, bias_acc, state = refs
    step = pl.program_id(0)
    count = pl.num_programs(0)
    width = qkv.shape[0] // 3
    size = width // heads
    rows = size + PAD
    used = heads * rows
    row = seg[...]
    end = row[:, -1:]

    @pl.when(step == 0)
    def _():
        start = jnp.zeros((used, 2 * size), f32)
        place = lax.rem(ids[1], pieces)
        for hop in range(hops):
            source = jnp.minimum(ids[1] + 1 + hop, received.shape[0] - 1)
            linked = (received[source, used:, :].astype(f32)[:1] == end).astype(f32)
            linked = linked * (place + hop + 1 < pieces).astype(f32)
            start = start + linked * received[source, :used, :].astype(f32)
        state[...] = start
        if first:
            weight_acc[...] = jnp.zeros_like(weight_acc)
            map_acc[...] = jnp.zeros_like(map_acc)
            bias_acc[...] = jnp.zeros_like(bias_acc)
        else:
            weight_acc[...] = weight_in[...]
            map_acc[...] = map_in[...]
            bias_acc[...] = bias_in[...]

    before = before_segment(pieces, count - 1 - step, ids, entering, seg_before)
    mask = pair_mask(seg_col[...], row)
    carried = (row == before).astype(f32)
    tail = (row == end).astype(f32)
    keep = (before == end).astype(f32)
    mapped = [dot_nn(maps[part], qkv[part * width : (part + 1) * width, :]) for part in range(2)]
    back = [[], []]
    grad_values = []
    for head in range(heads):
        query = feats[head * 2 * size : (head + 1) * 2 * size, :]
        key = feats[(heads + head) * 2 * size : (heads + head + 1) * 2 * size, :]
        at = 2 * width + head * size
        value = with_ones(qkv[at : at + size, :])
        value_two = jnp.concatenate([value, value], axis=0)
        own = grads[head * rows : (head + 1) * rows, :]
        high, low = split(own)
        grad_two = jnp.concatenate([high, low], axis=0)
        scores = (dot_tn(key, query) * mask).astype(bf16)
        grad_scores = (dot_tn(value_two, grad_two) * mask).astype(bf16)
        into = states[head * rows : (head + 1) * rows, :]
        into_high, into_low = split(into)
        inter = dot_tn(
            jnp.concatenate([into_high, into_low, into_high], axis=0),
            jnp.concatenate([high, high, low], axis=0),
        )
        grad_query = dot_nn(key, grad_scores) + carried * inter
        after = state[head * rows : (head + 1) * rows, :]
        after_two = jnp.concatenate(split(after), axis=0)
        grad_key = dot_nt(query, grad_scores) + tail * dot_tn(after_two, value_two)
        straight = dot_nt(grad_two, scores)
        through = dot_nn(after_two, key)
        grad_values.append(
            straight[:size] + straight[rows : rows + size] + tail * (through[:size] + through[rows : rows + size])
        )
        carried_two = jnp.concatenate(split(own * carried), axis=0)
        added = dot_nt(carried_two, query)
        state[head * rows : (head + 1) * rows, :] = keep * after + added[:rows] + added[rows:]
        for part, grad in ((0, grad_query), (1, grad_key)):
            plain = mapped[part][head * size : (head + 1) * size]
            back[part].append(softmax_back(grad, softmax_rows(plain), softmax_rows(-plain)))
    pieces_low = []
    for part in range(2):
        grad_mapped = jnp.concatenate(back[part], axis=0).astype(bf16)
        map_acc[part] += dot_nt(qkv[part * width : (part + 1) * width, :], grad_mapped)
        pieces_low.append(dot_nn(maps_back[part], grad_mapped))
    pieces_low.append(jnp.concatenate(grad_values, axis=0))
    grad_qkv = jnp.concatenate(pieces_low, axis=0).astype(bf16)
    part_low = dot_nt(grad_qkv.T, weight[:, : 3 * width]).astype(bf16)
    store_slots(count - 1 - step, ids, part_low, slots)
    weight_acc[...] += dot_nn(grad_qkv, attn_in[...])
    bias_acc[...] += jnp.sum(grad_qkv.astype(f32), axis=1, keepdims=True)
    if not first:

        @pl.when(step == count - 1)
        def _():
            wide = weight[:, : 3 * width].astype(f32)
            total = weight_acc[...].T
            bias_row = turn_columns(bias_acc[...])[0:1]
            sums = turn_columns(
                jnp.sum(wide * total, axis=1, keepdims=True), jnp.sum(wide * bias_row, axis=1, keepdims=True)
            )
            dim = wide.shape[0]
            blocks = []
            for part in range(2):
                lane = lax.broadcasted_iota(jnp.int32, (size, width), 1) // size
                own = jnp.zeros((size, width), f32)
                for head in range(heads):
                    own = jnp.where(lane == head, map_acc[part, head * size : (head + 1) * size, :], own)
                blocks.append(own)
            half = size // 2
            turned = jnp.concatenate(
                [blocks[0][:half], blocks[1][:half], blocks[0][half:], blocks[1][half:]], axis=1
            )
            lines = [
                (sums[0:1] - shift[...] * sums[1:2]) / gain[...],
                sums[1:2],
                sums_a[...] + sums_b[...],
                mlp_rows[...],
                jnp.concatenate([bias_row, jnp.zeros((1, dim - 3 * width), f32)], axis=1),
                turned,
            ]
            small = jnp.concatenate(lines, axis=0)
            small = jnp.concatenate([small, jnp.zeros((SMALL - small.shape[0], dim), f32)], axis=0).astype(bf16)
            shard = total.shape[0] // packed.shape[0]
            for copy in range(packed.shape[0]):
                packed[copy, :SMALL, :] = small
                at = copy * shard
                packed[copy, SMALL:, : 3 * width] = total[at : at + shard].astype(bf16)
                packed[copy, SMALL:, 3 * width :] = product[at : at + shard, :]


def exchange(array):
    return lax.all_to_all(array, "dp", 0, 0)


def gather_dp(array):
    return exchange(jnp.broadcast_to(array, (lax.axis_size("dp"),) + array.shape)).reshape(-1, array.shape[1])


def swap(array, bit):
    return lax.ppermute(array, "tensor", [(i, i ^ bit) for i in range(4)])


def gather_tensor(array, across=None):
    if across is None:
        return (array, swap(array, 2), swap(array, 1), swap(array, 3))
    return (array, across, swap(array, 1), swap(across, 1))


def scatter_tensor(slots):
    return (slots[0], swap(slots[1], 2), swap(slots[2], 1), swap(slots[3], 3))


def block_diagonal(blocks):
    count, size, _ = blocks.shape
    eye = jnp.eye(count, dtype=blocks.dtype)
    return (eye[:, None, :, None] * blocks[:, :, None, :]).reshape(count * size, count * size)


def on_device(
    inputs, cotangent, segment, attn_gain, attn_shift, qkv_weight, qkv_bias, query_map, key_map,
    proj_weight, proj_bias, mlp_gain, mlp_shift, fc_weight, fc_bias, out_weight, out_bias,
):
    micro, tokens, dim = inputs.shape
    heads, size, _ = query_map.shape
    width = heads * size
    units = fc_weight.shape[1]
    count = lax.axis_size("dp")
    tiles = lax.axis_size("tensor")
    tile = tokens // tiles
    pieces = SEQ_LEN // tokens
    hops = min(-(-MAX_SEGMENT // tokens), pieces - 1)
    rows = size + PAD
    used = heads * rows
    shard = dim // count
    ids = jnp.stack([lax.axis_index("tensor"), lax.axis_index("dp")]).astype(jnp.int32)

    weight = gather_dp(jnp.concatenate([qkv_weight.reshape(shard, 3 * width), proj_weight.T], axis=1))
    proj_t = weight[:, 3 * width :]

    row = lambda v: v.astype(f32).reshape(1, -1)
    gain_a, shift_a, gain_m, shift_m = row(attn_gain), row(attn_shift), row(mlp_gain), row(mlp_shift)
    bias_p, bias_f, bias_o = row(proj_bias), row(fc_bias), row(out_bias)
    bias_qkv = qkv_bias.astype(f32).reshape(3 * width, 1)
    maps_back = jnp.stack([block_diagonal(query_map), block_diagonal(key_map)])
    maps = jnp.swapaxes(maps_back, 1, 2)
    seg = segment.astype(f32).reshape(micro, tiles, 1, tile)
    seg_col = segment.astype(f32).reshape(micro, tiles, tile, 1)

    def rows_of(array, m, at=None):
        return (array, (None, tile, dim), lambda i, ids: (m, i if at is None else at(i, ids), 0))

    def own_rows(array, m):
        return (array, (None, tile, dim), lambda i, ids: (m, ids[0], 0))

    def columns(array, at=None, m=0):
        return (
            array, (array.shape[0], tile), lambda i, ids: (0, m * tiles + (i if at is None else at(i, ids)))
        )

    def columns_out(height, kind, at=None):
        return ((height, tokens), kind, (height, tile), lambda i, ids: (0, i if at is None else at(i, ids)))

    def seg_row(m, at=None):
        return (seg, (None, None, 1, tile), lambda i, ids: (m, i if at is None else at(i, ids), 0, 0))

    def seg_column(m, at=None):
        return (seg_col, (None, None, tile, 1), lambda i, ids: (m, i if at is None else at(i, ids), 0, 0))

    def states_of(m):
        return [(a, (used + PAD, 2 * size), lambda i, ids: (m, 0)) for a in incoming]

    def entering(m):
        return (incoming[0], (PAD, 2 * size), lambda i, ids: ((m * (used + PAD) + used) // PAD, 0))

    def half(array, at):
        return (array, (None, tile, dim), lambda i, ids: (at, 0, 0))

    near = lambda i, ids: ids[0] ^ relative(i)

    def pin(*arrays):
        nonlocal ids
        ids, arrays = lax.optimization_barrier((ids, arrays))
        return arrays

    def run(*arguments, **options):
        return pin(*call(arguments[0], arguments[1], ids, *arguments[2:], **options))

    def fold(*pairs):
        (result,) = run(
            functools.partial(fold_kernel, len(pairs)), (1,),
            [half(a, 1) for pair in pairs for a in pair],
            [whole_out((len(pairs), tile, dim), bf16)], [], 3,
        )
        return result

    rest_own = jnp.concatenate([fc_weight, out_weight.T], axis=1)
    rest = lax.all_gather(rest_own, "dp", axis=0, tiled=True)
    maps, maps_back, bias_qkv, seg, seg_col = pin(maps, maps_back, bias_qkv, seg, seg_col)
    gain_a, shift_a, gain_m, shift_m, bias_p, bias_f, bias_o = pin(gain_a, shift_a, gain_m, shift_m, bias_p, bias_f, bias_o)
    row_tile = lambda array: (array, (None, tile, dim), lambda i, ids: (lax.div(i, tiles), lax.rem(i, tiles), 0))
    (attn_in,) = run(
        norm_kernel, (micro * tiles,), [row_tile(inputs), whole(gain_a), whole(shift_a)],
        [((micro, tokens, dim), bf16) + row_tile(inputs)[1:]], [], 8,
    )
    fc_block = (rest, (dim, units), lambda i, ids: (0, 0))
    out_block = (rest, (dim, units), lambda i, ids: (0, 1))
    state_out = ((count, used + PAD, 2 * size), bf16)
    proj_across = swap(proj_t, 2)
    every = micro * tiles
    qkv, feats, state = run(
        functools.partial(project_kernel, heads, tiles), (every,),
        [
            row_tile(attn_in), whole(weight), whole(bias_qkv), whole(maps),
            (seg, (None, None, 1, tile), lambda i, ids: (lax.div(i, tiles), lax.rem(i, tiles), 0, 0)),
            (seg, (None, None, 1, tile), lambda i, ids: (lax.div(i, tiles), tiles - 1, 0, 0)),
        ],
        [
            ((3 * width, micro * tokens), bf16, (3 * width, tile), lambda i, ids: (0, i)),
            ((4 * width, micro * tokens), bf16, (4 * width, tile), lambda i, ids: (0, i)),
            (
                (micro * (used + PAD), 2 * size), bf16, (used + PAD, 2 * size),
                lambda i, ids: (lax.div(i, tiles), 0),
            ),
        ],
        [pltpu.VMEM((used, 2 * size), f32), pltpu.VMEM((3 * width, dim), bf16)],
        13,
    )
    incoming = [
        lax.ppermute(state, "dp", [(i, i + k) for i in range(count) if i % pieces + k < pieces])
        for k in range(1, hops + 1)
    ]
    (proj_across,) = pin(proj_across)
    proj_slots = pin(*gather_tensor(proj_t, proj_across))
    attended, attended_low, denominators, states = [], [], [], []
    for m in range(micro):
        result = run(
            functools.partial(attend_kernel, heads, pieces, hops), (tiles,),
            [
                (qkv, (width, tile), lambda i, ids, m=m: (2, m * tiles + i)), columns(feats, None, m), seg_row(m), seg_column(m),
            ]
            + states_of(m),
            [
                columns_out(width, f32), columns_out(width, bf16), columns_out(8, f32),
                ((tiles, used, 2 * size), f32, (None, used, 2 * size), lambda i, ids: (i, 0, 0)),
            ],
            [pltpu.VMEM((used, 2 * size), f32), pltpu.VMEM((1, tile), f32)],
            6.5,
        )
        attended.append(result[0])
        attended_low.append(result[1])
        denominators.append(result[2])
        states.append(result[3])
        if m == 0:
            across = swap(result[1], 2)
        else:
            (across,) = pin(across)
            slots = [gather_tensor(attended_low[0], across), gather_tensor(result[1])]

    acc = ()
    residuals, mlp_terms, out_pairs = [], [], []
    for m in range(micro):
        final = m == micro - 1
        kept = [((dim, units), f32), ((dim, units), f32), ((1, units), f32)]
        pair = [whole_out((2, tile, dim), bf16)] * 2
        result = run(
            functools.partial(mlp_kernel, not final), (tiles,),
            [rows_of(inputs, m), rows_of(cotangent, m)]
            + [columns(a) for a in slots[m]]
            + [whole(a) for a in proj_slots]
            + [whole(bias_p), whole(gain_m), whole(shift_m), fc_block, out_block, whole(bias_f)]
            + [whole(a) for a in acc],
            [((tiles, tile, dim), f32, (None, tile, dim), lambda i, ids: (i, 0, 0))]
            + (pair if final else [whole_out((tile, dim), bf16)] * 4)
            + pair
            + ([whole_out((3, dim), f32), whole_out((dim, 2 * units), bf16)] if final else [whole_out(*k) for k in kept]),
            [pltpu.VMEM(*k) for k in kept] if final else [],
            21,
        )
        residuals.append(result[0])
        parts = result[1:3] if final else result[1:5]
        mlp_terms.append((parts[0], swap(parts[1], 1)) if final else scatter_tensor(parts))
        result = result[3:] if final else result[5:]
        out_pairs.append((result[0], swap(result[1], 1)))
        acc = result[2:]
    mlp_rows, rest_grads = acc

    own_tile = lambda array: (array, (None, tile, dim), lambda i, ids: (ids[0], 0, 0))
    grad_residuals, grad_slots, row_sums = [], [], []

    def middle(m, terms):
        grad_residual, grad_attn, sums = run(
            middle_kernel, (1,), [own_tile(residuals[m]), own_rows(cotangent, m), whole(gain_m)] + terms,
            [whole_out((tile, dim), f32), whole_out((tile, dim), bf16), whole_out((2, dim), f32)],
            [], 4,
        )
        grad_residuals.append(grad_residual)
        row_sums.append(sums)
        return grad_attn, swap(grad_attn, 2)

    proj_acc = ()
    grads, returned = [], []

    def grads_in(m, *gathered):
        nonlocal proj_acc
        grad_slots.append(gathered)
        result = run(
            functools.partial(grads_in_kernel, heads, pieces, m == 0), (tiles,),
            [whole(a) for a in grad_slots[m]]
            + [
                whole(proj_t), (feats, (2 * width, tile), lambda i, ids: (0, m * tiles + near(i, ids))),
                columns(attended[m], near), columns(attended_low[m], near), columns(denominators[m], near),
                seg_row(m, near), entering(m),
            ]
            + [whole(a) for a in proj_acc],
            [
                columns_out(used, f32, near), whole_out(*state_out),
                whole_out((width, dim), f32) if m == 0 else whole_out((dim, width), bf16),
            ],
            [pltpu.VMEM((used, 2 * size), f32), pltpu.VMEM((width, dim), bf16)]
            + ([] if m == 0 else [pltpu.VMEM((width, dim), f32)]),
            7,
        )
        grads.append(result[0])
        proj_acc = (result[2],)
        returned.append(exchange(result[1]))

    acc = ()
    turned = lambda i, ids: tiles - 1 - i

    def attention_back(m):
        nonlocal acc
        final = m == micro - 1
        kept = [((3 * width, dim), f32), ((2, width, width), f32), ((3 * width, 1), f32)]
        result = run(
            functools.partial(grads_kernel, heads, pieces, hops, not final), (tiles,),
            [
                columns(qkv, turned, m), columns(feats, turned, m), columns(grads[m], turned),
                (states[m], (None, used, 2 * size), lambda i, ids: (tiles - 1 - i, 0, 0)),
                seg_row(m, turned), seg_column(m, turned), seg_row(m, lambda i, ids: jnp.maximum(tiles - 2 - i, 0)),
                entering(m), rows_of(attn_in, m, turned),
                whole(weight), whole(maps), whole(maps_back), whole(returned[m]),
            ]
            + [whole(a) for a in acc]
            + ([whole(a) for a in (proj_acc[0], gain_a, shift_a, mlp_rows, *row_sums)] if final else []),
            ([whole_out((2, tile, dim), bf16)] * 2 if final else [whole_out((tile, dim), bf16)] * 4)
            + ([whole_out((count, SMALL + shard, 4 * width), bf16)] if final else [whole_out(*k) for k in kept]),
            ([pltpu.VMEM(*k) for k in kept] if final else []) + [pltpu.VMEM((used, 2 * size), f32)],
            0 if final else 16,
        )
        acc = result[2:] if final else result[4:]
        return result[:2] if final else result[:4]

    def last(m, terms):
        (finished,) = run(
            last_kernel, (1,), [own_rows(inputs, m), whole(grad_residuals[m]), whole(gain_a)] + terms,
            [whole_out((tile, dim), bf16)], [], 4,
        )
        return finished

    def ordered(parts, m, base=()):
        (result,) = run(
            functools.partial(order_kernel, tiles), (tiles,),
            [whole(a) for a in parts] + [(a, None, None) for a in base],
            [((micro, tokens, dim), bf16, (None, tile, dim), lambda i, ids: (m, ids[0] ^ relative(i), 0))],
            [], 4, aliases={tiles + 1: 0} if base else None,
        )
        return result

    def paired(pair, crossed):
        return [half(pair[0], 0), half(pair[1], 0), half(crossed, 0)]

    (rest_grads,) = pin(rest_grads)
    rest_sum = lax.psum_scatter(rest_grads, "dp", scatter_dimension=0, tiled=True)
    moved = middle(0, [whole(a) for a in mlp_terms[0]])
    crossed = swap(fold(mlp_terms[1]), 2)
    array, across = moved
    (across,) = pin(across)
    grads_in(0, *gather_tensor(array, across))
    moved = middle(1, paired(mlp_terms[1], crossed))
    out_crossed = swap(fold(*out_pairs), 2)
    array, across = moved
    returned[0], across = pin(returned[0], across)
    moved = gather_tensor(array, across)
    first_terms = scatter_tensor(attention_back(0))
    grads_in(1, *moved)
    (rest_sum,) = pin(rest_sum)
    (finished,) = run(
        functools.partial(finish_kernel, micro), (1,),
        [whole(bias_o), whole(out_crossed)]
        + [spec for m in range(micro) for spec in (own_tile(residuals[m]), half(out_pairs[m][0], 0), half(out_pairs[m][1], 0))],
        [whole_out((micro, tile, dim), bf16)], [], 4,
    )
    out_across = swap(finished, 2)
    early = last(0, [whole(a) for a in first_terms])
    early_across = swap(early, 2)
    kept, away = attention_back(1)
    kept, away, packed, out_across, early_across = pin(kept, away, acc[0], out_across, early_across)
    last_pair = (kept, swap(away, 1))
    total = exchange(packed)
    crossed = swap(fold(last_pair), 2)
    outputs = gather_tensor(finished, out_across)
    (output,) = run(
        functools.partial(order_kernel, tiles), (every,),
        [(a, (None, tile, dim), lambda i, ids: (lax.div(i, tiles), 0, 0)) for a in outputs],
        [(
            (micro, tokens, dim), bf16, (None, tile, dim),
            lambda i, ids: (lax.div(i, tiles), ids[0] ^ relative(lax.rem(i, tiles)), 0),
        )],
        [], 6,
    )
    rest_sum = rest_sum.astype(f32)
    fc_grad, out_grad = pin(rest_sum[:, :units], rest_sum[:, units:].T)
    late = last(1, paired(last_pair, crossed))
    late_across = swap(late, 2)
    input_grad = ordered(gather_tensor(early, early_across), 0)
    (late_across,) = pin(late_across)
    input_grad = ordered(gather_tensor(late, late_across), 1, (input_grad,))
    (total,) = pin(total)
    total = jnp.sum(total.astype(f32), axis=0)
    shared = total[:6]
    shared = (shared + swap(shared, 1)) + (swap(shared, 2) + swap(shared, 3))
    blocks = total[8 : 8 + size // 2].reshape(size // 2, 2, 2, heads, size)
    blocks = jnp.transpose(blocks, (2, 3, 1, 0, 4)).reshape(2, heads, size, size)
    qkv_sum, proj_sum = total[SMALL:, : 3 * width], total[SMALL:, 3 * width :].T
    return (
        output,
        input_grad,
        shared[0],
        shared[1],
        qkv_sum.reshape(shard, 3, width),
        total[7, : 3 * width].reshape(3, width),
        blocks[0],
        blocks[1],
        proj_sum,
        shared[2],
        shared[4],
        shared[5],
        fc_grad,
        total[6],
        out_grad,
        shared[3],
    )


def solution(mesh):
    in_specs = (
        P(None, "dp", None), P(None, "dp", None), P(None, "dp"), P(), P(), P("dp", None, "tensor"),
        P(None, "tensor"), P("tensor", None, None), P("tensor", None, None), P("tensor", "dp"), P(), P(), P(),
        P("dp", "tensor"), P("tensor"), P("tensor", "dp"), P(),
    )
    out_specs = (
        P(None, "dp", None), P(None, "dp", None), P(), P(), P("dp", None, "tensor"), P(None, "tensor"),
        P("tensor", None, None), P("tensor", None, None), P("tensor", "dp"), P(), P(), P(),
        P("dp", "tensor"), P("tensor"), P("tensor", "dp"), P(),
    )
    return jax.shard_map(
        on_device, mesh=mesh, in_specs=in_specs, out_specs=out_specs, check_vma=False
    )
```

```python
import functools

import jax
import jax.numpy as jnp
from jax import lax
from jax.experimental import pallas as pl
from jax.experimental.pallas import tpu as pltpu
from jax.sharding import PartitionSpec as P

SEQ_LEN = 8192
MAX_SEGMENT = 4096
EPSILON = 1e-05
GELU_SCALE = 0.7978845608028654
GELU_CUBIC = 0.044715
PAD = 16
SMALL = 40
RATE = 1.1e9

f32 = jnp.float32
bf16 = jnp.bfloat16


def dot_nn(a, b):
    return lax.dot_general(a, b, (((1,), (0,)), ((), ())), preferred_element_type=f32)


def dot_nt(a, b):
    return lax.dot_general(a, b, (((1,), (1,)), ((), ())), preferred_element_type=f32)


def dot_tn(a, b):
    return lax.dot_general(a, b, (((0,), (0,)), ((), ())), preferred_element_type=f32)


def split(value):
    high = value.astype(bf16)
    return high, (value - high.astype(f32)).astype(bf16)


def norm_parts(values):
    centred = values - jnp.mean(values, axis=-1, keepdims=True)
    inverse = lax.rsqrt(jnp.mean(centred * centred, axis=-1, keepdims=True) + EPSILON)
    return centred * inverse, inverse


def norm_back(grad, normed, inverse, gain):
    scaled = grad * gain
    return inverse * (
        scaled
        - jnp.mean(scaled, axis=-1, keepdims=True)
        - normed * jnp.mean(scaled * normed, axis=-1, keepdims=True)
    )


def softmax_rows(values):
    raised = jnp.exp(values - jnp.max(values, axis=0, keepdims=True))
    return raised * (1.0 / jnp.sum(raised, axis=0, keepdims=True))


def relative(value):
    return ((value & 1) << 1) | (value >> 1)


def with_ones(values):
    width = values.shape[1]
    rows = lax.broadcasted_iota(jnp.int32, (PAD, width), 0)
    return jnp.concatenate([values, (rows == 0).astype(f32).astype(bf16)], axis=0)


def call(kernel, grid, ids, inputs, outputs, scratch, micros, aliases=None):
    moved = sum(a.size * a.dtype.itemsize for a, _, _ in inputs) if micros else 0
    return pl.pallas_call(
        kernel,
        grid_spec=pltpu.PrefetchScalarGridSpec(
            num_scalar_prefetch=1,
            grid=grid,
            in_specs=[
                pl.BlockSpec(memory_space=pl.ANY) if not block
                else pl.BlockSpec(memory_space=pltpu.VMEM) if block == array.shape
                else pl.BlockSpec(block, index)
                for array, block, index in inputs
            ],
            out_specs=[pl.BlockSpec(block, index) for _, _, block, index in outputs],
            scratch_shapes=scratch,
        ),
        out_shape=[jax.ShapeDtypeStruct(shape, kind) for shape, kind, _, _ in outputs],
        cost_estimate=pl.CostEstimate(flops=int(micros * RATE), bytes_accessed=moved, transcendentals=0),
        input_output_aliases=aliases or {},
        compiler_params=pltpu.CompilerParams(dimension_semantics=("arbitrary",) * len(grid)),
    )(ids, *[a for a, _, _ in inputs])


def whole(array):
    return (array, array.shape, lambda i, ids: (0,) * array.ndim)


def whole_out(shape, kind):
    return (shape, kind, shape, lambda i, ids: (0,) * len(shape))


def norm_kernel(ids, x, gain, shift, attn_in):
    normed, _ = norm_parts(x[...].astype(f32))
    attn_in[...] = (normed * gain[...] + shift[...]).astype(bf16)


def project_kernel(heads, tiles, ids, attn_in, weight, bias, maps, seg, seg_last, qkv, feats, state, total, turned):
    step = pl.program_id(0)
    wide = bias.shape[0]

    @pl.when(step == 0)
    def _():
        turned[...] = weight[:, :wide].T

    low = (dot_nt(turned[...], attn_in[...]) + bias[...]).astype(bf16)
    qkv[...] = low
    width = wide // 3
    size = width // heads
    mapped = [dot_nn(maps[part], low[part * width : (part + 1) * width]) for part in range(2)]

    @pl.when(lax.rem(step, tiles) == 0)
    def _():
        total[...] = jnp.zeros_like(total)

    tail = (seg[...] == seg_last[:, -1:]).astype(f32).astype(bf16)
    for head in range(heads):
        for part in range(2):
            own = mapped[part][head * size : (head + 1) * size]
            both = jnp.concatenate([softmax_rows(own), softmax_rows(-own)], axis=0).astype(bf16)
            at = (part * heads + head) * 2 * size
            feats[at : at + 2 * size, :] = both
        value = with_ones(low[2 * width + head * size : 2 * width + (head + 1) * size])
        at = head * (size + PAD)
        total[at : at + size + PAD, :] += dot_nt(value * tail, both)

    @pl.when(lax.rem(step, tiles) == tiles - 1)
    def _():
        state[...] = jnp.concatenate(
            [total[...], jnp.broadcast_to(seg_last[:, -1:], (PAD, 2 * size))], axis=0
        ).astype(bf16)


def pair_mask(seg_col, seg_row):
    tile = seg_row.shape[1]
    early = lax.broadcasted_iota(jnp.int32, (tile, tile), 0)
    late = lax.broadcasted_iota(jnp.int32, (tile, tile), 1)
    return jnp.where(early <= late, (seg_col == seg_row).astype(f32), 0.0)


def attend_kernel(
    heads, pieces, hops, ids, qkv_v, feats, seg, seg_col, *refs
):
    received, (attended, attended_low, denominators, states, state, previous) = refs[:hops], refs[hops:]
    step = pl.program_id(0)
    size = qkv_v.shape[0] // heads
    rows = size + PAD
    used = heads * rows
    place = lax.rem(ids[1], pieces)

    @pl.when(step == 0)
    def _():
        start = jnp.zeros((used, 2 * size), f32)
        latest = received[0][used:, :].astype(f32)[:1]
        for hop in range(hops):
            linked = (received[hop][used:, :].astype(f32)[:1] == latest).astype(f32)
            linked = linked * (place > hop).astype(f32)
            start = start + linked * received[hop][:used, :].astype(f32)
        state[...] = start
        first = latest[:, :1]
        previous[...] = jnp.broadcast_to(jnp.where(place > 0, first, -2.0), previous.shape)

    row = seg[...]
    end = row[:, -1:]
    mask = pair_mask(seg_col[...], row)
    before = previous[...]
    carried = (row == before).astype(f32)
    tail = (row == end).astype(f32).astype(bf16)
    keep = (before[:, : 2 * size] == end).astype(f32)
    states[...] = state[...]
    for head in range(heads):
        query = feats[head * 2 * size : (head + 1) * 2 * size, :]
        key = feats[(heads + head) * 2 * size : (heads + head + 1) * 2 * size, :]
        value = with_ones(qkv_v[head * size : (head + 1) * size, :])
        scores = (dot_tn(key, query) * mask).astype(bf16)
        own = state[head * rows : (head + 1) * rows, :]
        inter = dot_nn(jnp.concatenate(split(own), axis=0), query)
        both = dot_nn(value, scores) + carried * (inter[:rows] + inter[rows:])
        lower = both[size : size + 1]
        result = both[:size] / lower
        attended[head * size : (head + 1) * size, :] = result
        attended_low[head * size : (head + 1) * size, :] = result.astype(bf16)
        denominators[head : head + 1, :] = lower
        state[head * rows : (head + 1) * rows, :] = keep * own + dot_nt(value * tail, key)
    previous[...] = jnp.broadcast_to(end, previous.shape)


def sum_of(*terms):
    total = terms[0][...].astype(f32)
    for term in terms[1:]:
        total = total + term[...].astype(f32)
    return total


def store_slots(step, ids, low, slots):
    apart = ids[0] ^ step
    if len(slots) == 4:
        slot = relative(apart)
        for at in range(4):

            @pl.when(slot == at)
            def _():
                slots[at][...] = low
    else:
        for at in range(2):

            @pl.when((apart & 1) == at)
            def _():
                slots[at][apart >> 1] = low


def turn_columns(*columns):
    lane = lax.broadcasted_iota(jnp.int32, (columns[0].shape[0], 128), 1)
    wide = jnp.zeros(lane.shape, f32)
    for at, column in enumerate(columns):
        wide = jnp.where(lane == at, column, wide)
    return wide.T[:8]


def mlp_kernel(first, ids, x, cot, a0, a1, a2, a3, p0, p1, p2, p3, proj_bias, gain, shift, fc, out_t, fc_bias, *refs):
    if not first:
        fc_in, out_in, bias_in = refs[:3]
        refs = refs[3:]
    slots = 4 if first else 2
    residual, grad_slots, out_slots, refs = refs[0], refs[1 : 1 + slots], refs[1 + slots : 3 + slots], refs[3 + slots :]
    if not first:
        vectors, products = refs[:2]
        refs = refs[2:]
    fc_acc, out_acc, bias_acc = refs
    step = pl.program_id(0)

    @pl.when(step == 0)
    def _():
        if first:
            fc_acc[...] = jnp.zeros_like(fc_acc)
            out_acc[...] = jnp.zeros_like(out_acc)
            bias_acc[...] = jnp.zeros_like(bias_acc)
        else:
            fc_acc[...] = fc_in[...]
            out_acc[...] = out_in[...]
            bias_acc[...] = bias_in[...]

    resid = x[...].astype(f32) + proj_bias[...]
    for part, proj in zip((a0, a1, a2, a3), (p0, p1, p2, p3)):
        resid = resid + dot_nt(part[...].T, proj[...])
    residual[...] = resid
    normed, _ = norm_parts(resid)
    mlp_in = (normed * gain[...] + shift[...]).astype(bf16)
    preact = dot_nn(mlp_in, fc[...]) + fc_bias[...]
    square = preact * preact
    tangent = jnp.tanh(GELU_SCALE * (preact + GELU_CUBIC * square * preact))
    half = 0.5 * (1.0 + tangent)
    activ = (preact * half).astype(bf16)
    slope = half + 0.5 * preact * (1.0 - tangent * tangent) * GELU_SCALE * (1.0 + 3.0 * GELU_CUBIC * square)
    top = cot[...]
    grad_pre = (dot_nn(top, out_t[...]) * slope).astype(bf16)
    grad_low = dot_nt(grad_pre, fc[...]).astype(bf16)
    out_low = dot_nt(activ, out_t[...]).astype(bf16)
    store_slots(step, ids, grad_low, grad_slots)
    store_slots(step, ids, out_low, out_slots)
    fc_acc[...] += dot_tn(mlp_in, grad_pre)
    out_acc[...] += dot_tn(top, activ)
    bias_acc[...] += jnp.sum(grad_pre.astype(f32), axis=0, keepdims=True)
    if not first:

        @pl.when(step == pl.num_programs(0) - 1)
        def _():
            width = fc_acc.shape[1]
            products[:, :width] = fc_acc[...].astype(bf16)
            products[:, width:] = out_acc[...].astype(bf16)
            wide = fc[...].astype(f32)
            sums = turn_columns(
                jnp.sum(wide * fc_acc[...], axis=1, keepdims=True),
                jnp.sum(wide * bias_acc[...], axis=1, keepdims=True),
            )
            vectors[0:1, :] = (sums[0:1] - shift[...] * sums[1:2]) / gain[...]
            vectors[1:2, :] = sums[1:2]
            vectors[2:3, :] = bias_acc[...]


def middle_kernel(ids, residual, cot, gain, *refs):
    grad_residual, grad_attn, sums = refs[-3:]
    normed, inverse = norm_parts(residual[...])
    grad = sum_of(*refs[:-3])
    top = cot[...].astype(f32)
    total = top + norm_back(grad, normed, inverse, gain[...])
    grad_residual[...] = total
    low = total.astype(bf16)
    grad_attn[...] = low
    sums[0:1, :] = jnp.sum(low.astype(f32), axis=0, keepdims=True)
    sums[1:2, :] = jnp.sum(top, axis=0, keepdims=True)


def last_kernel(ids, x, grad_residual, gain, *refs):
    normed, inverse = norm_parts(x[...].astype(f32))
    grad = sum_of(*refs[:-1])
    refs[-1][...] = (grad_residual[...] + norm_back(grad, normed, inverse, gain[...])).astype(bf16)


def finish_kernel(micro, ids, bias, crossed, *refs):
    out = refs[-1]
    for m in range(micro):
        out[m] = (sum_of(*refs[3 * m : 3 * m + 3]) + bias[...] + crossed[m].astype(f32)).astype(bf16)


def fold_kernel(count, ids, *refs):
    out = refs[-1]
    for at in range(count):
        out[at] = sum_of(*refs[2 * at : 2 * at + 2]).astype(bf16)


def order_kernel(tiles, ids, *refs):
    out = refs[-1]
    for at in range(tiles):

        @pl.when(lax.rem(pl.program_id(0), tiles) == at)
        def _():
            out[...] = refs[at][...]


def before_segment(pieces, tile_index, ids, received, seg_before):
    entering = jnp.where(lax.rem(ids[1], pieces) > 0, received[...].astype(f32)[:1, :1], -2.0)
    return jnp.where(tile_index == 0, entering, seg_before[:, -1:])


def grads_in_kernel(heads, pieces, first, ids, g0, g1, g2, g3, proj_t, feats_q, attended, attended_low, denominators, seg, received, *refs):
    if first:
        grads, state, proj_acc, total, proj = refs
    else:
        proj_in, grads, state, product, total, proj, proj_acc = refs
    step = pl.program_id(0)
    size = attended.shape[0] // heads
    rows = size + PAD
    used = heads * rows
    before = before_segment(pieces, 0, ids, received, seg)

    @pl.when(step == 0)
    def _():
        proj[...] = proj_t[...].T
        total[...] = jnp.zeros_like(total)
        proj_acc[...] = jnp.zeros_like(proj_acc) if first else proj_in[...]

    def work(source):
        grad = source[...]
        proj_acc[...] += dot_nn(attended_low[...], grad)
        grad_att = dot_nt(proj[...], grad)
        carried = (seg[...] == before).astype(f32)
        for head in range(heads):
            own = grad_att[head * size : (head + 1) * size]
            inverse = 1.0 / denominators[head : head + 1, :]
            lower = -inverse * jnp.sum(own * attended[head * size : (head + 1) * size, :], axis=0, keepdims=True)
            filler = lax.broadcasted_iota(jnp.int32, (PAD, own.shape[1]), 0)
            both = jnp.concatenate([own * inverse, jnp.where(filler == 0, lower, 0.0)], axis=0)
            grads[head * rows : (head + 1) * rows, :] = both
            query = feats_q[head * 2 * size : (head + 1) * 2 * size, :]
            sums = dot_nt(jnp.concatenate(split(both * carried), axis=0), query)
            total[head * rows : (head + 1) * rows, :] += sums[:rows] + sums[rows:]

    for at, source in enumerate((g0, g1, g2, g3)):

        @pl.when(step == at)
        def _():
            work(source)

    @pl.when(step == pl.num_programs(0) - 1)
    def _():
        whole_state = jnp.concatenate(
            [total[...], jnp.broadcast_to(before, (PAD, 2 * size))], axis=0
        ).astype(bf16)
        for copy in range(state.shape[0]):
            state[copy] = whole_state
        if not first:
            product[...] = proj_acc[...].T.astype(bf16)


def softmax_back(grad, positive, negative):
    size = positive.shape[0]
    upper, lower = grad[:size], grad[size:]
    return positive * (upper - jnp.sum(positive * upper, axis=0, keepdims=True)) - negative * (
        lower - jnp.sum(negative * lower, axis=0, keepdims=True)
    )


def grads_kernel(
    heads, pieces, hops, first, ids, qkv, feats, grads, states, seg, seg_col, seg_before, entering, attn_in, weight, maps, maps_back,
    received, *refs
):
    if not first:
        weight_in, map_in, bias_in, product, gain, shift, mlp_rows, sums_a, sums_b = refs[:9]
        refs = refs[9:]
    slots, refs = (refs[:4], refs[4:]) if first else (refs[:2], refs[2:])
    if not first:
        packed, refs = refs[0], refs[1:]
    weight_acc, map_acc, bias_acc, state = refs
    step = pl.program_id(0)
    count = pl.num_programs(0)
    width = qkv.shape[0] // 3
    size = width // heads
    rows = size + PAD
    used = heads * rows
    row = seg[...]
    end = row[:, -1:]

    @pl.when(step == 0)
    def _():
        start = jnp.zeros((used, 2 * size), f32)
        place = lax.rem(ids[1], pieces)
        for hop in range(hops):
            source = jnp.minimum(ids[1] + 1 + hop, received.shape[0] - 1)
            linked = (received[source, used:, :].astype(f32)[:1] == end).astype(f32)
            linked = linked * (place + hop + 1 < pieces).astype(f32)
            start = start + linked * received[source, :used, :].astype(f32)
        state[...] = start
        if first:
            weight_acc[...] = jnp.zeros_like(weight_acc)
            map_acc[...] = jnp.zeros_like(map_acc)
            bias_acc[...] = jnp.zeros_like(bias_acc)
        else:
            weight_acc[...] = weight_in[...]
            map_acc[...] = map_in[...]
            bias_acc[...] = bias_in[...]

    before = before_segment(pieces, count - 1 - step, ids, entering, seg_before)
    mask = pair_mask(seg_col[...], row)
    carried = (row == before).astype(f32)
    tail = (row == end).astype(f32)
    keep = (before == end).astype(f32)
    mapped = [dot_nn(maps[part], qkv[part * width : (part + 1) * width, :]) for part in range(2)]
    back = [[], []]
    grad_values = []
    for head in range(heads):
        query = feats[head * 2 * size : (head + 1) * 2 * size, :]
        key = feats[(heads + head) * 2 * size : (heads + head + 1) * 2 * size, :]
        at = 2 * width + head * size
        value = with_ones(qkv[at : at + size, :])
        value_two = jnp.concatenate([value, value], axis=0)
        own = grads[head * rows : (head + 1) * rows, :]
        high, low = split(own)
        grad_two = jnp.concatenate([high, low], axis=0)
        scores = (dot_tn(key, query) * mask).astype(bf16)
        grad_scores = (dot_tn(value_two, grad_two) * mask).astype(bf16)
        into = states[head * rows : (head + 1) * rows, :]
        into_high, into_low = split(into)
        inter = dot_tn(
            jnp.concatenate([into_high, into_low, into_high], axis=0),
            jnp.concatenate([high, high, low], axis=0),
        )
        grad_query = dot_nn(key, grad_scores) + carried * inter
        after = state[head * rows : (head + 1) * rows, :]
        after_two = jnp.concatenate(split(after), axis=0)
        grad_key = dot_nt(query, grad_scores) + tail * dot_tn(after_two, value_two)
        straight = dot_nt(grad_two, scores)
        through = dot_nn(after_two, key)
        grad_values.append(
            straight[:size] + straight[rows : rows + size] + tail * (through[:size] + through[rows : rows + size])
        )
        carried_two = jnp.concatenate(split(own * carried), axis=0)
        added = dot_nt(carried_two, query)
        state[head * rows : (head + 1) * rows, :] = keep * after + added[:rows] + added[rows:]
        for part, grad in ((0, grad_query), (1, grad_key)):
            plain = mapped[part][head * size : (head + 1) * size]
            back[part].append(softmax_back(grad, softmax_rows(plain), softmax_rows(-plain)))
    pieces_low = []
    for part in range(2):
        grad_mapped = jnp.concatenate(back[part], axis=0).astype(bf16)
        map_acc[part] += dot_nt(qkv[part * width : (part + 1) * width, :], grad_mapped)
        pieces_low.append(dot_nn(maps_back[part], grad_mapped))
    pieces_low.append(jnp.concatenate(grad_values, axis=0))
    grad_qkv = jnp.concatenate(pieces_low, axis=0).astype(bf16)
    part_low = dot_nt(grad_qkv.T, weight[:, : 3 * width]).astype(bf16)
    store_slots(count - 1 - step, ids, part_low, slots)
    weight_acc[...] += dot_nn(grad_qkv, attn_in[...])
    bias_acc[...] += jnp.sum(grad_qkv.astype(f32), axis=1, keepdims=True)
    if not first:

        @pl.when(step == count - 1)
        def _():
            wide = weight[:, : 3 * width].astype(f32)
            total = weight_acc[...].T
            bias_row = turn_columns(bias_acc[...])[0:1]
            sums = turn_columns(
                jnp.sum(wide * total, axis=1, keepdims=True), jnp.sum(wide * bias_row, axis=1, keepdims=True)
            )
            dim = wide.shape[0]
            blocks = []
            for part in range(2):
                lane = lax.broadcasted_iota(jnp.int32, (size, width), 1) // size
                own = jnp.zeros((size, width), f32)
                for head in range(heads):
                    own = jnp.where(lane == head, map_acc[part, head * size : (head + 1) * size, :], own)
                blocks.append(own)
            half = size // 2
            turned = jnp.concatenate(
                [blocks[0][:half], blocks[1][:half], blocks[0][half:], blocks[1][half:]], axis=1
            )
            lines = [
                (sums[0:1] - shift[...] * sums[1:2]) / gain[...],
                sums[1:2],
                sums_a[...] + sums_b[...],
                mlp_rows[...],
                jnp.concatenate([bias_row, jnp.zeros((1, dim - 3 * width), f32)], axis=1),
                turned,
            ]
            small = jnp.concatenate(lines, axis=0).astype(bf16)
            shard = total.shape[0] // packed.shape[0]
            for copy in range(packed.shape[0]):
                packed[copy, :SMALL, :] = small
                at = copy * shard
                packed[copy, SMALL:, : 3 * width] = total[at : at + shard].astype(bf16)
                packed[copy, SMALL:, 3 * width :] = product[at : at + shard, :]


def exchange(array):
    return lax.all_to_all(array, "dp", 0, 0)


def gather_dp(array):
    return exchange(jnp.broadcast_to(array, (lax.axis_size("dp"),) + array.shape)).reshape(-1, array.shape[1])


def swap(array, bit):
    return lax.ppermute(array, "tensor", [(i, i ^ bit) for i in range(4)])


def gather_tensor(array, across=None):
    if across is None:
        return (array, swap(array, 2), swap(array, 1), swap(array, 3))
    return (array, across, swap(array, 1), swap(across, 1))


def scatter_tensor(slots):
    return (slots[0], swap(slots[1], 2), swap(slots[2], 1), swap(slots[3], 3))


def block_diagonal(blocks):
    count, size, _ = blocks.shape
    eye = jnp.eye(count, dtype=blocks.dtype)
    return (eye[:, None, :, None] * blocks[:, :, None, :]).reshape(count * size, count * size)


def on_device(
    inputs, cotangent, segment, attn_gain, attn_shift, qkv_weight, qkv_bias, query_map, key_map,
    proj_weight, proj_bias, mlp_gain, mlp_shift, fc_weight, fc_bias, out_weight, out_bias,
):
    micro, tokens, dim = inputs.shape
    heads, size, _ = query_map.shape
    width = heads * size
    units = fc_weight.shape[1]
    count = lax.axis_size("dp")
    tiles = lax.axis_size("tensor")
    tile = tokens // tiles
    pieces = SEQ_LEN // tokens
    hops = min(-(-MAX_SEGMENT // tokens), pieces - 1)
    rows = size + PAD
    used = heads * rows
    shard = dim // count
    ids = jnp.stack([lax.axis_index("tensor"), lax.axis_index("dp")]).astype(jnp.int32)

    weight = gather_dp(jnp.concatenate([qkv_weight.reshape(shard, 3 * width), proj_weight.T], axis=1))
    proj_t = weight[:, 3 * width :]

    row = lambda v: v.astype(f32).reshape(1, -1)
    gain_a, shift_a, gain_m, shift_m = row(attn_gain), row(attn_shift), row(mlp_gain), row(mlp_shift)
    bias_p, bias_f, bias_o = row(proj_bias), row(fc_bias), row(out_bias)
    bias_qkv = qkv_bias.astype(f32).reshape(3 * width, 1)
    maps_back = jnp.stack([block_diagonal(query_map), block_diagonal(key_map)])
    maps = jnp.swapaxes(maps_back, 1, 2)
    seg = segment.astype(f32).reshape(micro, tiles, 1, tile)
    seg_col = segment.astype(f32).reshape(micro, tiles, tile, 1)

    def rows_of(array, m, at=None):
        return (array, (None, tile, dim), lambda i, ids: (m, i if at is None else at(i, ids), 0))

    def own_rows(array, m):
        return (array, (None, tile, dim), lambda i, ids: (m, ids[0], 0))

    def columns(array, at=None, m=0):
        return (
            array, (array.shape[0], tile), lambda i, ids: (0, m * tiles + (i if at is None else at(i, ids)))
        )

    def columns_out(height, kind, at=None):
        return ((height, tokens), kind, (height, tile), lambda i, ids: (0, i if at is None else at(i, ids)))

    def seg_row(m, at=None):
        return (seg, (None, None, 1, tile), lambda i, ids: (m, i if at is None else at(i, ids), 0, 0))

    def seg_column(m, at=None):
        return (seg_col, (None, None, tile, 1), lambda i, ids: (m, i if at is None else at(i, ids), 0, 0))

    def states_of(m):
        return [(a, (used + PAD, 2 * size), lambda i, ids: (m, 0)) for a in incoming]

    def entering(m):
        return (incoming[0], (PAD, 2 * size), lambda i, ids: ((m * (used + PAD) + used) // PAD, 0))

    def half(array, at):
        return (array, (None, tile, dim), lambda i, ids: (at, 0, 0))

    near = lambda i, ids: ids[0] ^ relative(i)

    def pin(*arrays):
        nonlocal ids
        ids, arrays = lax.optimization_barrier((ids, arrays))
        return arrays

    def run(*arguments, **options):
        return pin(*call(arguments[0], arguments[1], ids, *arguments[2:], **options))

    def fold(*pairs):
        (result,) = run(
            functools.partial(fold_kernel, len(pairs)), (1,),
            [half(a, 1) for pair in pairs for a in pair],
            [whole_out((len(pairs), tile, dim), bf16)], [], 3,
        )
        return result

    rest_own = jnp.concatenate([fc_weight, out_weight.T], axis=1)
    rest = lax.all_gather(rest_own, "dp", axis=0, tiled=True)
    maps, maps_back, bias_qkv, seg, seg_col = pin(maps, maps_back, bias_qkv, seg, seg_col)
    gain_a, shift_a, gain_m, shift_m, bias_p, bias_f, bias_o = pin(gain_a, shift_a, gain_m, shift_m, bias_p, bias_f, bias_o)
    row_tile = lambda array: (array, (None, tile, dim), lambda i, ids: (lax.div(i, tiles), lax.rem(i, tiles), 0))
    (attn_in,) = run(
        norm_kernel, (micro * tiles,), [row_tile(inputs), whole(gain_a), whole(shift_a)],
        [((micro, tokens, dim), bf16) + row_tile(inputs)[1:]], [], 8,
    )
    fc_block = (rest, (dim, units), lambda i, ids: (0, 0))
    out_block = (rest, (dim, units), lambda i, ids: (0, 1))
    state_out = ((count, used + PAD, 2 * size), bf16)
    proj_across = swap(proj_t, 2)
    every = micro * tiles
    qkv, feats, state = run(
        functools.partial(project_kernel, heads, tiles), (every,),
        [
            row_tile(attn_in), whole(weight), whole(bias_qkv), whole(maps),
            (seg, (None, None, 1, tile), lambda i, ids: (lax.div(i, tiles), lax.rem(i, tiles), 0, 0)),
            (seg, (None, None, 1, tile), lambda i, ids: (lax.div(i, tiles), tiles - 1, 0, 0)),
        ],
        [
            ((3 * width, micro * tokens), bf16, (3 * width, tile), lambda i, ids: (0, i)),
            ((4 * width, micro * tokens), bf16, (4 * width, tile), lambda i, ids: (0, i)),
            (
                (micro * (used + PAD), 2 * size), bf16, (used + PAD, 2 * size),
                lambda i, ids: (lax.div(i, tiles), 0),
            ),
        ],
        [pltpu.VMEM((used, 2 * size), f32), pltpu.VMEM((3 * width, dim), bf16)],
        13,
    )
    incoming = [
        lax.ppermute(state, "dp", [(i, i + k) for i in range(count) if i % pieces + k < pieces])
        for k in range(1, hops + 1)
    ]
    (proj_across,) = pin(proj_across)
    proj_slots = pin(*gather_tensor(proj_t, proj_across))
    attended, attended_low, denominators, states = [], [], [], []
    for m in range(micro):
        result = run(
            functools.partial(attend_kernel, heads, pieces, hops), (tiles,),
            [
                (qkv, (width, tile), lambda i, ids, m=m: (2, m * tiles + i)), columns(feats, None, m), seg_row(m), seg_column(m),
            ]
            + states_of(m),
            [
                columns_out(width, f32), columns_out(width, bf16), columns_out(8, f32),
                ((tiles, used, 2 * size), f32, (None, used, 2 * size), lambda i, ids: (i, 0, 0)),
            ],
            [pltpu.VMEM((used, 2 * size), f32), pltpu.VMEM((1, tile), f32)],
            6.5,
        )
        attended.append(result[0])
        attended_low.append(result[1])
        denominators.append(result[2])
        states.append(result[3])
        if m == 0:
            across = swap(result[1], 2)
        else:
            (across,) = pin(across)
            slots = [gather_tensor(attended_low[0], across), gather_tensor(result[1])]

    acc = ()
    residuals, mlp_terms, out_pairs = [], [], []
    for m in range(micro):
        final = m == micro - 1
        kept = [((dim, units), f32), ((dim, units), f32), ((1, units), f32)]
        pair = [whole_out((2, tile, dim), bf16)] * 2
        result = run(
            functools.partial(mlp_kernel, not final), (tiles,),
            [rows_of(inputs, m), rows_of(cotangent, m)]
            + [columns(a) for a in slots[m]]
            + [whole(a) for a in proj_slots]
            + [whole(bias_p), whole(gain_m), whole(shift_m), fc_block, out_block, whole(bias_f)]
            + [whole(a) for a in acc],
            [((tiles, tile, dim), f32, (None, tile, dim), lambda i, ids: (i, 0, 0))]
            + (pair if final else [whole_out((tile, dim), bf16)] * 4)
            + pair
            + ([whole_out((3, dim), f32), whole_out((dim, 2 * units), bf16)] if final else [whole_out(*k) for k in kept]),
            [pltpu.VMEM(*k) for k in kept] if final else [],
            21,
        )
        residuals.append(result[0])
        parts = result[1:3] if final else result[1:5]
        mlp_terms.append((parts[0], swap(parts[1], 1)) if final else scatter_tensor(parts))
        result = result[3:] if final else result[5:]
        out_pairs.append((result[0], swap(result[1], 1)))
        acc = result[2:]
    mlp_rows, rest_grads = acc

    own_tile = lambda array: (array, (None, tile, dim), lambda i, ids: (ids[0], 0, 0))
    grad_residuals, grad_slots, row_sums = [], [], []

    def middle(m, terms):
        grad_residual, grad_attn, sums = run(
            middle_kernel, (1,), [own_tile(residuals[m]), own_rows(cotangent, m), whole(gain_m)] + terms,
            [whole_out((tile, dim), f32), whole_out((tile, dim), bf16), whole_out((2, dim), f32)],
            [], 4,
        )
        grad_residuals.append(grad_residual)
        row_sums.append(sums)
        return grad_attn, swap(grad_attn, 2)

    proj_acc = ()
    grads, returned = [], []

    def grads_in(m, *gathered):
        nonlocal proj_acc
        grad_slots.append(gathered)
        result = run(
            functools.partial(grads_in_kernel, heads, pieces, m == 0), (tiles,),
            [whole(a) for a in grad_slots[m]]
            + [
                whole(proj_t), (feats, (2 * width, tile), lambda i, ids: (0, m * tiles + near(i, ids))),
                columns(attended[m], near), columns(attended_low[m], near), columns(denominators[m], near),
                seg_row(m, near), entering(m),
            ]
            + [whole(a) for a in proj_acc],
            [
                columns_out(used, f32, near), whole_out(*state_out),
                whole_out((width, dim), f32) if m == 0 else whole_out((dim, width), bf16),
            ],
            [pltpu.VMEM((used, 2 * size), f32), pltpu.VMEM((width, dim), bf16)]
            + ([] if m == 0 else [pltpu.VMEM((width, dim), f32)]),
            7,
        )
        grads.append(result[0])
        proj_acc = (result[2],)
        returned.append(exchange(result[1]))

    acc = ()
    turned = lambda i, ids: tiles - 1 - i

    def attention_back(m):
        nonlocal acc
        final = m == micro - 1
        kept = [((3 * width, dim), f32), ((2, width, width), f32), ((3 * width, 1), f32)]
        result = run(
            functools.partial(grads_kernel, heads, pieces, hops, not final), (tiles,),
            [
                columns(qkv, turned, m), columns(feats, turned, m), columns(grads[m], turned),
                (states[m], (None, used, 2 * size), lambda i, ids: (tiles - 1 - i, 0, 0)),
                seg_row(m, turned), seg_column(m, turned), seg_row(m, lambda i, ids: jnp.maximum(tiles - 2 - i, 0)),
                entering(m), rows_of(attn_in, m, turned),
                whole(weight), whole(maps), whole(maps_back), whole(returned[m]),
            ]
            + [whole(a) for a in acc]
            + ([whole(a) for a in (proj_acc[0], gain_a, shift_a, mlp_rows, *row_sums)] if final else []),
            ([whole_out((2, tile, dim), bf16)] * 2 if final else [whole_out((tile, dim), bf16)] * 4)
            + ([whole_out((count, SMALL + shard, 4 * width), bf16)] if final else [whole_out(*k) for k in kept]),
            ([pltpu.VMEM(*k) for k in kept] if final else []) + [pltpu.VMEM((used, 2 * size), f32)],
            0 if final else 16,
        )
        acc = result[2:] if final else result[4:]
        return result[:2] if final else result[:4]

    def last(m, terms):
        (finished,) = run(
            last_kernel, (1,), [own_rows(inputs, m), whole(grad_residuals[m]), whole(gain_a)] + terms,
            [whole_out((tile, dim), bf16)], [], 4,
        )
        return finished

    def ordered(parts, m, base=()):
        (result,) = run(
            functools.partial(order_kernel, tiles), (tiles,),
            [whole(a) for a in parts] + [(a, None, None) for a in base],
            [((micro, tokens, dim), bf16, (None, tile, dim), lambda i, ids: (m, ids[0] ^ relative(i), 0))],
            [], 4, aliases={tiles + 1: 0} if base else None,
        )
        return result

    def paired(pair, crossed):
        return [half(pair[0], 0), half(pair[1], 0), half(crossed, 0)]

    (rest_grads,) = pin(rest_grads)
    rest_sum = lax.psum_scatter(rest_grads, "dp", scatter_dimension=0, tiled=True)
    moved = middle(0, [whole(a) for a in mlp_terms[0]])
    crossed = swap(fold(mlp_terms[1]), 2)
    array, across = moved
    (across,) = pin(across)
    grads_in(0, *gather_tensor(array, across))
    moved = middle(1, paired(mlp_terms[1], crossed))
    out_crossed = swap(fold(*out_pairs), 2)
    array, across = moved
    returned[0], across = pin(returned[0], across)
    moved = gather_tensor(array, across)
    first_terms = scatter_tensor(attention_back(0))
    grads_in(1, *moved)
    (rest_sum,) = pin(rest_sum)
    (finished,) = run(
        functools.partial(finish_kernel, micro), (1,),
        [whole(bias_o), whole(out_crossed)]
        + [spec for m in range(micro) for spec in (own_tile(residuals[m]), half(out_pairs[m][0], 0), half(out_pairs[m][1], 0))],
        [whole_out((micro, tile, dim), bf16)], [], 4,
    )
    out_across = swap(finished, 2)
    early = last(0, [whole(a) for a in first_terms])
    early_across = swap(early, 2)
    kept, away = attention_back(1)
    kept, away, packed, out_across, early_across = pin(kept, away, acc[0], out_across, early_across)
    last_pair = (kept, swap(away, 1))
    total = exchange(packed)
    crossed = swap(fold(last_pair), 2)
    outputs = gather_tensor(finished, out_across)
    (output,) = run(
        functools.partial(order_kernel, tiles), (every,),
        [(a, (None, tile, dim), lambda i, ids: (lax.div(i, tiles), 0, 0)) for a in outputs],
        [(
            (micro, tokens, dim), bf16, (None, tile, dim),
            lambda i, ids: (lax.div(i, tiles), ids[0] ^ relative(lax.rem(i, tiles)), 0),
        )],
        [], 6,
    )
    rest_sum = rest_sum.astype(f32)
    fc_grad, out_grad = pin(rest_sum[:, :units], rest_sum[:, units:].T)
    late = last(1, paired(last_pair, crossed))
    late_across = swap(late, 2)
    input_grad = ordered(gather_tensor(early, early_across), 0)
    (late_across,) = pin(late_across)
    input_grad = ordered(gather_tensor(late, late_across), 1, (input_grad,))
    (total,) = pin(total)
    total = jnp.sum(total.astype(f32), axis=0)
    shared = total[:6]
    shared = (shared + swap(shared, 1)) + (swap(shared, 2) + swap(shared, 3))
    blocks = total[8 : 8 + size // 2].reshape(size // 2, 2, 2, heads, size)
    blocks = jnp.transpose(blocks, (2, 3, 1, 0, 4)).reshape(2, heads, size, size)
    qkv_sum, proj_sum = total[SMALL:, : 3 * width], total[SMALL:, 3 * width :].T
    return (
        output,
        input_grad,
        shared[0],
        shared[1],
        qkv_sum.reshape(shard, 3, width),
        total[7, : 3 * width].reshape(3, width),
        blocks[0],
        blocks[1],
        proj_sum,
        shared[2],
        shared[4],
        shared[5],
        fc_grad,
        total[6],
        out_grad,
        shared[3],
    )


def solution(mesh):
    in_specs = (
        P(None, "dp", None), P(None, "dp", None), P(None, "dp"), P(), P(), P("dp", None, "tensor"),
        P(None, "tensor"), P("tensor", None, None), P("tensor", None, None), P("tensor", "dp"), P(), P(), P(),
        P("dp", "tensor"), P("tensor"), P("tensor", "dp"), P(),
    )
    out_specs = (
        P(None, "dp", None), P(None, "dp", None), P(), P(), P("dp", None, "tensor"), P(None, "tensor"),
        P("tensor", None, None), P("tensor", None, None), P("tensor", "dp"), P(), P(), P(),
        P("dp", "tensor"), P("tensor"), P("tensor", "dp"), P(),
    )
    return jax.shard_map(
        on_device, mesh=mesh, in_specs=in_specs, out_specs=out_specs, check_vma=False
    )
```
